32 devices in a mesh: ctx: 4 (over z), head: 8 (over y, x, core).
Axes of the slice: x: 2, y: 2, z: 4, core: 2. Of those that a mesh axis runs over, the one named last changes fastest.
Arguments:
- hidden: float32 [1024, 2304], P(('ctx', 'head')), may hold values from -40 to 40
- w_query: float32 [2304, 1536], P(None, 'head'), may hold values from -0.125 to 0.125
- w_down: float32 [2304, 576], replicated, may hold values from -0.125 to 0.125
- latent_gain: float32 [512], replicated, may hold values from 0.25 to 1.75
- w_key_up: float32 [512, 1024], P(None, 'head'), may hold values from -0.25 to 0.25
- w_value_up: float32 [512, 1024], P(None, 'head'), may hold values from -0.25 to 0.25
- w_out: float32 [1024, 2304], P('head'), may hold values from -0.1875 to 0.1875
Outputs:
- output: float32 [1024, 2304], P(('ctx', 'head'))
The draws below stay inside these ranges and needn't reach their ends.
All inputs are finite; a program needn't handle non-finite values.
Results may differ from the reference program's by a relative error of at most 0.0003.
Values sent between devices are 32-bit elements; how exact they have to be, the bound alone decides.
A program may use at most 64 MiB of HBM per device.

```python
import jax
import jax.numpy as jnp
from jax import lax

D = 2304
HEADS = 8
RANK = 512
SHARED = 64
NOPE = 128
VDIM = 128
TOKENS = 1024


def draw_hidden(key, part):
    base_key = jax.random.fold_in(jax.random.fold_in(key, 17), 0)
    values = jnp.clip(jax.random.normal(base_key, (TOKENS, D), jnp.float32), -4.0, 4.0)
    return values.astype(jnp.float32)


def level_of(rng, extent, shards, low, largest):
    level = 1.0
    for position, parts in shards:
        steps = jax.random.uniform(jax.random.fold_in(jax.random.fold_in(rng, 6), position), (parts,), jnp.float32, low / len(shards), largest / len(shards))
        level = level * jnp.repeat(jnp.exp(steps), extent[position] // parts).reshape((-1,) + (1,) * (len(extent) - 1 - position))
    return level


def centred(stream_key, dims, width, reach, cuts=(), kind=jnp.bfloat16):
    array = jax.random.normal(stream_key, dims, jnp.float32) * width
    if len(cuts) > 0:
        array = level_of(stream_key, dims, cuts, -0.22, 0.18) * array
    return jnp.clip(array, min=-reach, max=reach).astype(kind)


def setup_inputs(seed: int = 0) -> dict:
    key_of = jax.random.split(jax.random.key(seed), 8)
    hidden = draw_hidden(jax.random.fold_in(key_of[7], 71), 0)
    w_query = centred(key_of[1], (D, HEADS * (NOPE + SHARED)), D ** -0.5, 0.125, ((1, 8),), jnp.float32)
    w_down = centred(key_of[2], (D, RANK + SHARED), D ** -0.5, 0.125, (), jnp.float32)
    latent_gain = jnp.clip(1.0 + 0.15 * jax.random.normal(key_of[3], (RANK,), jnp.float32), 0.25, 1.75)
    w_key_up = centred(key_of[4], (RANK, HEADS * NOPE), RANK ** -0.5, 0.25, ((1, 8),), jnp.float32)
    w_value_up = centred(key_of[5], (RANK, HEADS * VDIM), RANK ** -0.5, 0.25, ((1, 8),), jnp.float32)
    w_out = centred(key_of[6], (HEADS * VDIM, D), (HEADS * VDIM) ** -0.5, 0.1875, ((0, 8),), jnp.float32)
    return dict(hidden=hidden, w_query=w_query, w_down=w_down, latent_gain=latent_gain, w_key_up=w_key_up, w_value_up=w_value_up, w_out=w_out)


EXACT = lax.Precision.HIGHEST

def matmul(left, right):
    return jnp.dot(left, right, precision=EXACT, preferred_element_type=jnp.float32)

def reference(hidden, w_query, w_down, latent_gain, w_key_up, w_value_up, w_out):
    down_part = matmul(hidden, w_down)
    raw_latent = down_part[:, :RANK]
    key_shared = down_part[:, RANK:]
    meansq = lax.optimization_barrier(jnp.mean(raw_latent * raw_latent, axis=-1, keepdims=True))
    latent = raw_latent * lax.rsqrt(meansq + 1e-06) * latent_gain
    queries = matmul(hidden, w_query).reshape(TOKENS, HEADS, NOPE + SHARED).transpose(1, 0, 2)
    key_own = matmul(latent, w_key_up).reshape(TOKENS, HEADS, NOPE).transpose(1, 0, 2)
    values = matmul(latent, w_value_up).reshape(TOKENS, HEADS, VDIM).transpose(1, 0, 2)
    positions = jnp.arange(TOKENS, dtype=jnp.int32)
    causal = positions[:, None] >= positions[None, :]
    score_scale = (NOPE + SHARED) ** (-0.5)

    def per_head(operands):
        head_query, head_key, head_value = operands
        scores = (matmul(head_query[:, :NOPE], head_key.T) + matmul(head_query[:, NOPE:], key_shared.T)) * score_scale
        scores = jnp.where(causal, scores, -jnp.inf)
        weights = jax.nn.softmax(scores, axis=-1)
        return matmul(weights, head_value)
    attended = lax.map(per_head, (queries, key_own, values))
    attended = attended.transpose(1, 0, 2).reshape(TOKENS, HEADS * VDIM)
    return matmul(attended, w_out)
```

```python
import functools

import jax
import jax.numpy as jnp
from jax import lax
from jax.experimental import pallas as pl
from jax.experimental.pallas import tpu as pltpu
from jax.sharding import PartitionSpec as P

EPSILON = 1e-06
FLOOR = -1e30
CORES = 2
LANE = 128
DIRECT = ((1, 0), (2, 1), (1, 1), (2, 0))
REST = ((1, 1), (2, 0), (3, 0), (3, 1))
MESH = pl.DeviceIdType.MESH
NN = (((1,), (0,)), ((), ()))
NT = (((1,), (1,)), ((), ()))


def halves(value):
    high = value.astype(jnp.bfloat16)
    return high, (value - high.astype(jnp.float32)).astype(jnp.bfloat16)


def product(left, right, dims=NN):
    (lh, ll), (rh, rl) = left, right
    dot = functools.partial(lax.dot_general, dimension_numbers=dims, preferred_element_type=jnp.float32)
    return dot(lh, rh) + (dot(ll, rh) + dot(lh, rl))


def general_kernel(
    ctx_n, chips, square, steps, pieces,
    hidden, w_query, w_down, gain, w_key, w_value, w_out, out,
    hid, wd, wq, gn, wk, wv, wo, lat, qh, ql, top, total, acc, part, landed,
    load_sem, swap_send, swap_recv, hid_send, hid_recv, col_send, col_recv,
    row_send, row_recv, twin_send, twin_recv, sum_send, sum_recv,
):
    rows, width = hidden.shape
    parts = 2 if square else 1
    rank = gn.shape[1]
    tail = wd.shape[0] - rank
    nope = wk.shape[2]
    per_core = chips * rows
    block = CORES * per_core
    lanes = lat.shape[1]
    ctx = lax.axis_index("ctx")
    head = lax.axis_index("head")
    chip, core = head // CORES, head % CORES
    twin = chip * CORES + (1 - core)

    def chip_at(offset):
        return lax.rem(chip + offset, chips)

    def to(o):
        if not square:
            return chip_at(o)
        return [chip, chip + 1 - 2 * lax.rem(chip, 2), lax.rem(chip + 2, 4), 3 - chip][o]

    def origin(o):
        return to(o) if square else chip_at(chips - o)

    def local(src, dst, sem):
        return pltpu.make_async_copy(src, dst, load_sem.at[sem])

    def remote(src, dst, send, recv, c, h):
        return pltpu.make_async_remote_copy(
            src_ref=src, dst_ref=dst, send_sem=send, recv_sem=recv,
            device_id={"ctx": c, "head": h}, device_id_type=MESH,
        )

    def at_rows(start, size):
        return pl.ds(pl.multiple_of(start, 8), size)

    my_hid = hid.at[at_rows(chip * rows, rows)]
    depth = width // steps
    loads = [local(hidden, my_hid, 0), local(gain, gn, 1)]
    for s in range(steps):
        span = pl.ds(s * depth, depth)
        loads.append(local(w_down.at[:, span], wd.at[:, span], 2 + s))
    pairs = [(w_query, wq), (w_key, wk), (w_value, wv), (w_out, wo)]
    own = [local(src, dst.at[core], 2 + steps + i) for i, (src, dst) in enumerate(pairs)]
    for copy in loads:
        copy.start()

    barrier = pltpu.get_barrier_semaphore()
    for o in range(1, chips):
        pl.semaphore_signal(barrier, inc=1, device_id={"ctx": ctx, "head": chip_at(o) * CORES + core}, device_id_type=MESH)
    pl.semaphore_signal(barrier, inc=1, device_id={"ctx": ctx, "head": twin}, device_id_type=MESH)
    for o in range(1, ctx_n):
        pl.semaphore_signal(barrier, inc=1, device_id={"ctx": lax.rem(ctx + o, ctx_n), "head": head}, device_id_type=MESH)
    pl.semaphore_wait(barrier, chips - 1 + 1 + ctx_n - 1)

    def share(source, spot, send, recv):
        def start_of(o, h):
            target = to(o)
            return remote(source(h), spot(chip, h), send(o, h), recv(o, h), ctx, target * CORES + core)

        def seen(o, h):
            place_of = spot(origin(o), h)
            return remote(place_of, place_of, send(o, h), recv(o, h), ctx, twin)

        def passed(h):
            place_of = spot(to(1 + h), h)
            return remote(place_of, place_of, send(3, h), recv(3, h), ctx, to(2 - h) * CORES + core)

        direct = [(1, 0), (2, 1), (1, 1), (2, 0)] if square else [(o, 0) for o in range(1, chips)]

        def start():
            for o, h in direct:
                start_of(o, h).start()

        def relay():
            if square:
                for h in range(2):
                    seen(1 + h, h).wait_recv()
                    passed(h).start()

        def finish():
            for o, h in [(1, 1), (2, 0), (3, 0), (3, 1)] if square else direct:
                seen(o, h).wait_recv()

        def drain():
            for o, h in direct:
                start_of(o, h).wait_send()
            if square:
                for h in range(2):
                    passed(h).wait_send()

        return start, relay, finish, drain

    half = width // parts

    def hid_half(h):
        return pl.ds(h * half, half)

    hid_start, hid_relay, hid_finish, hid_drain = share(
        lambda h: hidden.at[:, hid_half(h)],
        lambda k, h: hid.at[at_rows(k * rows, rows), hid_half(h)],
        lambda o, h: hid_send.at[o, h],
        lambda o, h: hid_recv.at[o, h],
    )
    hid_start()
    swaps = [remote(src, dst.at[core], swap_send.at[i], swap_recv.at[i], ctx, twin) for i, (src, dst) in enumerate(pairs)]
    for copy in own:
        copy.start()
    for copy in swaps:
        copy.start()

    loads[0].wait()
    loads[1].wait()
    down = jnp.zeros((rows, rank + tail), jnp.float32)
    for s in range(steps):
        loads[2 + s].wait()
        span = pl.ds(s * depth, depth)
        down += product(halves(my_hid[:, span]), halves(wd[:, span]), NT)
    raw = down[:, :rank]
    meansq = jnp.mean(raw * raw, axis=-1, keepdims=True)
    blank = jnp.zeros((rows, lanes - rank - tail), jnp.float32)

    def place(b, p, k):
        return ((b * CORES + p) * chips + k) * rows

    mine = at_rows(place(ctx, core, chip), rows)
    lat[mine, :rank] = raw * lax.rsqrt(meansq + EPSILON) * gn[...]
    lat[mine, rank:] = jnp.concatenate([down[:, rank:], blank], axis=1)

    def col_copy(b):
        spot = lat.at[at_rows(place(b, core, chip), rows)]
        return remote(spot, spot, col_send.at[b], col_recv.at[b], jnp.minimum(ctx + 1, ctx_n - 1), head)

    def latents(b):
        def spot(k, h):
            return lat.at[at_rows(place(b, core, k) + h * (rows // parts), rows // parts)]

        return share(
            lambda h: spot(chip, h), spot, lambda o, h: row_send.at[b, o, h], lambda o, h: row_recv.at[b, o, h]
        )

    def twin_copy(b, p):
        spot = lat.at[at_rows(place(b, p, 0), per_core)]
        return remote(spot, spot, twin_send.at[b], twin_recv.at[b], ctx, twin)

    def spread(b):
        @pl.when(ctx + 1 < ctx_n)
        def _():
            col_copy(b).start()

        latents(b)[0]()

    def gather_rows(b):
        latents(b)[2]()
        twin_copy(b, core).start()

    spread(ctx)
    hid_relay()
    for d in range(1, ctx_n):
        @pl.when(d <= ctx)
        def _():
            col_copy(ctx - d).wait_recv()
            spread(ctx - d)

    latents(ctx)[1]()

    hid_finish()
    for i in range(2):
        own[i].wait()
        swaps[i].wait()
    scale = wq.shape[1] ** (-0.5)
    pad = jnp.zeros((per_core, lanes - rank - tail), jnp.float32)
    query = [jnp.zeros((per_core, wq.shape[1]), jnp.float32) for _ in range(CORES)]
    for s in range(steps):
        span = pl.ds(s * depth, depth)
        piece = halves(hid[:, span])
        for p in range(CORES):
            query[p] += product(piece, halves(wq[p, :, span]), NT)
    for p in range(CORES):
        wide = product(halves(query[p][:, :nope] * scale), halves(wk[p]), NT)
        span = pl.ds(p * per_core, per_core)
        qh[span, :rank], ql[span, :rank] = halves(wide)
        qh[span, rank:], ql[span, rank:] = halves(jnp.concatenate([query[p][:, nope:] * scale, pad], axis=1))

    def spots(index, parity):
        inner = lax.rem(index, per_core)
        return (lax.div(inner, rows) * CORES + parity) * rows + lax.rem(inner, rows)

    def attend(b, first):
        keys = halves(lat[at_rows(place(b, 0, 0), block), :])
        scores = product((qh[...], ql[...]), keys, NT)
        if first:
            line = lax.broadcasted_iota(jnp.int32, (block, 1), 0)
            column = lax.broadcasted_iota(jnp.int32, (1, block), 1)
            causal = spots(line, core) >= spots(column, lax.div(column, per_core))
            scores = jnp.where(causal, scores, FLOOR)
            peak = jnp.max(scores, axis=1, keepdims=True)
        else:
            peak = jnp.maximum(top[...], jnp.max(scores, axis=1, keepdims=True))
        weights = jnp.exp(scores - peak)
        if first:
            weights = jnp.where(causal, weights, 0.0)
        mixed = product(halves(weights), (keys[0][:, :rank], keys[1][:, :rank]))
        added = jnp.sum(weights, axis=1, keepdims=True)
        if first:
            total[...] = added
            acc[...] = mixed
        else:
            fade = jnp.exp(top[...] - peak)
            total[...] = total[...] * fade + added
            acc[...] = acc[...] * fade + mixed
        top[...] = peak

    def relay_at(d):
        if d < ctx_n:
            @pl.when(d <= ctx)
            def _():
                latents(ctx - d)[1]()

    relay_at(1)
    gather_rows(ctx)
    twin_copy(ctx, 1 - core).wait_recv()
    attend(ctx, True)
    for d in range(1, ctx_n):
        @pl.when(d <= ctx)
        def _():
            relay_at(d + 1)
            gather_rows(ctx - d)
            twin_copy(ctx - d, 1 - core).wait_recv()
            attend(ctx - d, False)

    for i in range(2, 4):
        own[i].wait()
        swaps[i].wait()
    heads = []
    for p in range(CORES):
        span = pl.ds(p * per_core, per_core)
        heads.append(product(halves(acc[span, :] / total[span, :]), halves(wv[p])))
    attended = halves(jnp.concatenate(heads, axis=1))
    columns = width // pieces

    def cut(ref, k, t):
        return ref.at[at_rows(k * rows, rows), pl.ds(t * columns, columns)]

    def axes_of(t):
        return (1, 2) if t % 2 == 0 else (2, 1)

    def sum_copy(t, j):
        if not square:
            return remote(
                cut(part, chip_at(j), t), cut(landed, chip, t), sum_send.at[t, j], sum_recv.at[t, j],
                ctx, chip_at(j) * CORES + core,
            )
        first, second = axes_of(t)
        src = [to(3), to(first), to(second)][j]
        dst = [to(3), to(first), to(3)][j]
        target = [to(first), to(first), to(second)][j]
        return remote(cut(part, src, t), cut(landed, dst, t), sum_send.at[t, j], sum_recv.at[t, j], ctx, target * CORES + core)

    def second_stage(t):
        sum_copy(t, 0).wait_recv()
        keep = to(axes_of(t)[1])
        cut(part, keep, t)[...] = cut(part, keep, t)[...] + cut(landed, keep, t)[...]
        sum_copy(t, 2).start()

    kinds = (0, 1) if square else tuple(range(1, chips))
    for t in range(pieces):
        span = pl.ds(t * columns, columns)
        weight = jnp.concatenate([wo[p, :, span] for p in range(CORES)], axis=0)
        part[:, span] = product(attended, halves(weight))
        for j in kinds:
            sum_copy(t, j).start()
        if square and t >= 2:
            second_stage(t - 2)
    if square:
        for t in range(max(pieces - 2, 0), pieces):
            second_stage(t)
    for t in range(pieces):
        result = cut(part, chip, t)[...]
        if square:
            for j in (1, 2):
                sum_copy(t, j).wait_recv()
            result += cut(landed, chip, t)[...] + cut(landed, to(axes_of(t)[0]), t)[...]
        else:
            for j in kinds:
                sum_copy(t, j).wait_recv()
                result += cut(landed, origin(j), t)[...]
        out[:, pl.ds(t * columns, columns)] = result

    hid_drain()
    for t in range(pieces):
        for j in kinds + ((2,) if square else ()):
            sum_copy(t, j).wait_send()
    for d in range(ctx_n):
        @pl.when(d <= ctx)
        def _():
            @pl.when(ctx + 1 < ctx_n)
            def _():
                col_copy(ctx - d).wait_send()

            latents(ctx - d)[3]()
            twin_copy(ctx - d, core).wait_send()


def square_kernel(
    ctx_n, chunks, cuts,
    hidden, w_query, w_down, gain, w_key, w_value, w_out, out,
    mine, hid, wd, gn, wq, wqh, wql, wk, wv, wo, woh, wol, lat, kh, kl, qh, ql, top, total, acc,
    part, mid, fwd, near, last, res,
    load_sem, out_sem, swap_send, swap_recv, hid_send, hid_recv, far_sem, z_send, z_recv,
    lat_send, lat_recv, twin_send, twin_recv, sum_send, sum_recv,
):
    rows, width = hidden.shape
    rank = gn.shape[1]
    tail = wd.shape[0] - rank
    nope, vdim = wk.shape[2], wv.shape[2]
    key_width = wq.shape[1]
    lanes = kh.shape[1]
    r = rows // chunks
    group = 4 * r
    many = CORES * group
    block = CORES * 4 * rows
    hr = rows // 2
    tiles = rank // LANE
    piece = hr * tiles + hr // 2
    slot = 2 * piece
    half = width // 2
    steps = 3 if width % 384 == 0 else 1
    depth = width // steps
    ctx = lax.axis_index("ctx")
    head = lax.axis_index("head")
    chip, core = head // CORES, head % CORES
    twin = chip * CORES + (1 - core)
    xbit, ybit = lax.rem(chip, 2), lax.div(chip, 2)
    side = [None, (2 * ybit + 1 - xbit) * CORES + core, (2 * (1 - ybit) + xbit) * CORES + core]

    def local(src, dst, sem):
        return pltpu.make_async_copy(src, dst, sem)

    def remote(src, dst, send, recv, h, c=ctx):
        return pltpu.make_async_remote_copy(
            src_ref=src, dst_ref=dst, send_sem=send, recv_sem=recv,
            device_id={"ctx": c, "head": h}, device_id_type=MESH,
        )

    def signal(sem, c, h):
        pl.semaphore_signal(sem, inc=1, device_id={"ctx": c, "head": h}, device_id_type=MESH)

    def when(condition, *actions):
        @pl.when(condition)
        def _():
            for action in actions:
                action()

    def spot(q, s, h):
        return hid.at[pl.ds((q * 4 + s) * r, r), pl.ds(h * half, half)]

    def hid_direct(q):
        return [
            remote(
                hidden.at[pl.ds(q * r, r), pl.ds(h * half, half)], spot(q, a, h),
                hid_send.at[q, a - 1, h], hid_recv.at[q, a - 1, h], side[a],
            )
            for a, h in DIRECT
        ]

    def hid_passed(q, h):
        return remote(spot(q, 1 + h, h), spot(q, 3, h), hid_send.at[q, 2, h], hid_recv.at[q, 2, h], side[2 - h])

    def hid_landed(q, s, h):
        return remote(spot(q, s, h), spot(q, s, h), hid_send.at[q, s - 1, h], hid_recv.at[q, s - 1, h], twin)

    def lat_at(d, p, s, h=0, size=piece):
        return lat.at[pl.ds(((d * CORES + p) * 4 + s) * slot + h * piece, size)]

    def lat_direct(d):
        return [
            remote(lat_at(d, 0, 0, h), lat_at(d, 0, a, h), lat_send.at[d, a - 1, h], lat_recv.at[d, a - 1, h], side[a])
            for a, h in DIRECT
        ]

    def lat_passed(d, h):
        return remote(
            lat_at(d, 0, 1 + h, h), lat_at(d, 0, 3, h), lat_send.at[d, 2, h], lat_recv.at[d, 2, h], side[2 - h]
        )

    def lat_landed(d, s, h):
        return remote(lat_at(d, 0, s, h), lat_at(d, 0, s, h), lat_send.at[d, s - 1, h], lat_recv.at[d, s - 1, h], twin)

    def twin_own(d):
        return remote(lat_at(d, 0, 0, 0, slot), lat_at(d, 1, 0, 0, slot), twin_send.at[d, 0], twin_recv.at[d, 0], twin)

    def twin_rest(d):
        size = 3 * slot
        return remote(lat_at(d, 0, 1, 0, size), lat_at(d, 1, 1, 0, size), twin_send.at[d, 1], twin_recv.at[d, 1], twin)

    def z_copy(d):
        c = jnp.minimum(ctx + d, ctx_n - 1)
        return remote(lat_at(0, 0, 0, 0, slot), lat_at(d, 0, 0, 0, slot), z_send.at[d], z_recv.at[d], head, c)

    def lat_spread(d):
        for copy in lat_direct(d):
            copy.start()
        twin_own(d).start()

    def lat_fetch(d):
        z_copy(d).wait_recv()
        lat_spread(d)

    def lat_relay(d):
        for h in range(2):
            lat_landed(d, 1 + h, h).wait_recv()
            lat_passed(d, h).start()

    def lat_finish(d):
        for s, h in REST:
            lat_landed(d, s, h).wait_recv()
        twin_rest(d).start()

    def hid_relay(q):
        for h in range(2):
            hid_landed(q, 1 + h, h).wait_recv()
            hid_passed(q, h).start()

    def hid_finish(q):
        for s, h in REST:
            hid_landed(q, s, h).wait_recv()

    loads = [local(hidden, mine, load_sem.at[0]), local(gain, gn, load_sem.at[1])]
    for i in range(steps):
        span = pl.ds(i * depth, depth)
        loads.append(local(w_down.at[:, span], wd.at[:, span], load_sem.at[2 + i]))
    pairs = [(w_query, wq), (w_key, wk), (w_value, wv), (w_out, wo)]
    own = [local(src, dst.at[0], load_sem.at[2 + steps + i]) for i, (src, dst) in enumerate(pairs)]
    for q in range(chunks):
        own.append(
            local(hidden.at[pl.ds(q * r, r)], hid.at[pl.ds(q * group, r)], load_sem.at[2 + steps + len(pairs) + q])
        )
    for copy in loads:
        copy.start()

    barrier = pltpu.get_barrier_semaphore()
    for h in (twin, side[1], side[2]):
        signal(barrier, ctx, h)
    when(ctx > 0, lambda: signal(barrier, ctx - 1, head))
    when(ctx + 1 < ctx_n, lambda: signal(barrier, ctx + 1, head))
    pl.semaphore_wait(barrier, 3 + jnp.minimum(ctx, 1) + jnp.minimum(ctx_n - 1 - ctx, 1))

    for copy in hid_direct(0):
        copy.start()
    swaps = [remote(src, dst.at[1], swap_send.at[i], swap_recv.at[i], twin) for i, (src, dst) in enumerate(pairs)]
    for copy in own:
        copy.start()
    for copy in swaps:
        copy.start()

    if ctx_n > 2:
        when(jnp.logical_and(ctx >= 1, ctx + 2 <= ctx_n), lambda: signal(far_sem.at[2], ctx - 1, head))

    loads[0].wait()
    loads[1].wait()
    down = jnp.zeros((rows, rank + tail), jnp.float32)
    for i in range(steps):
        loads[2 + i].wait()
        span = pl.ds(i * depth, depth)
        down += product(halves(mine[:, span]), halves(wd[:, span]), NT)
    raw = down[:, :rank]
    meansq = jnp.mean(raw * raw, axis=-1, keepdims=True)
    latent = raw * lax.rsqrt(meansq + EPSILON) * gn[...]
    shared = jnp.concatenate([down[:hr, rank:], down[hr:, rank:]], axis=1)
    for h in range(2):
        for j in range(tiles):
            lat_at(0, 0, 0, h)[pl.ds(j * hr, hr), :] = latent[h * hr : (h + 1) * hr, j * LANE : (j + 1) * LANE]
        lat_at(0, 0, 0, h)[pl.ds(tiles * hr, hr // 2), :] = shared[h * hr // 2 : (h + 1) * hr // 2]

    for d in range(2, ctx_n):
        when(ctx + d < ctx_n, lambda d=d: pl.semaphore_wait(far_sem.at[d], 1))
        if d + 1 < ctx_n:
            when(
                jnp.logical_and(ctx >= 1, ctx + d < ctx_n),
                lambda d=d: signal(far_sem.at[d + 1], ctx - 1, head),
            )
    for d in range(ctx_n - 1, 0, -1):
        when(ctx + d < ctx_n, lambda d=d: z_copy(d).start())
    lat_spread(0)

    def split_query(p):
        wqh[p], wql[p] = halves(wq[p])

    hid_relay(0)
    own[0].wait()
    split_query(0)
    lat_relay(0)
    if ctx_n > 1:
        when(ctx >= 1, lambda: lat_fetch(1))
    for i in range(2):
        swaps[i].wait()
    own[1].wait()
    split_query(1)

    scale = key_width ** (-0.5)
    pad = jnp.zeros((group, lanes - rank - tail), jnp.float32)

    def queries(q):
        own[len(pairs) + q].wait()
        hid_finish(q)
        query = [jnp.zeros((group, key_width), jnp.float32) for _ in range(CORES)]
        for i in range(steps):
            span = pl.ds(i * depth, depth)
            given = halves(hid[pl.ds(q * group, group), span])
            for p in range(CORES):
                query[p] += product(given, (wqh[p, :, span], wql[p, :, span]), NT)
        for p in range(CORES):
            wide = product(halves(query[p][:, :nope] * scale), halves(wk[p]), NT)
            span = pl.ds(q * many + p * group, group)
            qh[span, :rank], ql[span, :rank] = halves(wide)
            rest = jnp.concatenate([query[p][:, nope:] * scale, pad], axis=1)
            qh[span, rank:], ql[span, rank:] = halves(rest)

    def keys(d):
        for p in range(CORES):
            for s in range(4):
                at = d * block + (p * 4 + s) * rows
                packed = jnp.concatenate(
                    [lat_at(d, p, s, h)[pl.ds(tiles * hr, hr // 2), :] for h in range(2)], axis=0
                )
                for h in range(2):
                    span = pl.ds(at + h * hr, hr)
                    for j in range(tiles):
                        lane = pl.ds(j * LANE, LANE)
                        kh[span, lane], kl[span, lane] = halves(lat_at(d, p, s, h)[pl.ds(j * hr, hr), :])
                    lane = pl.ds(rank, LANE)
                    kh[span, lane], kl[span, lane] = halves(packed if h == 0 else pltpu.roll(packed, tail, 1))

    def lat_ready(d):
        twin_own(d).wait_recv()
        twin_rest(d).wait_recv()
        keys(d)

    def place(s, parity, i):
        sx, sy = lax.rem(s, 2), lax.div(s, 2)
        x, y = lax.rem(xbit + sx, 2), lax.rem(ybit + sy, 2)
        return ((2 * y + x) * CORES + parity) * rows + i

    def attend(q, d):
        mine_q = pl.ds(q * many, many)
        those = pl.ds(d * block, block)
        scores = product((qh[mine_q, :], ql[mine_q, :]), (kh[those, :], kl[those, :]), NT)
        if d == 0:
            line = lax.rem(lax.broadcasted_iota(jnp.int32, (many, 1), 0), group)
            column = lax.broadcasted_iota(jnp.int32, (1, block), 1)
            there = lax.div(column, 4 * rows)
            column = lax.rem(column, 4 * rows)
            asked = place(lax.div(line, r), core, q * r + lax.rem(line, r))
            held = place(lax.div(column, rows), core + there - 2 * core * there, lax.rem(column, rows))
            causal = asked >= held
            scores = jnp.where(causal, scores, FLOOR)
            peak = jnp.max(scores, axis=1, keepdims=True)
        else:
            peak = jnp.maximum(top[mine_q, :], jnp.max(scores, axis=1, keepdims=True))
        weights = jnp.exp(scores - peak)
        if d == 0:
            weights = jnp.where(causal, weights, 0.0)
        mixed = product(halves(weights), (kh[those, :rank], kl[those, :rank]))
        added = jnp.sum(weights, axis=1, keepdims=True)
        if d == 0:
            total[mine_q, :] = added
            acc[mine_q, :] = mixed
        else:
            fade = jnp.exp(top[mine_q, :] - peak)
            total[mine_q, :] = total[mine_q, :] * fade + added
            acc[mine_q, :] = acc[mine_q, :] * fade + mixed
        top[mine_q, :] = peak

    def span_of(q, t):
        columns = width // cuts[q]
        return pl.ds(t * columns, columns)

    def axes_of(t):
        return (1, 2) if t % 2 == 0 else (2, 1)

    def sum_copy(q, t, j):
        first, second = axes_of(t)
        span = span_of(q, t)
        here = pl.ds(q * r, r)

        def part_of(s):
            return part.at[pl.ds(q * group + s * r, r), span]

        src, dst, target = [
            (part_of(3), mid.at[here, span], first),
            (part_of(first), near.at[here, span], first),
            (fwd.at[here, span], last.at[here, span], second),
        ][j]
        return remote(src, dst, sum_send.at[q, t, j], sum_recv.at[q, t, j], side[target])

    def project(q):
        found = []
        for p in range(CORES):
            span = pl.ds(q * many + p * group, group)
            found.append(product(halves(acc[span, :] / total[span, :]), halves(wv[p])))
        attended = halves(jnp.concatenate(found, axis=1))
        for t in range(cuts[q]):
            span = span_of(q, t)
            part[pl.ds(q * group, group), span] = product(attended, (woh[:, span], wol[:, span]))
            for j in range(2):
                sum_copy(q, t, j).start()

    def second_stage(q):
        here = pl.ds(q * r, r)
        for t in range(cuts[q]):
            span = span_of(q, t)
            sum_copy(q, t, 0).wait_recv()
            keep = axes_of(t)[1]
            fwd[here, span] = part[pl.ds(q * group + keep * r, r), span] + mid[here, span]
            sum_copy(q, t, 2).start()

    def out_copy(q, t):
        here, span = pl.ds(q * r, r), span_of(q, t)
        return local(res.at[here, span], out.at[here, span], out_sem.at[q, t])

    def collect(q):
        here = pl.ds(q * r, r)
        for t in range(cuts[q]):
            span = span_of(q, t)
            for j in (1, 2):
                sum_copy(q, t, j).wait_recv()
            res[here, span] = part[pl.ds(q * group, r), span] + near[here, span] + last[here, span]
            out_copy(q, t).start()

    def attend_all(q, ready):
        for d in range(1, ctx_n):
            def step(d=d):
                if ready:
                    lat_finish(d)
                    lat_ready(d)
                attend(q, d)

            when(d <= ctx, step)

    def split_out():
        for i in range(2, len(pairs)):
            own[i].wait()
            swaps[i].wait()
        for p in range(CORES):
            span = pl.ds(p * vdim, vdim)
            woh[span, :], wol[span, :] = halves(wo[p])

    queries(0)
    if ctx_n > 2:
        when(ctx >= 2, lambda: lat_fetch(2))
    if ctx_n > 1:
        when(ctx >= 1, lambda: lat_relay(1))
    for d in range(3, ctx_n):
        when(ctx >= d, lambda d=d: lat_fetch(d))
    lat_finish(0)
    split_out()
    lat_ready(0)
    attend(0, 0)
    for d in range(2, ctx_n):
        when(ctx >= d, lambda d=d: lat_relay(d))
    for q in range(1, chunks):
        for copy in hid_direct(q):
            copy.start()
    attend_all(0, True)
    for q in range(1, chunks):
        hid_relay(q)
    project(0)
    for q in range(1, chunks):
        queries(q)
        second_stage(q - 1)
        attend(q, 0)
        attend_all(q, False)
        project(q)
        collect(q - 1)
    second_stage(chunks - 1)
    collect(chunks - 1)

    for q in range(chunks):
        for copy in hid_direct(q) + [hid_passed(q, h) for h in range(2)]:
            copy.wait_send()
        for t in range(cuts[q]):
            for j in range(3):
                sum_copy(q, t, j).wait_send()
            out_copy(q, t).wait()
    for d in range(ctx_n):
        def drain(d=d):
            for copy in lat_direct(d) + [lat_passed(d, h) for h in range(2)] + [twin_own(d), twin_rest(d)]:
                copy.wait_send()

        when(d <= ctx, drain)
        if d > 0:
            when(ctx + d < ctx_n, lambda d=d: z_copy(d).wait_send())


def square_call(ctx_n, hidden, w_query, w_down, gain, w_key_up, w_value_up, w_out):
    rows, width = hidden.shape
    rank, nope = w_key_up.shape
    vdim = w_value_up.shape[1]
    f32, bf16, dma = jnp.float32, jnp.bfloat16, pltpu.SemaphoreType.DMA
    chunks = 2
    cuts = (2, 6)
    r = rows // chunks
    block = CORES * 4 * rows
    lanes = rank + LANE
    steps = 3 if width % 384 == 0 else 1
    slot = rows * (rank // LANE) + rows // 2
    query = (CORES,) + w_query.shape
    both = (CORES * vdim, width)
    return pl.pallas_call(
        functools.partial(square_kernel, ctx_n, chunks, cuts),
        out_shape=jax.ShapeDtypeStruct((rows, width), f32),
        in_specs=[pl.BlockSpec(memory_space=pltpu.HBM)] * 7,
        out_specs=pl.BlockSpec(memory_space=pltpu.HBM),
        scratch_shapes=[
            pltpu.VMEM((rows, width), f32),
            pltpu.VMEM((4 * rows, width), f32),
            pltpu.VMEM(w_down.shape, f32),
            pltpu.VMEM((1, rank), f32),
            pltpu.VMEM(query, f32), pltpu.VMEM(query, bf16), pltpu.VMEM(query, bf16),
            pltpu.VMEM((CORES, rank, nope), f32),
            pltpu.VMEM((CORES, rank, vdim), f32),
            pltpu.VMEM((CORES, vdim, width), f32), pltpu.VMEM(both, bf16), pltpu.VMEM(both, bf16),
            pltpu.VMEM((ctx_n * CORES * 4 * slot, LANE), f32),
            pltpu.VMEM((ctx_n * block, lanes), bf16), pltpu.VMEM((ctx_n * block, lanes), bf16),
            pltpu.VMEM((block, lanes), bf16), pltpu.VMEM((block, lanes), bf16),
            pltpu.VMEM((block, 1), f32),
            pltpu.VMEM((block, 1), f32),
            pltpu.VMEM((block, rank), f32),
            pltpu.VMEM((4 * rows, width), f32),
        ] + [pltpu.VMEM((rows, width), f32)] * 5 + [
            dma((2 + steps + 4 + chunks,)),
            dma((chunks, max(cuts))),
            dma((4,)), dma((4,)),
            dma((chunks, 3, 2)), dma((chunks, 3, 2)),
            pltpu.SemaphoreType.REGULAR((ctx_n,)),
            dma((ctx_n,)), dma((ctx_n,)),
            dma((ctx_n, 3, 2)), dma((ctx_n, 3, 2)),
            dma((ctx_n, 2)), dma((ctx_n, 2)),
            dma((chunks, max(cuts), 3)), dma((chunks, max(cuts), 3)),
        ],
        compiler_params=pltpu.CompilerParams(
            collective_id=0, has_side_effects=True, vmem_limit_bytes=60 * 1024 * 1024
        ),
    )(hidden, w_query, w_down, gain, w_key_up, w_value_up, w_out)


def on_device(ctx_n, chips, hidden, w_query, w_down, latent_gain, w_key_up, w_value_up, w_out):
    rows, width = hidden.shape
    rank, nope = w_key_up.shape
    vdim = w_value_up.shape[1]
    per_core = chips * rows
    block = CORES * per_core
    lanes = -(-w_down.shape[1] // 128) * 128
    steps = 3 if width % 384 == 0 else 1
    if chips == 4 and rows % 32 == 0 and width % 768 == 0 and rank % LANE == 0 and 2 * (w_down.shape[1] - rank) == LANE:
        return square_call(
            ctx_n, hidden, w_query.T, w_down.T, latent_gain.reshape(1, rank), w_key_up, w_value_up, w_out
        )
    square = chips == 4 and rows % 16 == 0 and width % 256 == 0
    pieces = 6 if width % 768 == 0 else 2
    f32, bf16, dma = jnp.float32, jnp.bfloat16, pltpu.SemaphoreType.DMA
    return pl.pallas_call(
        functools.partial(general_kernel, ctx_n, chips, square, steps, pieces),
        out_shape=jax.ShapeDtypeStruct((rows, width), f32),
        in_specs=[pl.BlockSpec(memory_space=pltpu.HBM)] * 7,
        out_specs=pl.BlockSpec(memory_space=pltpu.VMEM),
        scratch_shapes=[
            pltpu.VMEM((per_core, width), f32),
            pltpu.VMEM(w_down.shape[::-1], f32),
            pltpu.VMEM((CORES,) + w_query.shape[::-1], f32),
            pltpu.VMEM((1, rank), f32),
            pltpu.VMEM((CORES, rank, nope), f32),
            pltpu.VMEM((CORES, rank, vdim), f32),
            pltpu.VMEM((CORES, vdim, width), f32),
            pltpu.VMEM((ctx_n * block, lanes), f32),
            pltpu.VMEM((block, lanes), bf16),
            pltpu.VMEM((block, lanes), bf16),
            pltpu.VMEM((block, 1), f32),
            pltpu.VMEM((block, 1), f32),
            pltpu.VMEM((block, rank), f32),
            pltpu.VMEM((per_core, width), f32),
            pltpu.VMEM((per_core, width), f32),
            dma((2 + steps + 4,)),
            dma((4,)), dma((4,)),
            dma((chips, 2)), dma((chips, 2)),
            dma((ctx_n,)), dma((ctx_n,)),
            dma((ctx_n, chips, 2)), dma((ctx_n, chips, 2)),
            dma((ctx_n,)), dma((ctx_n,)),
            dma((pieces, chips)), dma((pieces, chips)),
        ],
        compiler_params=pltpu.CompilerParams(
            collective_id=0, has_side_effects=True, vmem_limit_bytes=60 * 1024 * 1024
        ),
    )(hidden, w_query.T, w_down.T, latent_gain.reshape(1, rank), w_key_up, w_value_up, w_out)


def solution(mesh):
    placed = (
        P(("ctx", "head"), None),
        P(None, "head"),
        P(),
        P(),
        P(None, "head"),
        P(None, "head"),
        P("head", None),
    )
    body = functools.partial(on_device, mesh.shape["ctx"], mesh.shape["head"] // CORES)
    return jax.shard_map(
        body, mesh=mesh, in_specs=placed, out_specs=P(("ctx", "head"), None), check_vma=False
    )
```

```python
import functools

import jax
import jax.numpy as jnp
from jax import lax
from jax.experimental import pallas as pl
from jax.experimental.pallas import tpu as pltpu
from jax.sharding import PartitionSpec as P

EPSILON = 1e-06
FLOOR = -1e30
CORES = 2
LANE = 128
FIRST = ((1, 0), (2, 1))
DIRECT = ((1, 0), (2, 1), (1, 1), (2, 0))
REST = ((1, 1), (2, 0), (3, 0), (3, 1))
MESH = pl.DeviceIdType.MESH
NN = (((1,), (0,)), ((), ()))
NT = (((1,), (1,)), ((), ()))


def halves(value):
    high = value.astype(jnp.bfloat16)
    return high, (value - high.astype(jnp.float32)).astype(jnp.bfloat16)


def product(left, right, dims=NN):
    (lh, ll), (rh, rl) = left, right
    dot = functools.partial(lax.dot_general, dimension_numbers=dims, preferred_element_type=jnp.float32)
    return dot(lh, rh) + (dot(ll, rh) + dot(lh, rl))


def stacked(left, right, dims=NN):
    (lh, ll), (rh, rl) = left, right
    dot = functools.partial(lax.dot_general, dimension_numbers=dims, preferred_element_type=jnp.float32)
    both = dot(jnp.concatenate([lh, ll], axis=0), rh)
    size = lh.shape[0]
    return both[:size] + (both[size:] + dot(lh, rl))


def general_kernel(
    ctx_n, chips, square, steps, pieces,
    hidden, w_query, w_down, gain, w_key, w_value, w_out, out,
    hid, wd, wq, gn, wk, wv, wo, lat, qh, ql, top, total, acc, part, landed,
    load_sem, swap_send, swap_recv, hid_send, hid_recv, col_send, col_recv,
    row_send, row_recv, twin_send, twin_recv, sum_send, sum_recv,
):
    rows, width = hidden.shape
    parts = 2 if square else 1
    rank = gn.shape[1]
    tail = wd.shape[0] - rank
    nope = wk.shape[2]
    per_core = chips * rows
    block = CORES * per_core
    lanes = lat.shape[1]
    ctx = lax.axis_index("ctx")
    head = lax.axis_index("head")
    chip, core = head // CORES, head % CORES
    twin = chip * CORES + (1 - core)

    def chip_at(offset):
        return lax.rem(chip + offset, chips)

    def to(o):
        if not square:
            return chip_at(o)
        return [chip, chip + 1 - 2 * lax.rem(chip, 2), lax.rem(chip + 2, 4), 3 - chip][o]

    def origin(o):
        return to(o) if square else chip_at(chips - o)

    def local(src, dst, sem):
        return pltpu.make_async_copy(src, dst, load_sem.at[sem])

    def remote(src, dst, send, recv, c, h):
        return pltpu.make_async_remote_copy(
            src_ref=src, dst_ref=dst, send_sem=send, recv_sem=recv,
            device_id={"ctx": c, "head": h}, device_id_type=MESH,
        )

    def at_rows(start, size):
        return pl.ds(pl.multiple_of(start, 8), size)

    my_hid = hid.at[at_rows(chip * rows, rows)]
    depth = width // steps
    loads = [local(hidden, my_hid, 0), local(gain, gn, 1)]
    for s in range(steps):
        span = pl.ds(s * depth, depth)
        loads.append(local(w_down.at[:, span], wd.at[:, span], 2 + s))
    pairs = [(w_query, wq), (w_key, wk), (w_value, wv), (w_out, wo)]
    own = [local(src, dst.at[core], 2 + steps + i) for i, (src, dst) in enumerate(pairs)]
    for copy in loads:
        copy.start()

    barrier = pltpu.get_barrier_semaphore()
    for o in range(1, chips):
        pl.semaphore_signal(barrier, inc=1, device_id={"ctx": ctx, "head": chip_at(o) * CORES + core}, device_id_type=MESH)
    pl.semaphore_signal(barrier, inc=1, device_id={"ctx": ctx, "head": twin}, device_id_type=MESH)
    for o in range(1, ctx_n):
        pl.semaphore_signal(barrier, inc=1, device_id={"ctx": lax.rem(ctx + o, ctx_n), "head": head}, device_id_type=MESH)
    pl.semaphore_wait(barrier, chips - 1 + 1 + ctx_n - 1)

    def share(source, spot, send, recv):
        def start_of(o, h):
            target = to(o)
            return remote(source(h), spot(chip, h), send(o, h), recv(o, h), ctx, target * CORES + core)

        def seen(o, h):
            place_of = spot(origin(o), h)
            return remote(place_of, place_of, send(o, h), recv(o, h), ctx, twin)

        def passed(h):
            place_of = spot(to(1 + h), h)
            return remote(place_of, place_of, send(3, h), recv(3, h), ctx, to(2 - h) * CORES + core)

        direct = [(1, 0), (2, 1), (1, 1), (2, 0)] if square else [(o, 0) for o in range(1, chips)]

        def start():
            for o, h in direct:
                start_of(o, h).start()

        def relay():
            if square:
                for h in range(2):
                    seen(1 + h, h).wait_recv()
                    passed(h).start()

        def finish():
            for o, h in [(1, 1), (2, 0), (3, 0), (3, 1)] if square else direct:
                seen(o, h).wait_recv()

        def drain():
            for o, h in direct:
                start_of(o, h).wait_send()
            if square:
                for h in range(2):
                    passed(h).wait_send()

        return start, relay, finish, drain

    half = width // parts

    def hid_half(h):
        return pl.ds(h * half, half)

    hid_start, hid_relay, hid_finish, hid_drain = share(
        lambda h: hidden.at[:, hid_half(h)],
        lambda k, h: hid.at[at_rows(k * rows, rows), hid_half(h)],
        lambda o, h: hid_send.at[o, h],
        lambda o, h: hid_recv.at[o, h],
    )
    hid_start()
    swaps = [remote(src, dst.at[core], swap_send.at[i], swap_recv.at[i], ctx, twin) for i, (src, dst) in enumerate(pairs)]
    for copy in own:
        copy.start()
    for copy in swaps:
        copy.start()

    loads[0].wait()
    loads[1].wait()
    down = jnp.zeros((rows, rank + tail), jnp.float32)
    for s in range(steps):
        loads[2 + s].wait()
        span = pl.ds(s * depth, depth)
        down += product(halves(my_hid[:, span]), halves(wd[:, span]), NT)
    raw = down[:, :rank]
    meansq = jnp.mean(raw * raw, axis=-1, keepdims=True)
    blank = jnp.zeros((rows, lanes - rank - tail), jnp.float32)

    def place(b, p, k):
        return ((b * CORES + p) * chips + k) * rows

    mine = at_rows(place(ctx, core, chip), rows)
    lat[mine, :rank] = raw * lax.rsqrt(meansq + EPSILON) * gn[...]
    lat[mine, rank:] = jnp.concatenate([down[:, rank:], blank], axis=1)

    def col_copy(b):
        spot = lat.at[at_rows(place(b, core, chip), rows)]
        return remote(spot, spot, col_send.at[b], col_recv.at[b], jnp.minimum(ctx + 1, ctx_n - 1), head)

    def latents(b):
        def spot(k, h):
            return lat.at[at_rows(place(b, core, k) + h * (rows // parts), rows // parts)]

        return share(
            lambda h: spot(chip, h), spot, lambda o, h: row_send.at[b, o, h], lambda o, h: row_recv.at[b, o, h]
        )

    def twin_copy(b, p):
        spot = lat.at[at_rows(place(b, p, 0), per_core)]
        return remote(spot, spot, twin_send.at[b], twin_recv.at[b], ctx, twin)

    def spread(b):
        @pl.when(ctx + 1 < ctx_n)
        def _():
            col_copy(b).start()

        latents(b)[0]()

    def gather_rows(b):
        latents(b)[2]()
        twin_copy(b, core).start()

    spread(ctx)
    hid_relay()
    for d in range(1, ctx_n):
        @pl.when(d <= ctx)
        def _():
            col_copy(ctx - d).wait_recv()
            spread(ctx - d)

    latents(ctx)[1]()

    hid_finish()
    for i in range(2):
        own[i].wait()
        swaps[i].wait()
    scale = wq.shape[1] ** (-0.5)
    pad = jnp.zeros((per_core, lanes - rank - tail), jnp.float32)
    query = [jnp.zeros((per_core, wq.shape[1]), jnp.float32) for _ in range(CORES)]
    for s in range(steps):
        span = pl.ds(s * depth, depth)
        piece = halves(hid[:, span])
        for p in range(CORES):
            query[p] += product(piece, halves(wq[p, :, span]), NT)
    for p in range(CORES):
        wide = product(halves(query[p][:, :nope] * scale), halves(wk[p]), NT)
        span = pl.ds(p * per_core, per_core)
        qh[span, :rank], ql[span, :rank] = halves(wide)
        qh[span, rank:], ql[span, rank:] = halves(jnp.concatenate([query[p][:, nope:] * scale, pad], axis=1))

    def spots(index, parity):
        inner = lax.rem(index, per_core)
        return (lax.div(inner, rows) * CORES + parity) * rows + lax.rem(inner, rows)

    def attend(b, first):
        keys = halves(lat[at_rows(place(b, 0, 0), block), :])
        scores = product((qh[...], ql[...]), keys, NT)
        if first:
            line = lax.broadcasted_iota(jnp.int32, (block, 1), 0)
            column = lax.broadcasted_iota(jnp.int32, (1, block), 1)
            causal = spots(line, core) >= spots(column, lax.div(column, per_core))
            scores = jnp.where(causal, scores, FLOOR)
            peak = jnp.max(scores, axis=1, keepdims=True)
        else:
            peak = jnp.maximum(top[...], jnp.max(scores, axis=1, keepdims=True))
        weights = jnp.exp(scores - peak)
        if first:
            weights = jnp.where(causal, weights, 0.0)
        mixed = product(halves(weights), (keys[0][:, :rank], keys[1][:, :rank]))
        added = jnp.sum(weights, axis=1, keepdims=True)
        if first:
            total[...] = added
            acc[...] = mixed
        else:
            fade = jnp.exp(top[...] - peak)
            total[...] = total[...] * fade + added
            acc[...] = acc[...] * fade + mixed
        top[...] = peak

    def relay_at(d):
        if d < ctx_n:
            @pl.when(d <= ctx)
            def _():
                latents(ctx - d)[1]()

    relay_at(1)
    gather_rows(ctx)
    twin_copy(ctx, 1 - core).wait_recv()
    attend(ctx, True)
    for d in range(1, ctx_n):
        @pl.when(d <= ctx)
        def _():
            relay_at(d + 1)
            gather_rows(ctx - d)
            twin_copy(ctx - d, 1 - core).wait_recv()
            attend(ctx - d, False)

    for i in range(2, 4):
        own[i].wait()
        swaps[i].wait()
    heads = []
    for p in range(CORES):
        span = pl.ds(p * per_core, per_core)
        heads.append(product(halves(acc[span, :] / total[span, :]), halves(wv[p])))
    attended = halves(jnp.concatenate(heads, axis=1))
    columns = width // pieces

    def cut(ref, k, t):
        return ref.at[at_rows(k * rows, rows), pl.ds(t * columns, columns)]

    def axes_of(t):
        return (1, 2) if t % 2 == 0 else (2, 1)

    def sum_copy(t, j):
        if not square:
            return remote(
                cut(part, chip_at(j), t), cut(landed, chip, t), sum_send.at[t, j], sum_recv.at[t, j],
                ctx, chip_at(j) * CORES + core,
            )
        first, second = axes_of(t)
        src = [to(3), to(first), to(second)][j]
        dst = [to(3), to(first), to(3)][j]
        target = [to(first), to(first), to(second)][j]
        return remote(cut(part, src, t), cut(landed, dst, t), sum_send.at[t, j], sum_recv.at[t, j], ctx, target * CORES + core)

    def second_stage(t):
        sum_copy(t, 0).wait_recv()
        keep = to(axes_of(t)[1])
        cut(part, keep, t)[...] = cut(part, keep, t)[...] + cut(landed, keep, t)[...]
        sum_copy(t, 2).start()

    kinds = (0, 1) if square else tuple(range(1, chips))
    for t in range(pieces):
        span = pl.ds(t * columns, columns)
        weight = jnp.concatenate([wo[p, :, span] for p in range(CORES)], axis=0)
        part[:, span] = product(attended, halves(weight))
        for j in kinds:
            sum_copy(t, j).start()
        if square and t >= 2:
            second_stage(t - 2)
    if square:
        for t in range(max(pieces - 2, 0), pieces):
            second_stage(t)
    for t in range(pieces):
        result = cut(part, chip, t)[...]
        if square:
            for j in (1, 2):
                sum_copy(t, j).wait_recv()
            result += cut(landed, chip, t)[...] + cut(landed, to(axes_of(t)[0]), t)[...]
        else:
            for j in kinds:
                sum_copy(t, j).wait_recv()
                result += cut(landed, origin(j), t)[...]
        out[:, pl.ds(t * columns, columns)] = result

    hid_drain()
    for t in range(pieces):
        for j in kinds + ((2,) if square else ()):
            sum_copy(t, j).wait_send()
    for d in range(ctx_n):
        @pl.when(d <= ctx)
        def _():
            @pl.when(ctx + 1 < ctx_n)
            def _():
                col_copy(ctx - d).wait_send()

            latents(ctx - d)[3]()
            twin_copy(ctx - d, core).wait_send()


def square_kernel(
    ctx_n, chunks, cuts,
    hidden, w_query, w_down, gain, w_key, w_value, w_out, out,
    mine, hid, wd, gn, wq, wqh, wql, wk, wv, wo, woh, wol, lat, kh, kl, qh, ql, top, total, acc,
    part, mid, fwd, near, last, res,
    load_sem, out_sem, swap_send, swap_recv, hid_send, hid_recv, far_sem, z_send, z_recv,
    lat_send, lat_recv, twin_recv, sum_send, sum_recv,
):
    rows, width = hidden.shape
    rank = gn.shape[1]
    tail = wd.shape[0] - rank
    nope, vdim = wk.shape[2], wv.shape[2]
    key_width = wq.shape[1]
    lanes = kh.shape[1]
    r = rows // chunks
    group = 4 * r
    many = CORES * group
    block = CORES * 4 * rows
    hr = rows // 2
    tiles = rank // LANE
    piece = hr * tiles + hr // 2
    slot = 2 * piece
    half = width // 2
    steps = 3 if width % 384 == 0 else 1
    depth = width // steps
    ctx = lax.axis_index("ctx")
    head = lax.axis_index("head")
    chip, core = head // CORES, head % CORES
    twin = chip * CORES + (1 - core)
    xbit, ybit = lax.rem(chip, 2), lax.div(chip, 2)
    side = [None, (2 * ybit + 1 - xbit) * CORES + core, (2 * (1 - ybit) + xbit) * CORES + core]

    def local(src, dst, sem):
        return pltpu.make_async_copy(src, dst, sem)

    def remote(src, dst, send, recv, h, c=ctx):
        return pltpu.make_async_remote_copy(
            src_ref=src, dst_ref=dst, send_sem=send, recv_sem=recv,
            device_id={"ctx": c, "head": h}, device_id_type=MESH,
        )

    def signal(sem, c, h):
        pl.semaphore_signal(sem, inc=1, device_id={"ctx": c, "head": h}, device_id_type=MESH)

    def when(condition, *actions):
        @pl.when(condition)
        def _():
            for action in actions:
                action()

    def spot(q, s, h):
        return hid.at[pl.ds((q * 4 + s) * r, r), pl.ds(h * half, half)]

    def hid_direct(q, order):
        for a, h in order:
            remote(
                hidden.at[pl.ds(q * r, r), pl.ds(h * half, half)], spot(q, a, h),
                hid_send.at[0], hid_recv.at[q, h if (a, h) in FIRST else 2], side[a],
            ).start()

    def hid_relay(q):
        for h in range(2):
            landed = spot(q, 1 + h, h)
            remote(landed, landed, hid_send.at[0], hid_recv.at[q, h], twin).wait_recv()
            remote(landed, spot(q, 3, h), hid_send.at[0], hid_recv.at[q, 2], side[2 - h]).start()

    def hid_finish(q):
        landed = hid.at[pl.ds((q * 4 + 1) * r, 2 * r)]
        remote(landed, landed, hid_send.at[0], hid_recv.at[q, 2], twin).wait_recv()

    def lat_at(d, p, s, h=0, size=piece):
        return lat.at[pl.ds(((d * CORES + p) * 4 + s) * slot + h * piece, size)]

    def lat_twin(d, s, count):
        size = count * slot
        remote(lat_at(d, 0, s, 0, size), lat_at(d, 1, s, 0, size), lat_send.at[d], twin_recv.at[d], twin).start()

    def z_copy(d, s, h, size):
        c = jnp.minimum(ctx + d, ctx_n - 1)
        return remote(lat_at(0, 0, s, h, size), lat_at(d, 0, s, h, size), z_send.at[d - 1], z_recv.at[d - 1], head, c)

    def z_wait(d):
        landed = lat_at(d, 0, 0, 0, 4 * slot if d == 1 else slot)
        remote(landed, landed, z_send.at[d - 1], z_recv.at[d - 1], head).wait_recv()

    def lat_spread(d):
        for a, h in DIRECT:
            remote(
                lat_at(d, 0, 0, h), lat_at(d, 0, a, h), lat_send.at[d],
                lat_recv.at[d, h if (a, h) in FIRST else 2], side[a],
            ).start()
        lat_twin(d, 0, 1)

    def lat_fetch(d):
        z_wait(d)
        lat_spread(d)

    def lat_relay(d):
        for h in range(2):
            landed = lat_at(d, 0, 1 + h, h)
            remote(landed, landed, lat_send.at[d], lat_recv.at[d, h], twin).wait_recv()
            remote(landed, lat_at(d, 0, 3, h), lat_send.at[d], lat_recv.at[d, 2], side[2 - h]).start()

    def lat_finish(d):
        landed = lat_at(d, 0, 1, 0, 2 * slot)
        remote(landed, landed, lat_send.at[d], lat_recv.at[d, 2], twin).wait_recv()
        lat_twin(d, 1, 3)

    def z_begin():
        z_copy(1, 0, 0, slot).start()
        z_copy(1, 1, 0, piece).start()
        z_copy(1, 2, 1, piece).start()

    def z_end():
        z_copy(1, 1, 1, 2 * piece).start()
        z_copy(1, 3, 0, slot).start()

    loads = [local(hidden, mine, load_sem.at[0]), local(gain, gn, load_sem.at[1])]
    for i in range(steps):
        span = pl.ds(i * depth, depth)
        loads.append(local(w_down.at[:, span], wd.at[:, span], load_sem.at[2 + i]))
    pairs = [(w_query, wq), (w_key, wk), (w_value, wv), (w_out, wo)]
    lots = (0, 1, 1, 2)
    own = [local(src, dst.at[0], load_sem.at[2 + steps + lot]) for (src, dst), lot in zip(pairs, lots)]
    for q in range(chunks):
        own.append(local(hidden.at[pl.ds(q * r, r)], hid.at[pl.ds(q * group, r)], load_sem.at[5 + steps]))
    for copy in loads:
        copy.start()

    barrier = pltpu.get_barrier_semaphore()
    for h in (twin, side[1], side[2]):
        signal(barrier, ctx, h)
    when(ctx > 0, lambda: signal(barrier, ctx - 1, head))
    when(ctx + 1 < ctx_n, lambda: signal(barrier, ctx + 1, head))
    pl.semaphore_wait(barrier, 3 + jnp.minimum(ctx, 1) + jnp.minimum(ctx_n - 1 - ctx, 1))

    hid_direct(0, FIRST + REST[:2])
    swaps = [
        remote(src, dst.at[1], swap_send.at[lot], swap_recv.at[lot], twin) for (src, dst), lot in zip(pairs, lots)
    ]
    for copy in own:
        copy.start()
    for copy in swaps:
        copy.start()

    if ctx_n > 2:
        when(jnp.logical_and(ctx >= 1, ctx + 2 <= ctx_n), lambda: signal(far_sem.at[0], ctx - 1, head))

    loads[0].wait()
    loads[1].wait()
    down = jnp.zeros((rows, rank + tail), jnp.float32)
    for i in range(steps):
        loads[2 + i].wait()
        span = pl.ds(i * depth, depth)
        down += stacked(halves(mine[:, span]), halves(wd[:, span]), NT)
    raw = down[:, :rank]
    meansq = jnp.mean(raw * raw, axis=-1, keepdims=True)
    latent = raw * lax.rsqrt(meansq + EPSILON) * gn[...]
    shared = jnp.concatenate([down[:hr, rank:], down[hr:, rank:]], axis=1)
    for h in range(2):
        for j in range(tiles):
            lat_at(0, 0, 0, h)[pl.ds(j * hr, hr), :] = latent[h * hr : (h + 1) * hr, j * LANE : (j + 1) * LANE]
        lat_at(0, 0, 0, h)[pl.ds(tiles * hr, hr // 2), :] = shared[h * hr // 2 : (h + 1) * hr // 2]

    for d in range(2, ctx_n):
        when(ctx + d < ctx_n, lambda d=d: pl.semaphore_wait(far_sem.at[d - 2], 1))
        if d + 1 < ctx_n:
            when(
                jnp.logical_and(ctx >= 1, ctx + d < ctx_n),
                lambda d=d: signal(far_sem.at[d - 1], ctx - 1, head),
            )
    for d in range(ctx_n - 1, 1, -1):
        when(ctx + d < ctx_n, lambda d=d: z_copy(d, 0, 0, slot).start())
    lat_spread(0)

    def split_query(p):
        wqh[p], wql[p] = halves(wq[p])

    def kept(lot):
        whole = {0: wq.at[0], 1: wk, 2: wo.at[0]}[lot]
        local(whole, whole, load_sem.at[2 + steps + lot]).wait()
        remote(whole, whole, swap_send.at[lot], swap_recv.at[lot], twin).wait()

    hid_relay(0)
    own[0].wait()
    split_query(0)
    lat_relay(0)
    if ctx_n > 1:
        when(ctx + 1 < ctx_n, z_begin)
    for q in range(1, chunks):
        hid_direct(q, FIRST)
    swaps[0].wait()
    split_query(1)
    for d in range(2, ctx_n):
        when(ctx >= d, lambda d=d: lat_fetch(d))
    lat_finish(0)
    if ctx_n > 1:
        when(ctx + 1 < ctx_n, z_end)
    kept(1)
    local(mine, mine, load_sem.at[5 + steps]).wait()

    scale = key_width ** (-0.5)
    pad = jnp.zeros((group, lanes - rank - tail), jnp.float32)

    def queries(q):
        hid_finish(q)
        query = [jnp.zeros((group, key_width), jnp.float32) for _ in range(CORES)]
        for i in range(steps):
            span = pl.ds(i * depth, depth)
            given = halves(hid[pl.ds(q * group, group), span])
            for p in range(CORES):
                query[p] += stacked(given, (wqh[p, :, span], wql[p, :, span]), NT)
        for p in range(CORES):
            wide = stacked(halves(query[p][:, :nope] * scale), halves(wk[p]), NT)
            span = pl.ds(q * many + p * group, group)
            qh[span, :rank], ql[span, :rank] = halves(wide)
            rest = jnp.concatenate([query[p][:, nope:] * scale, pad], axis=1)
            qh[span, rank:], ql[span, rank:] = halves(rest)

    def keys(d):
        for p in range(CORES):
            for s in range(4):
                at = d * block + (p * 4 + s) * rows
                packed = jnp.concatenate(
                    [lat_at(d, p, s, h)[pl.ds(tiles * hr, hr // 2), :] for h in range(2)], axis=0
                )
                for h in range(2):
                    span = pl.ds(at + h * hr, hr)
                    for j in range(tiles):
                        lane = pl.ds(j * LANE, LANE)
                        kh[span, lane], kl[span, lane] = halves(lat_at(d, p, s, h)[pl.ds(j * hr, hr), :])
                    lane = pl.ds(rank, LANE)
                    kh[span, lane], kl[span, lane] = halves(packed if h == 0 else pltpu.roll(packed, tail, 1))

    def lat_ready(d):
        landed = lat_at(d, 1, 0, 0, 4 * slot)
        remote(landed, landed, lat_send.at[d], twin_recv.at[d], twin).wait_recv()
        keys(d)

    def place(s, parity, i):
        sx, sy = lax.rem(s, 2), lax.div(s, 2)
        x, y = lax.rem(xbit + sx, 2), lax.rem(ybit + sy, 2)
        return ((2 * y + x) * CORES + parity) * rows + i

    def attend(q, d):
        mine_q = pl.ds(q * many, many)
        those = pl.ds(d * block, block)
        scores = stacked((qh[mine_q, :], ql[mine_q, :]), (kh[those, :], kl[those, :]), NT)
        if d == 0:
            line = lax.rem(lax.broadcasted_iota(jnp.int32, (many, 1), 0), group)
            column = lax.broadcasted_iota(jnp.int32, (1, block), 1)
            there = lax.div(column, 4 * rows)
            column = lax.rem(column, 4 * rows)
            asked = place(lax.div(line, r), core, q * r + lax.rem(line, r))
            held = place(lax.div(column, rows), core + there - 2 * core * there, lax.rem(column, rows))
            causal = asked >= held
            scores = jnp.where(causal, scores, FLOOR)
            peak = jnp.max(scores, axis=1, keepdims=True)
        else:
            peak = jnp.maximum(top[mine_q, :], jnp.max(scores, axis=1, keepdims=True))
        weights = jnp.exp(scores - peak)
        if d == 0:
            weights = jnp.where(causal, weights, 0.0)
        mixed = stacked(halves(weights), (kh[those, :rank], kl[those, :rank]))
        added = jnp.sum(weights, axis=1, keepdims=True)
        if d == 0:
            total[mine_q, :] = added
            acc[mine_q, :] = mixed
        else:
            fade = jnp.exp(top[mine_q, :] - peak)
            total[mine_q, :] = total[mine_q, :] * fade + added
            acc[mine_q, :] = acc[mine_q, :] * fade + mixed
        top[mine_q, :] = peak

    def span_of(q, t):
        columns = width // cuts[q]
        return pl.ds(t * columns, columns)

    def axes_of(t):
        return (1, 2) if t % 2 == 0 else (2, 1)

    def sum_copy(q, t, j):
        first, second = axes_of(t)
        span = span_of(q, t)
        here = pl.ds(q * r, r)

        def part_of(s):
            return part.at[pl.ds(q * group + s * r, r), span]

        src, dst, target = [
            (part_of(3), mid.at[here, span], first),
            (part_of(first), near.at[here, span], first),
            (fwd.at[here, span], last.at[here, span], second),
        ][j]
        return remote(src, dst, sum_send.at[0], sum_recv.at[sum(cuts[:q]) + t, min(j, 1)], side[target])

    def project(q):
        found = []
        for p in range(CORES):
            span = pl.ds(q * many + p * group, group)
            found.append(stacked(halves(acc[span, :] / total[span, :]), halves(wv[p])))
        attended = halves(jnp.concatenate(found, axis=1))
        for t in range(cuts[q]):
            span = span_of(q, t)
            part[pl.ds(q * group, group), span] = stacked(attended, (woh[:, span], wol[:, span]))
            for j in range(2):
                sum_copy(q, t, j).start()

    def second_stage(q):
        here = pl.ds(q * r, r)
        for t in range(cuts[q]):
            span = span_of(q, t)
            sum_copy(q, t, 0).wait_recv()
            keep = axes_of(t)[1]
            fwd[here, span] = part[pl.ds(q * group + keep * r, r), span] + mid[here, span]
            sum_copy(q, t, 2).start()

    def out_copy(q, t):
        here, span = pl.ds(q * r, r), span_of(q, t)
        return local(res.at[here, span], out.at[here, span], out_sem.at[0])

    def collect(q):
        here = pl.ds(q * r, r)
        for t in range(cuts[q]):
            span = span_of(q, t)
            landed = near.at[pl.ds(0, 2 * r), span]
            remote(landed, landed, sum_send.at[0], sum_recv.at[sum(cuts[:q]) + t, 1], twin).wait_recv()
            res[here, span] = part[pl.ds(q * group, r), span] + near[here, span] + last[here, span]
            out_copy(q, t).start()

    def attend_late(q, d, ready):
        def step():
            if ready and d == 1:
                z_wait(1)
                lat_twin(1, 0, 4)
            elif ready:
                lat_finish(d)
            if ready:
                lat_ready(d)
            attend(q, d)

        when(d <= ctx, step)

    def split_out():
        kept(2)
        for p in range(CORES):
            span = pl.ds(p * vdim, vdim)
            woh[span, :], wol[span, :] = halves(wo[p])

    late = list(range(2, ctx_n)) + [1] * (ctx_n > 1)
    queries(0)
    lat_ready(0)
    attend(0, 0)
    split_out()
    for d in range(2, ctx_n):
        when(ctx >= d, lambda d=d: lat_relay(d))
    for q in range(1, chunks):
        hid_relay(q)
        hid_direct(q, REST[:2])
    for d in late:
        attend_late(0, d, True)
    project(0)
    for q in range(1, chunks):
        queries(q)
        attend(q, 0)
        for d in late[:1]:
            attend_late(q, d, False)
        second_stage(q - 1)
        for d in late[1:]:
            attend_late(q, d, False)
        project(q)
        collect(q - 1)
    second_stage(chunks - 1)
    collect(chunks - 1)

    sent = hid.at[pl.ds(0, 3 * rows)]
    for sem in (hid_send.at[0], sum_send.at[0]):
        remote(sent, sent, sem, hid_recv.at[0, 0], twin).wait_send()
    local(res, out, out_sem.at[0]).wait()
    for d in range(ctx_n):
        def drain(d=d):
            sent = lat.at[pl.ds(0, (4 if d == 1 else 7) * slot)]
            remote(sent, sent, lat_send.at[d], twin_recv.at[d], twin).wait_send()

        def z_drain(d=d):
            sent = lat.at[pl.ds(0, (4 if d == 1 else 1) * slot)]
            remote(sent, sent, z_send.at[d - 1], z_recv.at[d - 1], head).wait_send()

        when(d <= ctx, drain)
        if d > 0:
            when(ctx + d < ctx_n, z_drain)


def square_call(ctx_n, hidden, w_query, w_down, gain, w_key_up, w_value_up, w_out):
    rows, width = hidden.shape
    rank, nope = w_key_up.shape
    vdim = w_value_up.shape[1]
    f32, bf16, dma = jnp.float32, jnp.bfloat16, pltpu.SemaphoreType.DMA
    chunks = 2
    cuts = (2, 6)
    r = rows // chunks
    block = CORES * 4 * rows
    lanes = rank + LANE
    steps = 3 if width % 384 == 0 else 1
    slot = rows * (rank // LANE) + rows // 2
    query = (CORES,) + w_query.shape
    both = (CORES * vdim, width)
    return pl.pallas_call(
        functools.partial(square_kernel, ctx_n, chunks, cuts),
        out_shape=jax.ShapeDtypeStruct((rows, width), f32),
        in_specs=[pl.BlockSpec(memory_space=pltpu.HBM)] * 7,
        out_specs=pl.BlockSpec(memory_space=pltpu.HBM),
        scratch_shapes=[
            pltpu.VMEM((rows, width), f32),
            pltpu.VMEM((4 * rows, width), f32),
            pltpu.VMEM(w_down.shape, f32),
            pltpu.VMEM((1, rank), f32),
            pltpu.VMEM(query, f32), pltpu.VMEM(query, bf16), pltpu.VMEM(query, bf16),
            pltpu.VMEM((CORES, rank, nope), f32),
            pltpu.VMEM((CORES, rank, vdim), f32),
            pltpu.VMEM((CORES, vdim, width), f32), pltpu.VMEM(both, bf16), pltpu.VMEM(both, bf16),
            pltpu.VMEM((ctx_n * CORES * 4 * slot, LANE), f32),
            pltpu.VMEM((ctx_n * block, lanes), bf16), pltpu.VMEM((ctx_n * block, lanes), bf16),
            pltpu.VMEM((block, lanes), bf16), pltpu.VMEM((block, lanes), bf16),
            pltpu.VMEM((block, 1), f32),
            pltpu.VMEM((block, 1), f32),
            pltpu.VMEM((block, rank), f32),
            pltpu.VMEM((4 * rows, width), f32),
        ] + [pltpu.VMEM((rows, width), f32)] * 5 + [
            dma((6 + steps,)),
            dma((1,)),
            dma((3,)), dma((3,)),
            dma((1,)), dma((chunks, 3)),
            pltpu.SemaphoreType.REGULAR((max(ctx_n - 2, 1),)),
            dma((max(ctx_n - 1, 1),)), dma((max(ctx_n - 1, 1),)),
            dma((ctx_n,)), dma((ctx_n, 3)),
            dma((ctx_n,)),
            dma((1,)), dma((sum(cuts), 2)),
        ],
        compiler_params=pltpu.CompilerParams(
            collective_id=0, has_side_effects=True, vmem_limit_bytes=60 * 1024 * 1024
        ),
    )(hidden, w_query, w_down, gain, w_key_up, w_value_up, w_out)


def on_device(ctx_n, chips, hidden, w_query, w_down, latent_gain, w_key_up, w_value_up, w_out):
    rows, width = hidden.shape
    rank, nope = w_key_up.shape
    vdim = w_value_up.shape[1]
    per_core = chips * rows
    block = CORES * per_core
    lanes = -(-w_down.shape[1] // 128) * 128
    steps = 3 if width % 384 == 0 else 1
    if chips == 4 and rows % 32 == 0 and width % 768 == 0 and rank % LANE == 0 and 2 * (w_down.shape[1] - rank) == LANE:
        return square_call(
            ctx_n, hidden, w_query.T, w_down.T, latent_gain.reshape(1, rank), w_key_up, w_value_up, w_out
        )
    square = chips == 4 and rows % 16 == 0 and width % 256 == 0
    pieces = 6 if width % 768 == 0 else 2
    f32, bf16, dma = jnp.float32, jnp.bfloat16, pltpu.SemaphoreType.DMA
    return pl.pallas_call(
        functools.partial(general_kernel, ctx_n, chips, square, steps, pieces),
        out_shape=jax.ShapeDtypeStruct((rows, width), f32),
        in_specs=[pl.BlockSpec(memory_space=pltpu.HBM)] * 7,
        out_specs=pl.BlockSpec(memory_space=pltpu.VMEM),
        scratch_shapes=[
            pltpu.VMEM((per_core, width), f32),
            pltpu.VMEM(w_down.shape[::-1], f32),
            pltpu.VMEM((CORES,) + w_query.shape[::-1], f32),
            pltpu.VMEM((1, rank), f32),
            pltpu.VMEM((CORES, rank, nope), f32),
            pltpu.VMEM((CORES, rank, vdim), f32),
            pltpu.VMEM((CORES, vdim, width), f32),
            pltpu.VMEM((ctx_n * block, lanes), f32),
            pltpu.VMEM((block, lanes), bf16),
            pltpu.VMEM((block, lanes), bf16),
            pltpu.VMEM((block, 1), f32),
            pltpu.VMEM((block, 1), f32),
            pltpu.VMEM((block, rank), f32),
            pltpu.VMEM((per_core, width), f32),
            pltpu.VMEM((per_core, width), f32),
            dma((2 + steps + 4,)),
            dma((4,)), dma((4,)),
            dma((chips, 2)), dma((chips, 2)),
            dma((ctx_n,)), dma((ctx_n,)),
            dma((ctx_n, chips, 2)), dma((ctx_n, chips, 2)),
            dma((ctx_n,)), dma((ctx_n,)),
            dma((pieces, chips)), dma((pieces, chips)),
        ],
        compiler_params=pltpu.CompilerParams(
            collective_id=0, has_side_effects=True, vmem_limit_bytes=60 * 1024 * 1024
        ),
    )(hidden, w_query.T, w_down.T, latent_gain.reshape(1, rank), w_key_up, w_value_up, w_out)


def solution(mesh):
    placed = (
        P(("ctx", "head"), None),
        P(None, "head"),
        P(),
        P(),
        P(None, "head"),
        P(None, "head"),
        P("head", None),
    )
    body = functools.partial(on_device, mesh.shape["ctx"], mesh.shape["head"] // CORES)
    return jax.shard_map(
        body, mesh=mesh, in_specs=placed, out_specs=P(("ctx", "head"), None), check_vma=False
    )
```

```python
import functools

import jax
import jax.numpy as jnp
from jax import lax
from jax.experimental import pallas as pl
from jax.experimental.pallas import tpu as pltpu
from jax.sharding import PartitionSpec as P

EPSILON = 1e-06
FLOOR = -1e30
CORES = 2
LANE = 128
FIRST = ((1, 0), (2, 1))
DIRECT = ((1, 0), (2, 1), (1, 1), (2, 0))
REST = ((1, 1), (2, 0), (3, 0), (3, 1))
MESH = pl.DeviceIdType.MESH
NN = (((1,), (0,)), ((), ()))
NT = (((1,), (1,)), ((), ()))


def halves(value):
    high = value.astype(jnp.bfloat16)
    return high, (value - high.astype(jnp.float32)).astype(jnp.bfloat16)


def product(left, right, dims=NN):
    (lh, ll), (rh, rl) = left, right
    dot = functools.partial(lax.dot_general, dimension_numbers=dims, preferred_element_type=jnp.float32)
    return dot(lh, rh) + (dot(ll, rh) + dot(lh, rl))


def stacked(left, right, dims=NN):
    (lh, ll), (rh, rl) = left, right
    dot = functools.partial(lax.dot_general, dimension_numbers=dims, preferred_element_type=jnp.float32)
    both = dot(jnp.concatenate([lh, ll], axis=0), rh)
    size = lh.shape[0]
    return both[:size] + (both[size:] + dot(lh, rl))


def general_kernel(
    ctx_n, chips, square, steps, pieces,
    hidden, w_query, w_down, gain, w_key, w_value, w_out, out,
    hid, wd, wq, gn, wk, wv, wo, lat, qh, ql, top, total, acc, part, landed,
    load_sem, swap_send, swap_recv, hid_send, hid_recv, col_send, col_recv,
    row_send, row_recv, twin_send, twin_recv, sum_send, sum_recv,
):
    rows, width = hidden.shape
    parts = 2 if square else 1
    rank = gn.shape[1]
    tail = wd.shape[0] - rank
    nope = wk.shape[2]
    per_core = chips * rows
    block = CORES * per_core
    lanes = lat.shape[1]
    ctx = lax.axis_index("ctx")
    head = lax.axis_index("head")
    chip, core = head // CORES, head % CORES
    twin = chip * CORES + (1 - core)

    def chip_at(offset):
        return lax.rem(chip + offset, chips)

    def to(o):
        if not square:
            return chip_at(o)
        return [chip, chip + 1 - 2 * lax.rem(chip, 2), lax.rem(chip + 2, 4), 3 - chip][o]

    def origin(o):
        return to(o) if square else chip_at(chips - o)

    def local(src, dst, sem):
        return pltpu.make_async_copy(src, dst, load_sem.at[sem])

    def remote(src, dst, send, recv, c, h):
        return pltpu.make_async_remote_copy(
            src_ref=src, dst_ref=dst, send_sem=send, recv_sem=recv,
            device_id={"ctx": c, "head": h}, device_id_type=MESH,
        )

    def at_rows(start, size):
        return pl.ds(pl.multiple_of(start, 8), size)

    my_hid = hid.at[at_rows(chip * rows, rows)]
    depth = width // steps
    loads = [local(hidden, my_hid, 0), local(gain, gn, 1)]
    for s in range(steps):
        span = pl.ds(s * depth, depth)
        loads.append(local(w_down.at[:, span], wd.at[:, span], 2 + s))
    pairs = [(w_query, wq), (w_key, wk), (w_value, wv), (w_out, wo)]
    own = [local(src, dst.at[core], 2 + steps + i) for i, (src, dst) in enumerate(pairs)]
    for copy in loads:
        copy.start()

    barrier = pltpu.get_barrier_semaphore()
    for o in range(1, chips):
        pl.semaphore_signal(barrier, inc=1, device_id={"ctx": ctx, "head": chip_at(o) * CORES + core}, device_id_type=MESH)
    pl.semaphore_signal(barrier, inc=1, device_id={"ctx": ctx, "head": twin}, device_id_type=MESH)
    for o in range(1, ctx_n):
        pl.semaphore_signal(barrier, inc=1, device_id={"ctx": lax.rem(ctx + o, ctx_n), "head": head}, device_id_type=MESH)
    pl.semaphore_wait(barrier, chips - 1 + 1 + ctx_n - 1)

    def share(source, spot, send, recv):
        def start_of(o, h):
            target = to(o)
            return remote(source(h), spot(chip, h), send(o, h), recv(o, h), ctx, target * CORES + core)

        def seen(o, h):
            place_of = spot(origin(o), h)
            return remote(place_of, place_of, send(o, h), recv(o, h), ctx, twin)

        def passed(h):
            place_of = spot(to(1 + h), h)
            return remote(place_of, place_of, send(3, h), recv(3, h), ctx, to(2 - h) * CORES + core)

        direct = [(1, 0), (2, 1), (1, 1), (2, 0)] if square else [(o, 0) for o in range(1, chips)]

        def start():
            for o, h in direct:
                start_of(o, h).start()

        def relay():
            if square:
                for h in range(2):
                    seen(1 + h, h).wait_recv()
                    passed(h).start()

        def finish():
            for o, h in [(1, 1), (2, 0), (3, 0), (3, 1)] if square else direct:
                seen(o, h).wait_recv()

        def drain():
            for o, h in direct:
                start_of(o, h).wait_send()
            if square:
                for h in range(2):
                    passed(h).wait_send()

        return start, relay, finish, drain

    half = width // parts

    def hid_half(h):
        return pl.ds(h * half, half)

    hid_start, hid_relay, hid_finish, hid_drain = share(
        lambda h: hidden.at[:, hid_half(h)],
        lambda k, h: hid.at[at_rows(k * rows, rows), hid_half(h)],
        lambda o, h: hid_send.at[o, h],
        lambda o, h: hid_recv.at[o, h],
    )
    hid_start()
    swaps = [remote(src, dst.at[core], swap_send.at[i], swap_recv.at[i], ctx, twin) for i, (src, dst) in enumerate(pairs)]
    for copy in own:
        copy.start()
    for copy in swaps:
        copy.start()

    loads[0].wait()
    loads[1].wait()
    down = jnp.zeros((rows, rank + tail), jnp.float32)
    for s in range(steps):
        loads[2 + s].wait()
        span = pl.ds(s * depth, depth)
        down += product(halves(my_hid[:, span]), halves(wd[:, span]), NT)
    raw = down[:, :rank]
    meansq = jnp.mean(raw * raw, axis=-1, keepdims=True)
    blank = jnp.zeros((rows, lanes - rank - tail), jnp.float32)

    def place(b, p, k):
        return ((b * CORES + p) * chips + k) * rows

    mine = at_rows(place(ctx, core, chip), rows)
    lat[mine, :rank] = raw * lax.rsqrt(meansq + EPSILON) * gn[...]
    lat[mine, rank:] = jnp.concatenate([down[:, rank:], blank], axis=1)

    def col_copy(b):
        spot = lat.at[at_rows(place(b, core, chip), rows)]
        return remote(spot, spot, col_send.at[b], col_recv.at[b], jnp.minimum(ctx + 1, ctx_n - 1), head)

    def latents(b):
        def spot(k, h):
            return lat.at[at_rows(place(b, core, k) + h * (rows // parts), rows // parts)]

        return share(
            lambda h: spot(chip, h), spot, lambda o, h: row_send.at[b, o, h], lambda o, h: row_recv.at[b, o, h]
        )

    def twin_copy(b, p):
        spot = lat.at[at_rows(place(b, p, 0), per_core)]
        return remote(spot, spot, twin_send.at[b], twin_recv.at[b], ctx, twin)

    def spread(b):
        @pl.when(ctx + 1 < ctx_n)
        def _():
            col_copy(b).start()

        latents(b)[0]()

    def gather_rows(b):
        latents(b)[2]()
        twin_copy(b, core).start()

    spread(ctx)
    hid_relay()
    for d in range(1, ctx_n):
        @pl.when(d <= ctx)
        def _():
            col_copy(ctx - d).wait_recv()
            spread(ctx - d)

    latents(ctx)[1]()

    hid_finish()
    for i in range(2):
        own[i].wait()
        swaps[i].wait()
    scale = wq.shape[1] ** (-0.5)
    pad = jnp.zeros((per_core, lanes - rank - tail), jnp.float32)
    query = [jnp.zeros((per_core, wq.shape[1]), jnp.float32) for _ in range(CORES)]
    for s in range(steps):
        span = pl.ds(s * depth, depth)
        piece = halves(hid[:, span])
        for p in range(CORES):
            query[p] += product(piece, halves(wq[p, :, span]), NT)
    for p in range(CORES):
        wide = product(halves(query[p][:, :nope] * scale), halves(wk[p]), NT)
        span = pl.ds(p * per_core, per_core)
        qh[span, :rank], ql[span, :rank] = halves(wide)
        qh[span, rank:], ql[span, rank:] = halves(jnp.concatenate([query[p][:, nope:] * scale, pad], axis=1))

    def spots(index, parity):
        inner = lax.rem(index, per_core)
        return (lax.div(inner, rows) * CORES + parity) * rows + lax.rem(inner, rows)

    def attend(b, first):
        keys = halves(lat[at_rows(place(b, 0, 0), block), :])
        scores = product((qh[...], ql[...]), keys, NT)
        if first:
            line = lax.broadcasted_iota(jnp.int32, (block, 1), 0)
            column = lax.broadcasted_iota(jnp.int32, (1, block), 1)
            causal = spots(line, core) >= spots(column, lax.div(column, per_core))
            scores = jnp.where(causal, scores, FLOOR)
            peak = jnp.max(scores, axis=1, keepdims=True)
        else:
            peak = jnp.maximum(top[...], jnp.max(scores, axis=1, keepdims=True))
        weights = jnp.exp(scores - peak)
        if first:
            weights = jnp.where(causal, weights, 0.0)
        mixed = product(halves(weights), (keys[0][:, :rank], keys[1][:, :rank]))
        added = jnp.sum(weights, axis=1, keepdims=True)
        if first:
            total[...] = added
            acc[...] = mixed
        else:
            fade = jnp.exp(top[...] - peak)
            total[...] = total[...] * fade + added
            acc[...] = acc[...] * fade + mixed
        top[...] = peak

    def relay_at(d):
        if d < ctx_n:
            @pl.when(d <= ctx)
            def _():
                latents(ctx - d)[1]()

    relay_at(1)
    gather_rows(ctx)
    twin_copy(ctx, 1 - core).wait_recv()
    attend(ctx, True)
    for d in range(1, ctx_n):
        @pl.when(d <= ctx)
        def _():
            relay_at(d + 1)
            gather_rows(ctx - d)
            twin_copy(ctx - d, 1 - core).wait_recv()
            attend(ctx - d, False)

    for i in range(2, 4):
        own[i].wait()
        swaps[i].wait()
    heads = []
    for p in range(CORES):
        span = pl.ds(p * per_core, per_core)
        heads.append(product(halves(acc[span, :] / total[span, :]), halves(wv[p])))
    attended = halves(jnp.concatenate(heads, axis=1))
    columns = width // pieces

    def cut(ref, k, t):
        return ref.at[at_rows(k * rows, rows), pl.ds(t * columns, columns)]

    def axes_of(t):
        return (1, 2) if t % 2 == 0 else (2, 1)

    def sum_copy(t, j):
        if not square:
            return remote(
                cut(part, chip_at(j), t), cut(landed, chip, t), sum_send.at[t, j], sum_recv.at[t, j],
                ctx, chip_at(j) * CORES + core,
            )
        first, second = axes_of(t)
        src = [to(3), to(first), to(second)][j]
        dst = [to(3), to(first), to(3)][j]
        target = [to(first), to(first), to(second)][j]
        return remote(cut(part, src, t), cut(landed, dst, t), sum_send.at[t, j], sum_recv.at[t, j], ctx, target * CORES + core)

    def second_stage(t):
        sum_copy(t, 0).wait_recv()
        keep = to(axes_of(t)[1])
        cut(part, keep, t)[...] = cut(part, keep, t)[...] + cut(landed, keep, t)[...]
        sum_copy(t, 2).start()

    kinds = (0, 1) if square else tuple(range(1, chips))
    for t in range(pieces):
        span = pl.ds(t * columns, columns)
        weight = jnp.concatenate([wo[p, :, span] for p in range(CORES)], axis=0)
        part[:, span] = product(attended, halves(weight))
        for j in kinds:
            sum_copy(t, j).start()
        if square and t >= 2:
            second_stage(t - 2)
    if square:
        for t in range(max(pieces - 2, 0), pieces):
            second_stage(t)
    for t in range(pieces):
        result = cut(part, chip, t)[...]
        if square:
            for j in (1, 2):
                sum_copy(t, j).wait_recv()
            result += cut(landed, chip, t)[...] + cut(landed, to(axes_of(t)[0]), t)[...]
        else:
            for j in kinds:
                sum_copy(t, j).wait_recv()
                result += cut(landed, origin(j), t)[...]
        out[:, pl.ds(t * columns, columns)] = result

    hid_drain()
    for t in range(pieces):
        for j in kinds + ((2,) if square else ()):
            sum_copy(t, j).wait_send()
    for d in range(ctx_n):
        @pl.when(d <= ctx)
        def _():
            @pl.when(ctx + 1 < ctx_n)
            def _():
                col_copy(ctx - d).wait_send()

            latents(ctx - d)[3]()
            twin_copy(ctx - d, core).wait_send()


def square_kernel(
    ctx_n, chunks, cuts,
    hidden, w_query, w_down, gain, w_key, w_value, w_out, out,
    mine, hid, wd, gn, wq, wqh, wql, wk, wv, wo, woh, wol, lat, kh, kl, qh, ql, top, total, acc,
    part, mid, fwd, near, last,
    load_sem, swap_send, swap_recv, hid_send, hid_recv, far_sem, z_send, z_recv,
    lat_send, lat_recv, twin_recv, sum_send, sum_recv,
):
    rows, width = hidden.shape
    rank = gn.shape[1]
    tail = wd.shape[0] - rank
    nope, vdim = wk.shape[2], wv.shape[2]
    key_width = wq.shape[1]
    lanes = kh.shape[1]
    r = rows // chunks
    group = 4 * r
    many = CORES * group
    block = CORES * 4 * rows
    hr = rows // 2
    tiles = rank // LANE
    piece = hr * tiles + hr // 2
    slot = 2 * piece
    half = width // 2
    steps = 3 if width % 384 == 0 else 1
    depth = width // steps
    ctx = lax.axis_index("ctx")
    head = lax.axis_index("head")
    chip, core = head // CORES, head % CORES
    twin = chip * CORES + (1 - core)
    xbit, ybit = lax.rem(chip, 2), lax.div(chip, 2)
    side = [None, (2 * ybit + 1 - xbit) * CORES + core, (2 * (1 - ybit) + xbit) * CORES + core]

    def local(src, dst, sem):
        return pltpu.make_async_copy(src, dst, sem)

    def remote(src, dst, send, recv, h, c=ctx):
        return pltpu.make_async_remote_copy(
            src_ref=src, dst_ref=dst, send_sem=send, recv_sem=recv,
            device_id={"ctx": c, "head": h}, device_id_type=MESH,
        )

    def signal(sem, c, h):
        pl.semaphore_signal(sem, inc=1, device_id={"ctx": c, "head": h}, device_id_type=MESH)

    def when(condition, *actions):
        @pl.when(condition)
        def _():
            for action in actions:
                action()

    def spot(q, s, h):
        return hid.at[pl.ds((q * 4 + s) * r, r), pl.ds(h * half, half)]

    def hid_direct(q, order):
        for a, h in order:
            remote(
                hidden.at[pl.ds(q * r, r), pl.ds(h * half, half)], spot(q, a, h),
                hid_send.at[0], hid_recv.at[q, h if (a, h) in FIRST else 2], side[a],
            ).start()

    def hid_relay(q):
        for h in range(2):
            landed = spot(q, 1 + h, h)
            remote(landed, landed, hid_send.at[0], hid_recv.at[q, h], twin).wait_recv()
            remote(landed, spot(q, 3, h), hid_send.at[0], hid_recv.at[q, 2], side[2 - h]).start()

    def hid_finish(q):
        landed = hid.at[pl.ds((q * 4 + 1) * r, 2 * r)]
        remote(landed, landed, hid_send.at[0], hid_recv.at[q, 2], twin).wait_recv()

    def lat_at(d, p, s, h=0, size=piece):
        return lat.at[pl.ds(((d * CORES + p) * 4 + s) * slot + h * piece, size)]

    def lat_twin(d, s, count):
        size = count * slot
        remote(lat_at(d, 0, s, 0, size), lat_at(d, 1, s, 0, size), lat_send.at[d], twin_recv.at[d], twin).start()

    def z_copy(d, s, h, size):
        c = jnp.minimum(ctx + d, ctx_n - 1)
        return remote(lat_at(0, 0, s, h, size), lat_at(d, 0, s, h, size), z_send.at[d - 1], z_recv.at[d - 1], head, c)

    def z_wait(d):
        landed = lat_at(d, 0, 0, 0, 4 * slot if d == 1 else slot)
        remote(landed, landed, z_send.at[d - 1], z_recv.at[d - 1], head).wait_recv()

    def lat_spread(d):
        for a, h in DIRECT:
            remote(
                lat_at(d, 0, 0, h), lat_at(d, 0, a, h), lat_send.at[d],
                lat_recv.at[d, h if (a, h) in FIRST else 2], side[a],
            ).start()
        lat_twin(d, 0, 1)

    def lat_fetch(d):
        z_wait(d)
        lat_spread(d)

    def lat_relay(d):
        for h in range(2):
            landed = lat_at(d, 0, 1 + h, h)
            remote(landed, landed, lat_send.at[d], lat_recv.at[d, h], twin).wait_recv()
            remote(landed, lat_at(d, 0, 3, h), lat_send.at[d], lat_recv.at[d, 2], side[2 - h]).start()

    def lat_finish(d):
        landed = lat_at(d, 0, 1, 0, 2 * slot)
        remote(landed, landed, lat_send.at[d], lat_recv.at[d, 2], twin).wait_recv()
        lat_twin(d, 1, 3)

    def z_begin():
        z_copy(1, 0, 0, slot).start()
        z_copy(1, 1, 0, piece).start()
        z_copy(1, 2, 1, piece).start()

    def z_end():
        z_copy(1, 1, 1, 2 * piece).start()
        z_copy(1, 3, 0, slot).start()

    loads = [local(hidden, mine, load_sem.at[0]), local(gain, gn, load_sem.at[1])]
    for i in range(steps):
        span = pl.ds(i * depth, depth)
        loads.append(local(w_down.at[:, span], wd.at[:, span], load_sem.at[2 + i]))
    pairs = [(w_query, wq), (w_key, wk), (w_value, wv), (w_out, wo)]
    lots = (0, 1, 1, 2)
    own = [local(src, dst.at[0], load_sem.at[2 + steps + lot]) for (src, dst), lot in zip(pairs, lots)]
    for q in range(chunks):
        own.append(local(hidden.at[pl.ds(q * r, r)], hid.at[pl.ds(q * group, r)], load_sem.at[5 + steps]))
    for copy in loads:
        copy.start()

    barrier = pltpu.get_barrier_semaphore()
    for h in (twin, side[1], side[2]):
        signal(barrier, ctx, h)
    when(ctx > 0, lambda: signal(barrier, ctx - 1, head))
    when(ctx + 1 < ctx_n, lambda: signal(barrier, ctx + 1, head))
    pl.semaphore_wait(barrier, 3 + jnp.minimum(ctx, 1) + jnp.minimum(ctx_n - 1 - ctx, 1))

    hid_direct(0, FIRST + REST[:2])
    swaps = [
        remote(src, dst.at[1], swap_send.at[lot], swap_recv.at[lot], twin) for (src, dst), lot in zip(pairs, lots)
    ]
    for copy in own:
        copy.start()
    for copy in swaps:
        copy.start()

    if ctx_n > 2:
        when(jnp.logical_and(ctx >= 1, ctx + 2 <= ctx_n), lambda: signal(far_sem.at[0], ctx - 1, head))

    loads[0].wait()
    loads[1].wait()
    down = jnp.zeros((rows, rank + tail), jnp.float32)
    for i in range(steps):
        loads[2 + i].wait()
        span = pl.ds(i * depth, depth)
        down += stacked(halves(mine[:, span]), halves(wd[:, span]), NT)
    raw = down[:, :rank]
    meansq = jnp.mean(raw * raw, axis=-1, keepdims=True)
    latent = raw * lax.rsqrt(meansq + EPSILON) * gn[...]
    shared = jnp.concatenate([down[:hr, rank:], down[hr:, rank:]], axis=1)
    for h in range(2):
        for j in range(tiles):
            lat_at(0, 0, 0, h)[pl.ds(j * hr, hr), :] = latent[h * hr : (h + 1) * hr, j * LANE : (j + 1) * LANE]
        lat_at(0, 0, 0, h)[pl.ds(tiles * hr, hr // 2), :] = shared[h * hr // 2 : (h + 1) * hr // 2]

    for d in range(2, ctx_n):
        when(ctx + d < ctx_n, lambda d=d: pl.semaphore_wait(far_sem.at[d - 2], 1))
        if d + 1 < ctx_n:
            when(
                jnp.logical_and(ctx >= 1, ctx + d < ctx_n),
                lambda d=d: signal(far_sem.at[d - 1], ctx - 1, head),
            )
    for d in range(ctx_n - 1, 1, -1):
        when(ctx + d < ctx_n, lambda d=d: z_copy(d, 0, 0, slot).start())
    lat_spread(0)

    def split_query(p):
        wqh[p], wql[p] = halves(wq[p])

    def kept(lot):
        whole = {0: wq.at[0], 1: wk, 2: wo.at[0]}[lot]
        local(whole, whole, load_sem.at[2 + steps + lot]).wait()
        remote(whole, whole, swap_send.at[lot], swap_recv.at[lot], twin).wait()

    hid_relay(0)
    own[0].wait()
    split_query(0)
    lat_relay(0)
    if ctx_n > 1:
        when(ctx + 1 < ctx_n, z_begin)
    swaps[0].wait()
    split_query(1)
    for d in range(2, ctx_n):
        when(ctx >= d, lambda d=d: lat_fetch(d))
    kept(1)
    local(mine, mine, load_sem.at[5 + steps]).wait()

    scale = key_width ** (-0.5)
    pad = jnp.zeros((group, lanes - rank - tail), jnp.float32)

    def queries(q):
        hid_finish(q)
        query = [jnp.zeros((group, key_width), jnp.float32) for _ in range(CORES)]
        for i in range(steps):
            span = pl.ds(i * depth, depth)
            given = halves(hid[pl.ds(q * group, group), span])
            for p in range(CORES):
                query[p] += stacked(given, (wqh[p, :, span], wql[p, :, span]), NT)
        for p in range(CORES):
            wide = stacked(halves(query[p][:, :nope] * scale), halves(wk[p]), NT)
            span = pl.ds(q * many + p * group, group)
            qh[span, :rank], ql[span, :rank] = halves(wide)
            rest = jnp.concatenate([query[p][:, nope:] * scale, pad], axis=1)
            qh[span, rank:], ql[span, rank:] = halves(rest)

    def keys(d):
        for p in range(CORES):
            for s in range(4):
                at = d * block + (p * 4 + s) * rows
                packed = jnp.concatenate(
                    [lat_at(d, p, s, h)[pl.ds(tiles * hr, hr // 2), :] for h in range(2)], axis=0
                )
                for h in range(2):
                    span = pl.ds(at + h * hr, hr)
                    for j in range(tiles):
                        lane = pl.ds(j * LANE, LANE)
                        kh[span, lane], kl[span, lane] = halves(lat_at(d, p, s, h)[pl.ds(j * hr, hr), :])
                    lane = pl.ds(rank, LANE)
                    kh[span, lane], kl[span, lane] = halves(packed if h == 0 else pltpu.roll(packed, tail, 1))

    def lat_ready(d):
        landed = lat_at(d, 1, 0, 0, 4 * slot)
        remote(landed, landed, lat_send.at[d], twin_recv.at[d], twin).wait_recv()
        keys(d)

    def place(s, parity, i):
        sx, sy = lax.rem(s, 2), lax.div(s, 2)
        x, y = lax.rem(xbit + sx, 2), lax.rem(ybit + sy, 2)
        return ((2 * y + x) * CORES + parity) * rows + i

    def causal_of(q, count):
        line = lax.rem(lax.broadcasted_iota(jnp.int32, (many, 1), 0), group)
        column = lax.broadcasted_iota(jnp.int32, (1, count * block), 1)
        there = lax.rem(lax.div(column, 4 * rows), CORES)
        inner = lax.rem(column, 4 * rows)
        asked = place(lax.div(line, r), core, q * r + lax.rem(line, r))
        held = place(lax.div(inner, rows), core + there - 2 * core * there, lax.rem(inner, rows))
        return asked >= jnp.where(column < block, held, -1)

    def attend(q, d, count=1):
        mine_q = pl.ds(q * many, many)
        those = pl.ds(d * block, count * block)
        scores = stacked((qh[mine_q, :], ql[mine_q, :]), (kh[those, :], kl[those, :]), NT)
        if d == 0:
            causal = causal_of(q, count)
            scores = jnp.where(causal, scores, FLOOR)
            peak = jnp.max(scores, axis=1, keepdims=True)
        else:
            peak = jnp.maximum(top[mine_q, :], jnp.max(scores, axis=1, keepdims=True))
        weights = jnp.exp(scores - peak)
        if d == 0:
            weights = jnp.where(causal, weights, 0.0)
        mixed = stacked(halves(weights), (kh[those, :rank], kl[those, :rank]))
        added = jnp.sum(weights, axis=1, keepdims=True)
        if d == 0:
            total[mine_q, :] = added
            acc[mine_q, :] = mixed
        else:
            fade = jnp.exp(top[mine_q, :] - peak)
            total[mine_q, :] = total[mine_q, :] * fade + added
            acc[mine_q, :] = acc[mine_q, :] * fade + mixed
        top[mine_q, :] = peak

    def attend_whole(q):
        for count in range(1, ctx_n + 1):
            when(ctx + 1 == count, lambda count=count: attend(q, 0, count))

    def span_of(q, t):
        low, high = [width // 2 // LANE * i // cuts[q] * LANE for i in (t // 2, t // 2 + 1)]
        return pl.ds(2 * low + t % 2 * (high - low), high - low)

    def axes_of(t):
        return (1, 2) if t % 2 == 0 else (2, 1)

    def sum_copy(q, t, j):
        first, second = axes_of(t)
        span = span_of(q, t)
        here = pl.ds(q * r, r)

        def part_of(s):
            return part.at[pl.ds(q * group + s * r, r), span]

        src, dst, target = [
            (part_of(3), mid.at[here, span], first),
            (part_of(first), near.at[here, span], first),
            (fwd.at[here, span], last.at[here, span], second),
        ][j]
        return remote(src, dst, sum_send.at[0], sum_recv.at[2 * sum(cuts[:q]) + t, min(j, 1)], side[target])

    def project(q):
        found = []
        for p in range(CORES):
            span = pl.ds(q * many + p * group, group)
            found.append(stacked(halves(acc[span, :] / total[span, :]), halves(wv[p])))
        attended = halves(jnp.concatenate(found, axis=1))
        for t in range(2 * cuts[q]):
            span = span_of(q, t)
            part[pl.ds(q * group, group), span] = stacked(attended, (woh[:, span], wol[:, span]))
            sum_copy(q, t, 0).start()
        for t in range(2 * cuts[q]):
            sum_copy(q, t, 1).start()

    def second_stage(q):
        here = pl.ds(q * r, r)
        for t in range(2 * cuts[q]):
            span = span_of(q, t)
            sum_copy(q, t, 0).wait_recv()
            keep = axes_of(t)[1]
            fwd[here, span] = part[pl.ds(q * group + keep * r, r), span] + mid[here, span]
            sum_copy(q, t, 2).start()

    def collect(q):
        here = pl.ds(q * r, r)
        for t in range(2 * cuts[q]):
            span = span_of(q, t)
            landed = near.at[pl.ds(0, 2 * r), span]
            remote(landed, landed, sum_send.at[0], sum_recv.at[2 * sum(cuts[:q]) + t, 1], twin).wait_recv()
            out[here, span] = part[pl.ds(q * group, r), span] + near[here, span] + last[here, span]

    def split_out():
        kept(2)
        for p in range(CORES):
            span = pl.ds(p * vdim, vdim)
            woh[span, :], wol[span, :] = halves(wo[p])

    def join(d):
        lat_ready(d)
        attend(0, d)

    def z_join():
        z_wait(1)
        lat_twin(1, 0, 4)

    def begin(d):
        when(ctx >= d, lambda: lat_relay(d))

    queries(0)
    lat_finish(0)
    if ctx_n > 1:
        when(ctx + 1 < ctx_n, z_end)
    if ctx_n > 2:
        begin(2)
    for q in range(1, chunks):
        hid_direct(q, FIRST)
    join(0)
    for d in range(3, ctx_n):
        begin(d)
    for q in range(1, chunks):
        hid_direct(q, REST[:2])
    split_out()
    if ctx_n > 2:
        when(ctx >= 2, lambda: lat_finish(2))
        when(ctx >= 2, lambda: join(2))
    if ctx_n > 1:
        when(ctx >= 1, z_join)
    for q in range(1, chunks):
        hid_relay(q)
    for d in range(3, ctx_n):
        when(ctx >= d, lambda d=d: lat_finish(d))
    for d in [1] * (ctx_n > 1) + list(range(3, ctx_n)):
        when(ctx >= d, lambda d=d: join(d))
    project(0)
    for q in range(1, chunks):
        queries(q)
        attend_whole(q)
        second_stage(q - 1)
        project(q)
        collect(q - 1)
    second_stage(chunks - 1)
    collect(chunks - 1)

    sent = hid.at[pl.ds(0, 3 * rows)]
    for sem in (hid_send.at[0], sum_send.at[0]):
        remote(sent, sent, sem, hid_recv.at[0, 0], twin).wait_send()
    for d in range(ctx_n):
        def drain(d=d):
            sent = lat.at[pl.ds(0, (4 if d == 1 else 7) * slot)]
            remote(sent, sent, lat_send.at[d], twin_recv.at[d], twin).wait_send()

        def z_drain(d=d):
            sent = lat.at[pl.ds(0, (4 if d == 1 else 1) * slot)]
            remote(sent, sent, z_send.at[d - 1], z_recv.at[d - 1], head).wait_send()

        when(d <= ctx, drain)
        if d > 0:
            when(ctx + d < ctx_n, z_drain)


def square_call(ctx_n, hidden, w_query, w_down, gain, w_key_up, w_value_up, w_out):
    rows, width = hidden.shape
    rank, nope = w_key_up.shape
    vdim = w_value_up.shape[1]
    f32, bf16, dma = jnp.float32, jnp.bfloat16, pltpu.SemaphoreType.DMA
    chunks = 2
    cuts = (1, 2)
    r = rows // chunks
    block = CORES * 4 * rows
    lanes = rank + LANE
    steps = 3 if width % 384 == 0 else 1
    slot = rows * (rank // LANE) + rows // 2
    query = (CORES,) + w_query.shape
    both = (CORES * vdim, width)
    return pl.pallas_call(
        functools.partial(square_kernel, ctx_n, chunks, cuts),
        out_shape=pltpu.VMEM((rows, width), f32),
        in_specs=[pl.BlockSpec(memory_space=pltpu.HBM)] * 7,
        out_specs=pl.BlockSpec(memory_space=pltpu.VMEM),
        scratch_shapes=[
            pltpu.VMEM((rows, width), f32),
            pltpu.VMEM((4 * rows, width), f32),
            pltpu.VMEM(w_down.shape, f32),
            pltpu.VMEM((1, rank), f32),
            pltpu.VMEM(query, f32), pltpu.VMEM(query, bf16), pltpu.VMEM(query, bf16),
            pltpu.VMEM((CORES, rank, nope), f32),
            pltpu.VMEM((CORES, rank, vdim), f32),
            pltpu.VMEM((CORES, vdim, width), f32), pltpu.VMEM(both, bf16), pltpu.VMEM(both, bf16),
            pltpu.VMEM((ctx_n * CORES * 4 * slot, LANE), f32),
            pltpu.VMEM((ctx_n * block, lanes), bf16), pltpu.VMEM((ctx_n * block, lanes), bf16),
            pltpu.VMEM((block, lanes), bf16), pltpu.VMEM((block, lanes), bf16),
            pltpu.VMEM((block, 1), f32),
            pltpu.VMEM((block, 1), f32),
            pltpu.VMEM((block, rank), f32),
            pltpu.VMEM((4 * rows, width), f32),
        ] + [pltpu.VMEM((rows, width), f32)] * 4 + [
            dma((6 + steps,)),
            dma((3,)), dma((3,)),
            dma((1,)), dma((chunks, 3)),
            pltpu.SemaphoreType.REGULAR((max(ctx_n - 2, 1),)),
            dma((max(ctx_n - 1, 1),)), dma((max(ctx_n - 1, 1),)),
            dma((ctx_n,)), dma((ctx_n, 3)),
            dma((ctx_n,)),
            dma((1,)), dma((2 * sum(cuts), 2)),
        ],
        compiler_params=pltpu.CompilerParams(
            collective_id=0, has_side_effects=True, vmem_limit_bytes=60 * 1024 * 1024
        ),
    )(hidden, w_query, w_down, gain, w_key_up, w_value_up, w_out)


def on_device(ctx_n, chips, hidden, w_query, w_down, latent_gain, w_key_up, w_value_up, w_out):
    rows, width = hidden.shape
    rank, nope = w_key_up.shape
    vdim = w_value_up.shape[1]
    per_core = chips * rows
    block = CORES * per_core
    lanes = -(-w_down.shape[1] // 128) * 128
    steps = 3 if width % 384 == 0 else 1
    if chips == 4 and rows % 32 == 0 and width % 768 == 0 and rank % LANE == 0 and 2 * (w_down.shape[1] - rank) == LANE:
        return square_call(
            ctx_n, hidden, w_query.T, w_down.T, latent_gain.reshape(1, rank), w_key_up, w_value_up, w_out
        )
    square = chips == 4 and rows % 16 == 0 and width % 256 == 0
    pieces = 6 if width % 768 == 0 else 2
    f32, bf16, dma = jnp.float32, jnp.bfloat16, pltpu.SemaphoreType.DMA
    return pl.pallas_call(
        functools.partial(general_kernel, ctx_n, chips, square, steps, pieces),
        out_shape=jax.ShapeDtypeStruct((rows, width), f32),
        in_specs=[pl.BlockSpec(memory_space=pltpu.HBM)] * 7,
        out_specs=pl.BlockSpec(memory_space=pltpu.VMEM),
        scratch_shapes=[
            pltpu.VMEM((per_core, width), f32),
            pltpu.VMEM(w_down.shape[::-1], f32),
            pltpu.VMEM((CORES,) + w_query.shape[::-1], f32),
            pltpu.VMEM((1, rank), f32),
            pltpu.VMEM((CORES, rank, nope), f32),
            pltpu.VMEM((CORES, rank, vdim), f32),
            pltpu.VMEM((CORES, vdim, width), f32),
            pltpu.VMEM((ctx_n * block, lanes), f32),
            pltpu.VMEM((block, lanes), bf16),
            pltpu.VMEM((block, lanes), bf16),
            pltpu.VMEM((block, 1), f32),
            pltpu.VMEM((block, 1), f32),
            pltpu.VMEM((block, rank), f32),
            pltpu.VMEM((per_core, width), f32),
            pltpu.VMEM((per_core, width), f32),
            dma((2 + steps + 4,)),
            dma((4,)), dma((4,)),
            dma((chips, 2)), dma((chips, 2)),
            dma((ctx_n,)), dma((ctx_n,)),
            dma((ctx_n, chips, 2)), dma((ctx_n, chips, 2)),
            dma((ctx_n,)), dma((ctx_n,)),
            dma((pieces, chips)), dma((pieces, chips)),
        ],
        compiler_params=pltpu.CompilerParams(
            collective_id=0, has_side_effects=True, vmem_limit_bytes=60 * 1024 * 1024
        ),
    )(hidden, w_query.T, w_down.T, latent_gain.reshape(1, rank), w_key_up, w_value_up, w_out)


def solution(mesh):
    placed = (
        P(("ctx", "head"), None),
        P(None, "head"),
        P(),
        P(),
        P(None, "head"),
        P(None, "head"),
        P("head", None),
    )
    body = functools.partial(on_device, mesh.shape["ctx"], mesh.shape["head"] // CORES)
    return jax.shard_map(
        body, mesh=mesh, in_specs=placed, out_specs=P(("ctx", "head"), None), check_vma=False
    )
```

```python
import functools

import jax
import jax.numpy as jnp
from jax import lax
from jax.experimental import pallas as pl
from jax.experimental.pallas import tpu as pltpu
from jax.sharding import PartitionSpec as P

EPSILON = 1e-06
FLOOR = -1e30
CORES = 2
LANE = 128
FIRST = ((1, 0), (2, 1))
DIRECT = ((1, 0), (2, 1), (1, 1), (2, 0))
REST = ((1, 1), (2, 0), (3, 0), (3, 1))
MESH = pl.DeviceIdType.MESH
NN = (((1,), (0,)), ((), ()))
NT = (((1,), (1,)), ((), ()))


def halves(value):
    high = value.astype(jnp.bfloat16)
    return high, (value - high.astype(jnp.float32)).astype(jnp.bfloat16)


def product(left, right, dims=NN):
    (lh, ll), (rh, rl) = left, right
    dot = functools.partial(lax.dot_general, dimension_numbers=dims, preferred_element_type=jnp.float32)
    return dot(lh, rh) + (dot(ll, rh) + dot(lh, rl))


def stacked(left, right, dims=NN):
    (lh, ll), (rh, rl) = left, right
    dot = functools.partial(lax.dot_general, dimension_numbers=dims, preferred_element_type=jnp.float32)
    both = dot(jnp.concatenate([lh, ll], axis=0), rh)
    size = lh.shape[0]
    return both[:size] + (both[size:] + dot(lh, rl))


def general_kernel(
    ctx_n, chips, square, steps, pieces,
    hidden, w_query, w_down, gain, w_key, w_value, w_out, out,
    hid, wd, wq, gn, wk, wv, wo, lat, qh, ql, top, total, acc, part, landed,
    load_sem, swap_send, swap_recv, hid_send, hid_recv, col_send, col_recv,
    row_send, row_recv, twin_send, twin_recv, sum_send, sum_recv,
):
    rows, width = hidden.shape
    parts = 2 if square else 1
    rank = gn.shape[1]
    tail = wd.shape[0] - rank
    nope = wk.shape[2]
    per_core = chips * rows
    block = CORES * per_core
    lanes = lat.shape[1]
    ctx = lax.axis_index("ctx")
    head = lax.axis_index("head")
    chip, core = head // CORES, head % CORES
    twin = chip * CORES + (1 - core)

    def chip_at(offset):
        return lax.rem(chip + offset, chips)

    def to(o):
        if not square:
            return chip_at(o)
        return [chip, chip + 1 - 2 * lax.rem(chip, 2), lax.rem(chip + 2, 4), 3 - chip][o]

    def origin(o):
        return to(o) if square else chip_at(chips - o)

    def local(src, dst, sem):
        return pltpu.make_async_copy(src, dst, load_sem.at[sem])

    def remote(src, dst, send, recv, c, h):
        return pltpu.make_async_remote_copy(
            src_ref=src, dst_ref=dst, send_sem=send, recv_sem=recv,
            device_id={"ctx": c, "head": h}, device_id_type=MESH,
        )

    def at_rows(start, size):
        return pl.ds(pl.multiple_of(start, 8), size)

    my_hid = hid.at[at_rows(chip * rows, rows)]
    depth = width // steps
    loads = [local(hidden, my_hid, 0), local(gain, gn, 1)]
    for s in range(steps):
        span = pl.ds(s * depth, depth)
        loads.append(local(w_down.at[:, span], wd.at[:, span], 2 + s))
    pairs = [(w_query, wq), (w_key, wk), (w_value, wv), (w_out, wo)]
    own = [local(src, dst.at[core], 2 + steps + i) for i, (src, dst) in enumerate(pairs)]
    for copy in loads:
        copy.start()

    barrier = pltpu.get_barrier_semaphore()
    for o in range(1, chips):
        pl.semaphore_signal(barrier, inc=1, device_id={"ctx": ctx, "head": chip_at(o) * CORES + core}, device_id_type=MESH)
    pl.semaphore_signal(barrier, inc=1, device_id={"ctx": ctx, "head": twin}, device_id_type=MESH)
    for o in range(1, ctx_n):
        pl.semaphore_signal(barrier, inc=1, device_id={"ctx": lax.rem(ctx + o, ctx_n), "head": head}, device_id_type=MESH)
    pl.semaphore_wait(barrier, chips - 1 + 1 + ctx_n - 1)

    def share(source, spot, send, recv):
        def start_of(o, h):
            target = to(o)
            return remote(source(h), spot(chip, h), send(o, h), recv(o, h), ctx, target * CORES + core)

        def seen(o, h):
            place_of = spot(origin(o), h)
            return remote(place_of, place_of, send(o, h), recv(o, h), ctx, twin)

        def passed(h):
            place_of = spot(to(1 + h), h)
            return remote(place_of, place_of, send(3, h), recv(3, h), ctx, to(2 - h) * CORES + core)

        direct = [(1, 0), (2, 1), (1, 1), (2, 0)] if square else [(o, 0) for o in range(1, chips)]

        def start():
            for o, h in direct:
                start_of(o, h).start()

        def relay():
            if square:
                for h in range(2):
                    seen(1 + h, h).wait_recv()
                    passed(h).start()

        def finish():
            for o, h in [(1, 1), (2, 0), (3, 0), (3, 1)] if square else direct:
                seen(o, h).wait_recv()

        def drain():
            for o, h in direct:
                start_of(o, h).wait_send()
            if square:
                for h in range(2):
                    passed(h).wait_send()

        return start, relay, finish, drain

    half = width // parts

    def hid_half(h):
        return pl.ds(h * half, half)

    hid_start, hid_relay, hid_finish, hid_drain = share(
        lambda h: hidden.at[:, hid_half(h)],
        lambda k, h: hid.at[at_rows(k * rows, rows), hid_half(h)],
        lambda o, h: hid_send.at[o, h],
        lambda o, h: hid_recv.at[o, h],
    )
    hid_start()
    swaps = [remote(src, dst.at[core], swap_send.at[i], swap_recv.at[i], ctx, twin) for i, (src, dst) in enumerate(pairs)]
    for copy in own:
        copy.start()
    for copy in swaps:
        copy.start()

    loads[0].wait()
    loads[1].wait()
    down = jnp.zeros((rows, rank + tail), jnp.float32)
    for s in range(steps):
        loads[2 + s].wait()
        span = pl.ds(s * depth, depth)
        down += product(halves(my_hid[:, span]), halves(wd[:, span]), NT)
    raw = down[:, :rank]
    meansq = jnp.mean(raw * raw, axis=-1, keepdims=True)
    blank = jnp.zeros((rows, lanes - rank - tail), jnp.float32)

    def place(b, p, k):
        return ((b * CORES + p) * chips + k) * rows

    mine = at_rows(place(ctx, core, chip), rows)
    lat[mine, :rank] = raw * lax.rsqrt(meansq + EPSILON) * gn[...]
    lat[mine, rank:] = jnp.concatenate([down[:, rank:], blank], axis=1)

    def col_copy(b):
        spot = lat.at[at_rows(place(b, core, chip), rows)]
        return remote(spot, spot, col_send.at[b], col_recv.at[b], jnp.minimum(ctx + 1, ctx_n - 1), head)

    def latents(b):
        def spot(k, h):
            return lat.at[at_rows(place(b, core, k) + h * (rows // parts), rows // parts)]

        return share(
            lambda h: spot(chip, h), spot, lambda o, h: row_send.at[b, o, h], lambda o, h: row_recv.at[b, o, h]
        )

    def twin_copy(b, p):
        spot = lat.at[at_rows(place(b, p, 0), per_core)]
        return remote(spot, spot, twin_send.at[b], twin_recv.at[b], ctx, twin)

    def spread(b):
        @pl.when(ctx + 1 < ctx_n)
        def _():
            col_copy(b).start()

        latents(b)[0]()

    def gather_rows(b):
        latents(b)[2]()
        twin_copy(b, core).start()

    spread(ctx)
    hid_relay()
    for d in range(1, ctx_n):
        @pl.when(d <= ctx)
        def _():
            col_copy(ctx - d).wait_recv()
            spread(ctx - d)

    latents(ctx)[1]()

    hid_finish()
    for i in range(2):
        own[i].wait()
        swaps[i].wait()
    scale = wq.shape[1] ** (-0.5)
    pad = jnp.zeros((per_core, lanes - rank - tail), jnp.float32)
    query = [jnp.zeros((per_core, wq.shape[1]), jnp.float32) for _ in range(CORES)]
    for s in range(steps):
        span = pl.ds(s * depth, depth)
        piece = halves(hid[:, span])
        for p in range(CORES):
            query[p] += product(piece, halves(wq[p, :, span]), NT)
    for p in range(CORES):
        wide = product(halves(query[p][:, :nope] * scale), halves(wk[p]), NT)
        span = pl.ds(p * per_core, per_core)
        qh[span, :rank], ql[span, :rank] = halves(wide)
        qh[span, rank:], ql[span, rank:] = halves(jnp.concatenate([query[p][:, nope:] * scale, pad], axis=1))

    def spots(index, parity):
        inner = lax.rem(index, per_core)
        return (lax.div(inner, rows) * CORES + parity) * rows + lax.rem(inner, rows)

    def attend(b, first):
        keys = halves(lat[at_rows(place(b, 0, 0), block), :])
        scores = product((qh[...], ql[...]), keys, NT)
        if first:
            line = lax.broadcasted_iota(jnp.int32, (block, 1), 0)
            column = lax.broadcasted_iota(jnp.int32, (1, block), 1)
            causal = spots(line, core) >= spots(column, lax.div(column, per_core))
            scores = jnp.where(causal, scores, FLOOR)
            peak = jnp.max(scores, axis=1, keepdims=True)
        else:
            peak = jnp.maximum(top[...], jnp.max(scores, axis=1, keepdims=True))
        weights = jnp.exp(scores - peak)
        if first:
            weights = jnp.where(causal, weights, 0.0)
        mixed = product(halves(weights), (keys[0][:, :rank], keys[1][:, :rank]))
        added = jnp.sum(weights, axis=1, keepdims=True)
        if first:
            total[...] = added
            acc[...] = mixed
        else:
            fade = jnp.exp(top[...] - peak)
            total[...] = total[...] * fade + added
            acc[...] = acc[...] * fade + mixed
        top[...] = peak

    def relay_at(d):
        if d < ctx_n:
            @pl.when(d <= ctx)
            def _():
                latents(ctx - d)[1]()

    relay_at(1)
    gather_rows(ctx)
    twin_copy(ctx, 1 - core).wait_recv()
    attend(ctx, True)
    for d in range(1, ctx_n):
        @pl.when(d <= ctx)
        def _():
            relay_at(d + 1)
            gather_rows(ctx - d)
            twin_copy(ctx - d, 1 - core).wait_recv()
            attend(ctx - d, False)

    for i in range(2, 4):
        own[i].wait()
        swaps[i].wait()
    heads = []
    for p in range(CORES):
        span = pl.ds(p * per_core, per_core)
        heads.append(product(halves(acc[span, :] / total[span, :]), halves(wv[p])))
    attended = halves(jnp.concatenate(heads, axis=1))
    columns = width // pieces

    def cut(ref, k, t):
        return ref.at[at_rows(k * rows, rows), pl.ds(t * columns, columns)]

    def axes_of(t):
        return (1, 2) if t % 2 == 0 else (2, 1)

    def sum_copy(t, j):
        if not square:
            return remote(
                cut(part, chip_at(j), t), cut(landed, chip, t), sum_send.at[t, j], sum_recv.at[t, j],
                ctx, chip_at(j) * CORES + core,
            )
        first, second = axes_of(t)
        src = [to(3), to(first), to(second)][j]
        dst = [to(3), to(first), to(3)][j]
        target = [to(first), to(first), to(second)][j]
        return remote(cut(part, src, t), cut(landed, dst, t), sum_send.at[t, j], sum_recv.at[t, j], ctx, target * CORES + core)

    def second_stage(t):
        sum_copy(t, 0).wait_recv()
        keep = to(axes_of(t)[1])
        cut(part, keep, t)[...] = cut(part, keep, t)[...] + cut(landed, keep, t)[...]
        sum_copy(t, 2).start()

    kinds = (0, 1) if square else tuple(range(1, chips))
    for t in range(pieces):
        span = pl.ds(t * columns, columns)
        weight = jnp.concatenate([wo[p, :, span] for p in range(CORES)], axis=0)
        part[:, span] = product(attended, halves(weight))
        for j in kinds:
            sum_copy(t, j).start()
        if square and t >= 2:
            second_stage(t - 2)
    if square:
        for t in range(max(pieces - 2, 0), pieces):
            second_stage(t)
    for t in range(pieces):
        result = cut(part, chip, t)[...]
        if square:
            for j in (1, 2):
                sum_copy(t, j).wait_recv()
            result += cut(landed, chip, t)[...] + cut(landed, to(axes_of(t)[0]), t)[...]
        else:
            for j in kinds:
                sum_copy(t, j).wait_recv()
                result += cut(landed, origin(j), t)[...]
        out[:, pl.ds(t * columns, columns)] = result

    hid_drain()
    for t in range(pieces):
        for j in kinds + ((2,) if square else ()):
            sum_copy(t, j).wait_send()
    for d in range(ctx_n):
        @pl.when(d <= ctx)
        def _():
            @pl.when(ctx + 1 < ctx_n)
            def _():
                col_copy(ctx - d).wait_send()

            latents(ctx - d)[3]()
            twin_copy(ctx - d, core).wait_send()


def square_kernel(
    ctx_n, chunks, cuts,
    hidden, w_query, w_down, gain, w_key, w_value, w_out, out,
    mine, hid, wd, gn, wq, wqh, wql, wk, wv, wo, woh, wol, lat, kh, kl, qh, ql, total, acc,
    part, mid, fwd, near, last,
    load_sem, swap_send, swap_recv, hid_send, hid_recv, far_sem, z_send, z_recv,
    lat_send, lat_recv, twin_recv, sum_send, sum_recv,
):
    rows, width = hidden.shape
    rank = gn.shape[1]
    tail = wd.shape[0] - rank
    nope, vdim = wk.shape[2], wv.shape[2]
    key_width = wq.shape[1]
    lanes = kh.shape[1]
    r = rows // chunks
    group = 4 * r
    many = CORES * group
    block = CORES * 4 * rows
    hr = rows // 2
    tiles = rank // LANE
    piece = hr * tiles + hr // 2
    slot = 2 * piece
    half = width // 2
    steps = 3 if width % 384 == 0 else 1
    depth = width // steps
    ctx = lax.axis_index("ctx")
    head = lax.axis_index("head")
    chip, core = head // CORES, head % CORES
    twin = chip * CORES + (1 - core)
    xbit, ybit = lax.rem(chip, 2), lax.div(chip, 2)
    side = [None, (2 * ybit + 1 - xbit) * CORES + core, (2 * (1 - ybit) + xbit) * CORES + core]

    def local(src, dst, sem):
        return pltpu.make_async_copy(src, dst, sem)

    def remote(src, dst, send, recv, h, c=ctx):
        return pltpu.make_async_remote_copy(
            src_ref=src, dst_ref=dst, send_sem=send, recv_sem=recv,
            device_id={"ctx": c, "head": h}, device_id_type=MESH,
        )

    def signal(sem, c, h):
        pl.semaphore_signal(sem, inc=1, device_id={"ctx": c, "head": h}, device_id_type=MESH)

    def when(condition, *actions):
        @pl.when(condition)
        def _():
            for action in actions:
                action()

    def spot(q, s, h):
        return hid.at[pl.ds((q * 4 + s) * r, r), pl.ds(h * half, half)]

    def hid_direct(q, order):
        for a, h in order:
            remote(
                hidden.at[pl.ds(q * r, r), pl.ds(h * half, half)], spot(q, a, h),
                hid_send.at[0], hid_recv.at[q, h if (a, h) in FIRST else 2], side[a],
            ).start()

    def hid_relay(q):
        for h in range(2):
            landed = spot(q, 1 + h, h)
            remote(landed, landed, hid_send.at[0], hid_recv.at[q, h], twin).wait_recv()
            remote(landed, spot(q, 3, h), hid_send.at[0], hid_recv.at[q, 2], side[2 - h]).start()

    def hid_finish(q):
        landed = hid.at[pl.ds((q * 4 + 1) * r, 2 * r)]
        remote(landed, landed, hid_send.at[0], hid_recv.at[q, 2], twin).wait_recv()

    def lat_at(d, p, s, h=0, size=piece):
        return lat.at[pl.ds(((d * CORES + p) * 4 + s) * slot + h * piece, size)]

    def lat_twin(d, s, count):
        size = count * slot
        remote(lat_at(d, 0, s, 0, size), lat_at(d, 1, s, 0, size), lat_send.at[d], twin_recv.at[d], twin).start()

    def z_copy(d, s, h, size):
        c = jnp.minimum(ctx + d, ctx_n - 1)
        return remote(lat_at(0, 0, s, h, size), lat_at(d, 0, s, h, size), z_send.at[d - 1], z_recv.at[d - 1], head, c)

    def z_wait(d):
        landed = lat_at(d, 0, 0, 0, 4 * slot if d == 1 else slot)
        remote(landed, landed, z_send.at[d - 1], z_recv.at[d - 1], head).wait_recv()

    def lat_direct(d, order):
        for a, h in order:
            remote(
                lat_at(d, 0, 0, h), lat_at(d, 0, a, h), lat_send.at[d],
                lat_recv.at[d, h if (a, h) in FIRST else 2], side[a],
            ).start()

    def lat_fetch(d):
        z_wait(d)
        lat_direct(d, FIRST)
        lat_twin(d, 0, 1)

    def lat_relay(d):
        for h in range(2):
            landed = lat_at(d, 0, 1 + h, h)
            remote(landed, landed, lat_send.at[d], lat_recv.at[d, h], twin).wait_recv()
            remote(landed, lat_at(d, 0, 3, h), lat_send.at[d], lat_recv.at[d, 2], side[2 - h]).start()

    def lat_finish(d):
        landed = lat_at(d, 0, 1, 0, 2 * slot)
        remote(landed, landed, lat_send.at[d], lat_recv.at[d, 2], twin).wait_recv()
        lat_twin(d, 1, 3)
    def z_begin():
        z_copy(1, 0, 0, slot).start()
        z_copy(1, 1, 0, piece).start()
        z_copy(1, 2, 1, piece).start()

    def z_end():
        z_copy(1, 1, 1, 2 * piece).start()
        z_copy(1, 3, 0, slot).start()

    loads = [local(hidden, mine, load_sem.at[0]), local(gain, gn, load_sem.at[1])]
    for i in range(steps):
        span = pl.ds(i * depth, depth)
        loads.append(local(w_down.at[:, span], wd.at[:, span], load_sem.at[2 + i]))
    pairs = [(w_query, wq), (w_key, wk), (w_value, wv), (w_out, wo)]
    lots = (0, 1, 1, 2)
    own = [local(src, dst.at[0], load_sem.at[2 + steps + lot]) for (src, dst), lot in zip(pairs, lots)]
    for q in range(chunks):
        own.append(local(hidden.at[pl.ds(q * r, r)], hid.at[pl.ds(q * group, r)], load_sem.at[5 + steps]))
    for copy in loads:
        copy.start()

    barrier = pltpu.get_barrier_semaphore()
    for h in (twin, side[1], side[2]):
        signal(barrier, ctx, h)
    when(ctx > 0, lambda: signal(barrier, ctx - 1, head))
    when(ctx + 1 < ctx_n, lambda: signal(barrier, ctx + 1, head))
    pl.semaphore_wait(barrier, 3 + jnp.minimum(ctx, 1) + jnp.minimum(ctx_n - 1 - ctx, 1))

    hid_direct(0, FIRST + REST[:2])
    swaps = [
        remote(src, dst.at[1], swap_send.at[lot], swap_recv.at[lot], twin) for (src, dst), lot in zip(pairs, lots)
    ]
    for copy in own:
        copy.start()
    for copy in swaps:
        copy.start()

    if ctx_n > 2:
        when(jnp.logical_and(ctx >= 1, ctx + 2 <= ctx_n), lambda: signal(far_sem.at[0], ctx - 1, head))

    loads[0].wait()
    loads[1].wait()
    down = jnp.zeros((rows, rank + tail), jnp.float32)
    for i in range(steps):
        loads[2 + i].wait()
        span = pl.ds(i * depth, depth)
        down += stacked(halves(mine[:, span]), halves(wd[:, span]), NT)
    raw = down[:, :rank]
    meansq = jnp.mean(raw * raw, axis=-1, keepdims=True)
    latent = raw * lax.rsqrt(meansq + EPSILON) * gn[...]
    shared = jnp.concatenate([down[:hr, rank:], down[hr:, rank:]], axis=1)
    for h in range(2):
        for j in range(tiles):
            lat_at(0, 0, 0, h)[pl.ds(j * hr, hr), :] = latent[h * hr : (h + 1) * hr, j * LANE : (j + 1) * LANE]
        lat_at(0, 0, 0, h)[pl.ds(tiles * hr, hr // 2), :] = shared[h * hr // 2 : (h + 1) * hr // 2]

    for d in range(2, ctx_n):
        when(ctx + d < ctx_n, lambda d=d: pl.semaphore_wait(far_sem.at[d - 2], 1))
        if d + 1 < ctx_n:
            when(
                jnp.logical_and(ctx >= 1, ctx + d < ctx_n),
                lambda d=d: signal(far_sem.at[d - 1], ctx - 1, head),
            )
    for d in range(ctx_n - 1, 1, -1):
        when(ctx + d < ctx_n, lambda d=d: z_copy(d, 0, 0, slot).start())
    lat_direct(0, DIRECT)
    lat_twin(0, 0, 1)

    def split_query(p):
        wqh[p], wql[p] = halves(wq[p])

    def kept(lot):
        whole = {0: wq.at[0], 1: wk, 2: wo.at[0]}[lot]
        local(whole, whole, load_sem.at[2 + steps + lot]).wait()
        remote(whole, whole, swap_send.at[lot], swap_recv.at[lot], twin).wait()

    hid_relay(0)
    own[0].wait()
    split_query(0)
    lat_relay(0)
    if ctx_n > 1:
        when(ctx + 1 < ctx_n, z_begin)
    swaps[0].wait()
    split_query(1)
    for d in range(2, ctx_n):
        when(ctx >= d, lambda d=d: lat_fetch(d))
    for d in range(2, ctx_n):
        when(ctx >= d, lambda d=d: lat_direct(d, REST[:2]))
    for q in range(1, chunks):
        when(jnp.logical_or(ctx < 2, core == 0), lambda q=q: hid_direct(q, FIRST))
    kept(1)
    local(mine, mine, load_sem.at[5 + steps]).wait()

    scale = key_width ** (-0.5)
    pad = jnp.zeros((group, lanes - rank - tail), jnp.float32)

    def queries(q):
        hid_finish(q)
        query = [jnp.zeros((group, key_width), jnp.float32) for _ in range(CORES)]
        for i in range(steps):
            span = pl.ds(i * depth, depth)
            given = halves(hid[pl.ds(q * group, group), span])
            for p in range(CORES):
                query[p] += stacked(given, (wqh[p, :, span], wql[p, :, span]), NT)
        for p in range(CORES):
            wide = stacked(halves(query[p][:, :nope] * scale), halves(wk[p]), NT)
            span = pl.ds(q * many + p * group, group)
            qh[span, :rank], ql[span, :rank] = halves(wide)
            rest = jnp.concatenate([query[p][:, nope:] * scale, pad], axis=1)
            qh[span, rank:], ql[span, rank:] = halves(rest)

    def keys(d, p):
        for s in range(4):
            at = d * block + (p * 4 + s) * rows
            packed = jnp.concatenate(
                [lat_at(d, p, s, h)[pl.ds(tiles * hr, hr // 2), :] for h in range(2)], axis=0
            )
            for h in range(2):
                span = pl.ds(at + h * hr, hr)
                for j in range(tiles):
                    lane = pl.ds(j * LANE, LANE)
                    kh[span, lane], kl[span, lane] = halves(lat_at(d, p, s, h)[pl.ds(j * hr, hr), :])
                lane = pl.ds(rank, LANE)
                kh[span, lane], kl[span, lane] = halves(packed if h == 0 else pltpu.roll(packed, tail, 1))

    def lat_ready(d):
        landed = lat_at(d, 1, 0, 0, 4 * slot)
        remote(landed, landed, lat_send.at[d], twin_recv.at[d], twin).wait_recv()
        keys(d, 1)

    def place(s, parity, i):
        sx, sy = lax.rem(s, 2), lax.div(s, 2)
        x, y = lax.rem(xbit + sx, 2), lax.rem(ybit + sy, 2)
        return ((2 * y + x) * CORES + parity) * rows + i

    def causal_of(q, count):
        line = lax.rem(lax.broadcasted_iota(jnp.int32, (many, 1), 0), group)
        column = lax.broadcasted_iota(jnp.int32, (1, count * block), 1)
        there = lax.rem(lax.div(column, 4 * rows), CORES)
        inner = lax.rem(column, 4 * rows)
        asked = place(lax.div(line, r), core, q * r + lax.rem(line, r))
        held = place(lax.div(inner, rows), core + there - 2 * core * there, lax.rem(inner, rows))
        return asked >= jnp.where(column < block, held, -1)

    def attend(q, count, between):
        mine_q = pl.ds(q * many, many)
        those = pl.ds(0, count * block)
        scores = stacked((qh[mine_q, :], ql[mine_q, :]), (kh[those, :], kl[those, :]), NT)
        causal = causal_of(q, count)
        scores = jnp.where(causal, scores, FLOOR)
        weights = jnp.where(causal, jnp.exp(scores - jnp.max(scores, axis=1, keepdims=True)), 0.0)
        between()
        total[mine_q, :] = jnp.sum(weights, axis=1, keepdims=True)
        acc[mine_q, :] = stacked(halves(weights), (kh[those, :rank], kl[those, :rank]))

    def attend_whole(q, between=lambda: None):
        for count in range(1, ctx_n + 1):
            when(ctx + 1 == count, lambda count=count: attend(q, count, between))

    def span_of(q, t):
        low, high = [width // 2 // LANE * i // cuts[q] * LANE for i in (t // 2, t // 2 + 1)]
        return pl.ds(2 * low + t % 2 * (high - low), high - low)

    def axes_of(t):
        return (1, 2) if t % 2 == 0 else (2, 1)

    def sum_copy(q, t, j):
        first, second = axes_of(t)
        span = span_of(q, t)
        here = pl.ds(q * r, r)

        def part_of(s):
            return part.at[pl.ds(q * group + s * r, r), span]

        src, dst, target = [
            (part_of(3), mid.at[here, span], first),
            (part_of(first), near.at[here, span], first),
            (fwd.at[here, span], last.at[here, span], second),
        ][j]
        return remote(src, dst, sum_send.at[0], sum_recv.at[2 * sum(cuts[:q]) + t, min(j, 1)], side[target])

    def project(q):
        found = []
        for p in range(CORES):
            span = pl.ds(q * many + p * group, group)
            found.append(stacked(halves(acc[span, :] / total[span, :]), halves(wv[p])))
        attended = halves(jnp.concatenate(found, axis=1))
        for t in range(2 * cuts[q]):
            span = span_of(q, t)
            part[pl.ds(q * group, group), span] = stacked(attended, (woh[:, span], wol[:, span]))
            sum_copy(q, t, 0).start()
        for t in range(2 * cuts[q]):
            sum_copy(q, t, 1).start()

    def second_stage(q):
        here = pl.ds(q * r, r)
        for t in range(2 * cuts[q]):
            span = span_of(q, t)
            sum_copy(q, t, 0).wait_recv()
            keep = axes_of(t)[1]
            fwd[here, span] = part[pl.ds(q * group + keep * r, r), span] + mid[here, span]
            sum_copy(q, t, 2).start()

    def collect(q):
        here = pl.ds(q * r, r)
        for t in range(2 * cuts[q]):
            span = span_of(q, t)
            landed = near.at[pl.ds(0, 2 * r), span]
            remote(landed, landed, sum_send.at[0], sum_recv.at[2 * sum(cuts[:q]) + t, 1], twin).wait_recv()
            out[here, span] = part[pl.ds(q * group, r), span] + near[here, span] + last[here, span]

    def split_out():
        kept(2)
        for p in range(CORES):
            span = pl.ds(p * vdim, vdim)
            woh[span, :], wol[span, :] = halves(wo[p])

    def z_join():
        z_wait(1)
        lat_twin(1, 0, 4)

    def begin(d):
        when(ctx >= d, lambda: lat_relay(d))

    def done(d):
        lat_finish(d)
        keys(d, 0)

    def z_done():
        z_join()
        keys(1, 0)

    queries(0)
    done(0)
    if ctx_n > 1:
        when(ctx + 1 < ctx_n, z_end)
    for d in range(2, ctx_n):
        begin(d)
    for q in range(1, chunks):
        when(jnp.logical_or(ctx < 2, core == 0), lambda q=q: hid_direct(q, REST[:2]))
    split_out()
    if ctx_n > 2:
        when(ctx >= 2, lambda: done(2))
    if ctx_n > 1:
        when(ctx >= 1, z_done)
    for d in range(3, ctx_n):
        when(ctx >= d, lambda d=d: done(d))
    for q in range(1, chunks):
        when(jnp.logical_and(ctx >= 2, core == 1), lambda q=q: hid_direct(q, FIRST + REST[:2]))
    for q in range(1, chunks):
        hid_relay(q)
    lat_ready(0)
    for d in range(1, ctx_n):
        when(ctx >= d, lambda d=d: lat_ready(d))
    attend_whole(0)
    project(0)
    for q in range(1, chunks):
        queries(q)
        attend_whole(q)
        second_stage(q - 1)
        project(q)
        collect(q - 1)
    second_stage(chunks - 1)
    collect(chunks - 1)

    sent = hid.at[pl.ds(0, 3 * rows)]
    for sem in (hid_send.at[0], sum_send.at[0]):
        remote(sent, sent, sem, hid_recv.at[0, 0], twin).wait_send()
    for d in range(ctx_n):
        def drain(d=d):
            sent = lat.at[pl.ds(0, (4 if d == 1 else 7) * slot)]
            remote(sent, sent, lat_send.at[d], twin_recv.at[d], twin).wait_send()

        def z_drain(d=d):
            sent = lat.at[pl.ds(0, (4 if d == 1 else 1) * slot)]
            remote(sent, sent, z_send.at[d - 1], z_recv.at[d - 1], head).wait_send()

        when(d <= ctx, drain)
        if d > 0:
            when(ctx + d < ctx_n, z_drain)


def square_call(ctx_n, hidden, w_query, w_down, gain, w_key_up, w_value_up, w_out):
    rows, width = hidden.shape
    rank, nope = w_key_up.shape
    vdim = w_value_up.shape[1]
    f32, bf16, dma = jnp.float32, jnp.bfloat16, pltpu.SemaphoreType.DMA
    chunks = 2
    cuts = (1, 2)
    r = rows // chunks
    block = CORES * 4 * rows
    lanes = rank + LANE
    steps = 3 if width % 384 == 0 else 1
    slot = rows * (rank // LANE) + rows // 2
    query = (CORES,) + w_query.shape
    both = (CORES * vdim, width)
    return pl.pallas_call(
        functools.partial(square_kernel, ctx_n, chunks, cuts),
        out_shape=pltpu.VMEM((rows, width), f32),
        in_specs=[pl.BlockSpec(memory_space=pltpu.HBM)] * 7,
        out_specs=pl.BlockSpec(memory_space=pltpu.VMEM),
        scratch_shapes=[
            pltpu.VMEM((rows, width), f32),
            pltpu.VMEM((4 * rows, width), f32),
            pltpu.VMEM(w_down.shape, f32),
            pltpu.VMEM((1, rank), f32),
            pltpu.VMEM(query, f32), pltpu.VMEM(query, bf16), pltpu.VMEM(query, bf16),
            pltpu.VMEM((CORES, rank, nope), f32),
            pltpu.VMEM((CORES, rank, vdim), f32),
            pltpu.VMEM((CORES, vdim, width), f32), pltpu.VMEM(both, bf16), pltpu.VMEM(both, bf16),
            pltpu.VMEM((ctx_n * CORES * 4 * slot, LANE), f32),
            pltpu.VMEM((ctx_n * block, lanes), bf16), pltpu.VMEM((ctx_n * block, lanes), bf16),
            pltpu.VMEM((block, lanes), bf16), pltpu.VMEM((block, lanes), bf16),
            pltpu.VMEM((block, 1), f32),
            pltpu.VMEM((block, rank), f32),
            pltpu.VMEM((4 * rows, width), f32),
        ] + [pltpu.VMEM((rows, width), f32)] * 4 + [
            dma((6 + steps,)),
            dma((3,)), dma((3,)),
            dma((1,)), dma((chunks, 3)),
            pltpu.SemaphoreType.REGULAR((max(ctx_n - 2, 1),)),
            dma((max(ctx_n - 1, 1),)), dma((max(ctx_n - 1, 1),)),
            dma((ctx_n,)), dma((ctx_n, 3)),
            dma((ctx_n,)),
            dma((1,)), dma((2 * sum(cuts), 2)),
        ],
        compiler_params=pltpu.CompilerParams(
            collective_id=0, has_side_effects=True, vmem_limit_bytes=60 * 1024 * 1024
        ),
    )(hidden, w_query, w_down, gain, w_key_up, w_value_up, w_out)


def on_device(ctx_n, chips, hidden, w_query, w_down, latent_gain, w_key_up, w_value_up, w_out):
    rows, width = hidden.shape
    rank, nope = w_key_up.shape
    vdim = w_value_up.shape[1]
    per_core = chips * rows
    block = CORES * per_core
    lanes = -(-w_down.shape[1] // 128) * 128
    steps = 3 if width % 384 == 0 else 1
    if chips == 4 and rows % 32 == 0 and width % 768 == 0 and rank % LANE == 0 and 2 * (w_down.shape[1] - rank) == LANE:
        return square_call(
            ctx_n, hidden, w_query.T, w_down.T, latent_gain.reshape(1, rank), w_key_up, w_value_up, w_out
        )
    square = chips == 4 and rows % 16 == 0 and width % 256 == 0
    pieces = 6 if width % 768 == 0 else 2
    f32, bf16, dma = jnp.float32, jnp.bfloat16, pltpu.SemaphoreType.DMA
    return pl.pallas_call(
        functools.partial(general_kernel, ctx_n, chips, square, steps, pieces),
        out_shape=jax.ShapeDtypeStruct((rows, width), f32),
        in_specs=[pl.BlockSpec(memory_space=pltpu.HBM)] * 7,
        out_specs=pl.BlockSpec(memory_space=pltpu.VMEM),
        scratch_shapes=[
            pltpu.VMEM((per_core, width), f32),
            pltpu.VMEM(w_down.shape[::-1], f32),
            pltpu.VMEM((CORES,) + w_query.shape[::-1], f32),
            pltpu.VMEM((1, rank), f32),
            pltpu.VMEM((CORES, rank, nope), f32),
            pltpu.VMEM((CORES, rank, vdim), f32),
            pltpu.VMEM((CORES, vdim, width), f32),
            pltpu.VMEM((ctx_n * block, lanes), f32),
            pltpu.VMEM((block, lanes), bf16),
            pltpu.VMEM((block, lanes), bf16),
            pltpu.VMEM((block, 1), f32),
            pltpu.VMEM((block, 1), f32),
            pltpu.VMEM((block, rank), f32),
            pltpu.VMEM((per_core, width), f32),
            pltpu.VMEM((per_core, width), f32),
            dma((2 + steps + 4,)),
            dma((4,)), dma((4,)),
            dma((chips, 2)), dma((chips, 2)),
            dma((ctx_n,)), dma((ctx_n,)),
            dma((ctx_n, chips, 2)), dma((ctx_n, chips, 2)),
            dma((ctx_n,)), dma((ctx_n,)),
            dma((pieces, chips)), dma((pieces, chips)),
        ],
        compiler_params=pltpu.CompilerParams(
            collective_id=0, has_side_effects=True, vmem_limit_bytes=60 * 1024 * 1024
        ),
    )(hidden, w_query.T, w_down.T, latent_gain.reshape(1, rank), w_key_up, w_value_up, w_out)


def solution(mesh):
    placed = (
        P(("ctx", "head"), None),
        P(None, "head"),
        P(),
        P(),
        P(None, "head"),
        P(None, "head"),
        P("head", None),
    )
    body = functools.partial(on_device, mesh.shape["ctx"], mesh.shape["head"] // CORES)
    return jax.shard_map(
        body, mesh=mesh, in_specs=placed, out_specs=P(("ctx", "head"), None), check_vma=False
    )
```

```python
import functools

import jax
import jax.numpy as jnp
from jax import lax
from jax.experimental import pallas as pl
from jax.experimental.pallas import tpu as pltpu
from jax.sharding import PartitionSpec as P

EPSILON = 1e-06
FLOOR = -1e30
CORES = 2
LANE = 128
FIRST = ((1, 0), (2, 1))
DIRECT = ((1, 0), (2, 1), (1, 1), (2, 0))
REST = ((1, 1), (2, 0), (3, 0), (3, 1))
MESH = pl.DeviceIdType.MESH
NN = (((1,), (0,)), ((), ()))
NT = (((1,), (1,)), ((), ()))


def halves(value):
    high = value.astype(jnp.bfloat16)
    return high, (value - high.astype(jnp.float32)).astype(jnp.bfloat16)


def product(left, right, dims=NN):
    (lh, ll), (rh, rl) = left, right
    dot = functools.partial(lax.dot_general, dimension_numbers=dims, preferred_element_type=jnp.float32)
    return dot(lh, rh) + (dot(ll, rh) + dot(lh, rl))


def stacked(left, right, dims=NN):
    (lh, ll), (rh, rl) = left, right
    dot = functools.partial(lax.dot_general, dimension_numbers=dims, preferred_element_type=jnp.float32)
    both = dot(jnp.concatenate([lh, ll], axis=0), rh)
    size = lh.shape[0]
    return both[:size] + (both[size:] + dot(lh, rl))


def general_kernel(
    ctx_n, chips, square, steps, pieces,
    hidden, w_query, w_down, gain, w_key, w_value, w_out, out,
    hid, wd, wq, gn, wk, wv, wo, lat, qh, ql, top, total, acc, part, landed,
    load_sem, swap_send, swap_recv, hid_send, hid_recv, col_send, col_recv,
    row_send, row_recv, twin_send, twin_recv, sum_send, sum_recv,
):
    rows, width = hidden.shape
    parts = 2 if square else 1
    rank = gn.shape[1]
    tail = wd.shape[0] - rank
    nope = wk.shape[2]
    per_core = chips * rows
    block = CORES * per_core
    lanes = lat.shape[1]
    ctx = lax.axis_index("ctx")
    head = lax.axis_index("head")
    chip, core = head // CORES, head % CORES
    twin = chip * CORES + (1 - core)

    def chip_at(offset):
        return lax.rem(chip + offset, chips)

    def to(o):
        if not square:
            return chip_at(o)
        return [chip, chip + 1 - 2 * lax.rem(chip, 2), lax.rem(chip + 2, 4), 3 - chip][o]

    def origin(o):
        return to(o) if square else chip_at(chips - o)

    def local(src, dst, sem):
        return pltpu.make_async_copy(src, dst, load_sem.at[sem])

    def remote(src, dst, send, recv, c, h):
        return pltpu.make_async_remote_copy(
            src_ref=src, dst_ref=dst, send_sem=send, recv_sem=recv,
            device_id={"ctx": c, "head": h}, device_id_type=MESH,
        )

    def at_rows(start, size):
        return pl.ds(pl.multiple_of(start, 8), size)

    my_hid = hid.at[at_rows(chip * rows, rows)]
    depth = width // steps
    loads = [local(hidden, my_hid, 0), local(gain, gn, 1)]
    for s in range(steps):
        span = pl.ds(s * depth, depth)
        loads.append(local(w_down.at[:, span], wd.at[:, span], 2 + s))
    pairs = [(w_query, wq), (w_key, wk), (w_value, wv), (w_out, wo)]
    own = [local(src, dst.at[core], 2 + steps + i) for i, (src, dst) in enumerate(pairs)]
    for copy in loads:
        copy.start()

    barrier = pltpu.get_barrier_semaphore()
    for o in range(1, chips):
        pl.semaphore_signal(barrier, inc=1, device_id={"ctx": ctx, "head": chip_at(o) * CORES + core}, device_id_type=MESH)
    pl.semaphore_signal(barrier, inc=1, device_id={"ctx": ctx, "head": twin}, device_id_type=MESH)
    for o in range(1, ctx_n):
        pl.semaphore_signal(barrier, inc=1, device_id={"ctx": lax.rem(ctx + o, ctx_n), "head": head}, device_id_type=MESH)
    pl.semaphore_wait(barrier, chips - 1 + 1 + ctx_n - 1)

    def share(source, spot, send, recv):
        def start_of(o, h):
            target = to(o)
            return remote(source(h), spot(chip, h), send(o, h), recv(o, h), ctx, target * CORES + core)

        def seen(o, h):
            place_of = spot(origin(o), h)
            return remote(place_of, place_of, send(o, h), recv(o, h), ctx, twin)

        def passed(h):
            place_of = spot(to(1 + h), h)
            return remote(place_of, place_of, send(3, h), recv(3, h), ctx, to(2 - h) * CORES + core)

        direct = [(1, 0), (2, 1), (1, 1), (2, 0)] if square else [(o, 0) for o in range(1, chips)]

        def start():
            for o, h in direct:
                start_of(o, h).start()

        def relay():
            if square:
                for h in range(2):
                    seen(1 + h, h).wait_recv()
                    passed(h).start()

        def finish():
            for o, h in [(1, 1), (2, 0), (3, 0), (3, 1)] if square else direct:
                seen(o, h).wait_recv()

        def drain():
            for o, h in direct:
                start_of(o, h).wait_send()
            if square:
                for h in range(2):
                    passed(h).wait_send()

        return start, relay, finish, drain

    half = width // parts

    def hid_half(h):
        return pl.ds(h * half, half)

    hid_start, hid_relay, hid_finish, hid_drain = share(
        lambda h: hidden.at[:, hid_half(h)],
        lambda k, h: hid.at[at_rows(k * rows, rows), hid_half(h)],
        lambda o, h: hid_send.at[o, h],
        lambda o, h: hid_recv.at[o, h],
    )
    hid_start()
    swaps = [remote(src, dst.at[core], swap_send.at[i], swap_recv.at[i], ctx, twin) for i, (src, dst) in enumerate(pairs)]
    for copy in own:
        copy.start()
    for copy in swaps:
        copy.start()

    loads[0].wait()
    loads[1].wait()
    down = jnp.zeros((rows, rank + tail), jnp.float32)
    for s in range(steps):
        loads[2 + s].wait()
        span = pl.ds(s * depth, depth)
        down += product(halves(my_hid[:, span]), halves(wd[:, span]), NT)
    raw = down[:, :rank]
    meansq = jnp.mean(raw * raw, axis=-1, keepdims=True)
    blank = jnp.zeros((rows, lanes - rank - tail), jnp.float32)

    def place(b, p, k):
        return ((b * CORES + p) * chips + k) * rows

    mine = at_rows(place(ctx, core, chip), rows)
    lat[mine, :rank] = raw * lax.rsqrt(meansq + EPSILON) * gn[...]
    lat[mine, rank:] = jnp.concatenate([down[:, rank:], blank], axis=1)

    def col_copy(b):
        spot = lat.at[at_rows(place(b, core, chip), rows)]
        return remote(spot, spot, col_send.at[b], col_recv.at[b], jnp.minimum(ctx + 1, ctx_n - 1), head)

    def latents(b):
        def spot(k, h):
            return lat.at[at_rows(place(b, core, k) + h * (rows // parts), rows // parts)]

        return share(
            lambda h: spot(chip, h), spot, lambda o, h: row_send.at[b, o, h], lambda o, h: row_recv.at[b, o, h]
        )

    def twin_copy(b, p):
        spot = lat.at[at_rows(place(b, p, 0), per_core)]
        return remote(spot, spot, twin_send.at[b], twin_recv.at[b], ctx, twin)

    def spread(b):
        @pl.when(ctx + 1 < ctx_n)
        def _():
            col_copy(b).start()

        latents(b)[0]()

    def gather_rows(b):
        latents(b)[2]()
        twin_copy(b, core).start()

    spread(ctx)
    hid_relay()
    for d in range(1, ctx_n):
        @pl.when(d <= ctx)
        def _():
            col_copy(ctx - d).wait_recv()
            spread(ctx - d)

    latents(ctx)[1]()

    hid_finish()
    for i in range(2):
        own[i].wait()
        swaps[i].wait()
    scale = wq.shape[1] ** (-0.5)
    pad = jnp.zeros((per_core, lanes - rank - tail), jnp.float32)
    query = [jnp.zeros((per_core, wq.shape[1]), jnp.float32) for _ in range(CORES)]
    for s in range(steps):
        span = pl.ds(s * depth, depth)
        piece = halves(hid[:, span])
        for p in range(CORES):
            query[p] += product(piece, halves(wq[p, :, span]), NT)
    for p in range(CORES):
        wide = product(halves(query[p][:, :nope] * scale), halves(wk[p]), NT)
        span = pl.ds(p * per_core, per_core)
        qh[span, :rank], ql[span, :rank] = halves(wide)
        qh[span, rank:], ql[span, rank:] = halves(jnp.concatenate([query[p][:, nope:] * scale, pad], axis=1))

    def spots(index, parity):
        inner = lax.rem(index, per_core)
        return (lax.div(inner, rows) * CORES + parity) * rows + lax.rem(inner, rows)

    def attend(b, first):
        keys = halves(lat[at_rows(place(b, 0, 0), block), :])
        scores = product((qh[...], ql[...]), keys, NT)
        if first:
            line = lax.broadcasted_iota(jnp.int32, (block, 1), 0)
            column = lax.broadcasted_iota(jnp.int32, (1, block), 1)
            causal = spots(line, core) >= spots(column, lax.div(column, per_core))
            scores = jnp.where(causal, scores, FLOOR)
            peak = jnp.max(scores, axis=1, keepdims=True)
        else:
            peak = jnp.maximum(top[...], jnp.max(scores, axis=1, keepdims=True))
        weights = jnp.exp(scores - peak)
        if first:
            weights = jnp.where(causal, weights, 0.0)
        mixed = product(halves(weights), (keys[0][:, :rank], keys[1][:, :rank]))
        added = jnp.sum(weights, axis=1, keepdims=True)
        if first:
            total[...] = added
            acc[...] = mixed
        else:
            fade = jnp.exp(top[...] - peak)
            total[...] = total[...] * fade + added
            acc[...] = acc[...] * fade + mixed
        top[...] = peak

    def relay_at(d):
        if d < ctx_n:
            @pl.when(d <= ctx)
            def _():
                latents(ctx - d)[1]()

    relay_at(1)
    gather_rows(ctx)
    twin_copy(ctx, 1 - core).wait_recv()
    attend(ctx, True)
    for d in range(1, ctx_n):
        @pl.when(d <= ctx)
        def _():
            relay_at(d + 1)
            gather_rows(ctx - d)
            twin_copy(ctx - d, 1 - core).wait_recv()
            attend(ctx - d, False)

    for i in range(2, 4):
        own[i].wait()
        swaps[i].wait()
    heads = []
    for p in range(CORES):
        span = pl.ds(p * per_core, per_core)
        heads.append(product(halves(acc[span, :] / total[span, :]), halves(wv[p])))
    attended = halves(jnp.concatenate(heads, axis=1))
    columns = width // pieces

    def cut(ref, k, t):
        return ref.at[at_rows(k * rows, rows), pl.ds(t * columns, columns)]

    def axes_of(t):
        return (1, 2) if t % 2 == 0 else (2, 1)

    def sum_copy(t, j):
        if not square:
            return remote(
                cut(part, chip_at(j), t), cut(landed, chip, t), sum_send.at[t, j], sum_recv.at[t, j],
                ctx, chip_at(j) * CORES + core,
            )
        first, second = axes_of(t)
        src = [to(3), to(first), to(second)][j]
        dst = [to(3), to(first), to(3)][j]
        target = [to(first), to(first), to(second)][j]
        return remote(cut(part, src, t), cut(landed, dst, t), sum_send.at[t, j], sum_recv.at[t, j], ctx, target * CORES + core)

    def second_stage(t):
        sum_copy(t, 0).wait_recv()
        keep = to(axes_of(t)[1])
        cut(part, keep, t)[...] = cut(part, keep, t)[...] + cut(landed, keep, t)[...]
        sum_copy(t, 2).start()

    kinds = (0, 1) if square else tuple(range(1, chips))
    for t in range(pieces):
        span = pl.ds(t * columns, columns)
        weight = jnp.concatenate([wo[p, :, span] for p in range(CORES)], axis=0)
        part[:, span] = product(attended, halves(weight))
        for j in kinds:
            sum_copy(t, j).start()
        if square and t >= 2:
            second_stage(t - 2)
    if square:
        for t in range(max(pieces - 2, 0), pieces):
            second_stage(t)
    for t in range(pieces):
        result = cut(part, chip, t)[...]
        if square:
            for j in (1, 2):
                sum_copy(t, j).wait_recv()
            result += cut(landed, chip, t)[...] + cut(landed, to(axes_of(t)[0]), t)[...]
        else:
            for j in kinds:
                sum_copy(t, j).wait_recv()
                result += cut(landed, origin(j), t)[...]
        out[:, pl.ds(t * columns, columns)] = result

    hid_drain()
    for t in range(pieces):
        for j in kinds + ((2,) if square else ()):
            sum_copy(t, j).wait_send()
    for d in range(ctx_n):
        @pl.when(d <= ctx)
        def _():
            @pl.when(ctx + 1 < ctx_n)
            def _():
                col_copy(ctx - d).wait_send()

            latents(ctx - d)[3]()
            twin_copy(ctx - d, core).wait_send()


def square_kernel(
    ctx_n, chunks, cuts,
    hidden, w_query, w_down, gain, w_key, w_value, w_out, out,
    mine, hid, wd, gn, wq, wqh, wql, wk, wv, wo, woh, wol, lat, kh, kl, qh, ql, total, acc,
    part, mid, fwd, near, last,
    load_sem, swap_send, swap_recv, hid_send, hid_recv, far_sem, z_send, z_recv,
    lat_send, lat_recv, twin_recv, sum_send, sum_recv,
):
    rows, width = hidden.shape
    rank = gn.shape[1]
    tail = wd.shape[0] - rank
    nope, vdim = wk.shape[2], wv.shape[2]
    key_width = wq.shape[1]
    lanes = kh.shape[1]
    r = rows // chunks
    group = 4 * r
    many = CORES * group
    block = CORES * 4 * rows
    hr = rows // 2
    tiles = rank // LANE
    piece = hr * tiles + hr // 2
    slot = 2 * piece
    half = width // 2
    steps = 3 if width % 384 == 0 else 1
    depth = width // steps
    ctx = lax.axis_index("ctx")
    head = lax.axis_index("head")
    chip, core = head // CORES, head % CORES
    twin = chip * CORES + (1 - core)
    xbit, ybit = lax.rem(chip, 2), lax.div(chip, 2)
    side = [None, (2 * ybit + 1 - xbit) * CORES + core, (2 * (1 - ybit) + xbit) * CORES + core]

    def local(src, dst, sem):
        return pltpu.make_async_copy(src, dst, sem)

    def remote(src, dst, send, recv, h, c=ctx):
        return pltpu.make_async_remote_copy(
            src_ref=src, dst_ref=dst, send_sem=send, recv_sem=recv,
            device_id={"ctx": c, "head": h}, device_id_type=MESH,
        )

    def signal(sem, c, h):
        pl.semaphore_signal(sem, inc=1, device_id={"ctx": c, "head": h}, device_id_type=MESH)

    def when(condition, *actions):
        @pl.when(condition)
        def _():
            for action in actions:
                action()

    def spot(q, s, h):
        return hid.at[pl.ds((q * 4 + s) * r, r), pl.ds(h * half, half)]

    def hid_direct(q, order):
        for a, h in order:
            remote(
                hidden.at[pl.ds(q * r, r), pl.ds(h * half, half)], spot(q, a, h),
                hid_send.at[0], hid_recv.at[q, h if (a, h) in FIRST else 2], side[a],
            ).start()

    def hid_relay(q):
        for h in range(2):
            landed = spot(q, 1 + h, h)
            remote(landed, landed, hid_send.at[0], hid_recv.at[q, h], twin).wait_recv()
            remote(landed, spot(q, 3, h), hid_send.at[0], hid_recv.at[q, 2], side[2 - h]).start()

    def hid_finish(q):
        landed = hid.at[pl.ds((q * 4 + 1) * r, 2 * r)]
        remote(landed, landed, hid_send.at[0], hid_recv.at[q, 2], twin).wait_recv()

    def lat_at(d, p, s, h=0, size=piece):
        return lat.at[pl.ds(((d * CORES + p) * 4 + s) * slot + h * piece, size)]

    def lat_twin(d, s, count):
        size = count * slot
        remote(lat_at(d, 0, s, 0, size), lat_at(d, 1, s, 0, size), lat_send.at[d], twin_recv.at[d], twin).start()

    def z_copy(d, s, h, size):
        c = jnp.minimum(ctx + d, ctx_n - 1)
        return remote(lat_at(0, 0, s, h, size), lat_at(d, 0, s, h, size), z_send.at[d - 1], z_recv.at[d - 1], head, c)

    def z_wait(d):
        landed = lat_at(d, 0, 0, 0, 4 * slot if d == 1 else slot)
        remote(landed, landed, z_send.at[d - 1], z_recv.at[d - 1], head).wait_recv()

    def lat_direct(d, order):
        for a, h in order:
            remote(
                lat_at(d, 0, 0, h), lat_at(d, 0, a, h), lat_send.at[d],
                lat_recv.at[d, h if (a, h) in FIRST else 2], side[a],
            ).start()

    def lat_fetch(d):
        z_wait(d)
        lat_direct(d, FIRST)
        lat_twin(d, 0, 1)

    def lat_relay(d):
        for h in range(2):
            landed = lat_at(d, 0, 1 + h, h)
            remote(landed, landed, lat_send.at[d], lat_recv.at[d, h], twin).wait_recv()
            remote(landed, lat_at(d, 0, 3, h), lat_send.at[d], lat_recv.at[d, 2], side[2 - h]).start()

    def lat_finish(d):
        landed = lat_at(d, 0, 1, 0, 2 * slot)
        remote(landed, landed, lat_send.at[d], lat_recv.at[d, 2], twin).wait_recv()
        lat_twin(d, 1, 3)
    def z_begin():
        z_copy(1, 0, 0, slot).start()
        z_copy(1, 1, 0, piece).start()
        z_copy(1, 2, 1, piece).start()

    def z_end():
        z_copy(1, 1, 1, 2 * piece).start()
        z_copy(1, 3, 0, slot).start()

    loads = [local(hidden, mine, load_sem.at[0]), local(gain, gn, load_sem.at[1])]
    for i in range(steps):
        span = pl.ds(i * depth, depth)
        loads.append(local(w_down.at[:, span], wd.at[:, span], load_sem.at[2 + i]))
    pairs = [(w_query, wq), (w_key, wk), (w_value, wv), (w_out, wo)]
    lots = (0, 1, 1, 2)
    own = [local(src, dst.at[0], load_sem.at[2 + steps + lot]) for (src, dst), lot in zip(pairs, lots)]
    for q in range(chunks):
        own.append(local(hidden.at[pl.ds(q * r, r)], hid.at[pl.ds(q * group, r)], load_sem.at[5 + steps]))
    for copy in loads:
        copy.start()

    barrier = pltpu.get_barrier_semaphore()
    for h in (twin, side[1], side[2]):
        signal(barrier, ctx, h)
    when(ctx > 0, lambda: signal(barrier, ctx - 1, head))
    when(ctx + 1 < ctx_n, lambda: signal(barrier, ctx + 1, head))
    pl.semaphore_wait(barrier, 3 + jnp.minimum(ctx, 1) + jnp.minimum(ctx_n - 1 - ctx, 1))

    hid_direct(0, FIRST)
    swaps = [
        remote(src, dst.at[1], swap_send.at[lot], swap_recv.at[lot], twin) for (src, dst), lot in zip(pairs, lots)
    ]
    for copy in own:
        copy.start()
    for copy in swaps:
        copy.start()

    if ctx_n > 2:
        when(jnp.logical_and(ctx >= 1, ctx + 2 <= ctx_n), lambda: signal(far_sem.at[0], ctx - 1, head))

    loads[0].wait()
    loads[1].wait()
    down = jnp.zeros((rows, rank + tail), jnp.float32)
    for i in range(steps):
        loads[2 + i].wait()
        span = pl.ds(i * depth, depth)
        down += stacked(halves(mine[:, span]), halves(wd[:, span]), NT)
    raw = down[:, :rank]
    meansq = jnp.mean(raw * raw, axis=-1, keepdims=True)
    latent = raw * lax.rsqrt(meansq + EPSILON) * gn[...]
    shared = jnp.concatenate([down[:hr, rank:], down[hr:, rank:]], axis=1)
    for h in range(2):
        for j in range(tiles):
            lat_at(0, 0, 0, h)[pl.ds(j * hr, hr), :] = latent[h * hr : (h + 1) * hr, j * LANE : (j + 1) * LANE]
        lat_at(0, 0, 0, h)[pl.ds(tiles * hr, hr // 2), :] = shared[h * hr // 2 : (h + 1) * hr // 2]

    for d in range(2, ctx_n):
        when(ctx + d < ctx_n, lambda d=d: pl.semaphore_wait(far_sem.at[d - 2], 1))
        if d + 1 < ctx_n:
            when(
                jnp.logical_and(ctx >= 1, ctx + d < ctx_n),
                lambda d=d: signal(far_sem.at[d - 1], ctx - 1, head),
            )
    for d in range(ctx_n - 1, 1, -1):
        when(ctx + d < ctx_n, lambda d=d: z_copy(d, 0, 0, slot).start())
    lat_direct(0, DIRECT)
    hid_direct(0, REST[:2])
    lat_twin(0, 0, 1)

    def split_query(p):
        wqh[p], wql[p] = halves(wq[p])

    def kept(lot):
        whole = {0: wq.at[0], 1: wk, 2: wo.at[0]}[lot]
        local(whole, whole, load_sem.at[2 + steps + lot]).wait()
        remote(whole, whole, swap_send.at[lot], swap_recv.at[lot], twin).wait()

    hid_relay(0)
    own[0].wait()
    split_query(0)
    lat_relay(0)
    if ctx_n > 1:
        when(ctx + 1 < ctx_n, z_begin)
    swaps[0].wait()
    split_query(1)
    for d in range(2, ctx_n):
        when(ctx >= d, lambda d=d: lat_fetch(d))
    for d in range(2, ctx_n):
        when(ctx >= d, lambda d=d: lat_direct(d, REST[:2]))
    for q in range(1, chunks):
        when(jnp.logical_or(ctx < 2, core == 0), lambda q=q: hid_direct(q, FIRST))
    kept(1)
    local(mine, mine, load_sem.at[5 + steps]).wait()

    scale = key_width ** (-0.5)
    pad = jnp.zeros((group, lanes - rank - tail), jnp.float32)

    def queries(q):
        hid_finish(q)
        query = [jnp.zeros((group, key_width), jnp.float32) for _ in range(CORES)]
        for i in range(steps):
            span = pl.ds(i * depth, depth)
            given = halves(hid[pl.ds(q * group, group), span])
            for p in range(CORES):
                query[p] += stacked(given, (wqh[p, :, span], wql[p, :, span]), NT)
        for p in range(CORES):
            wide = stacked(halves(query[p][:, :nope] * scale), halves(wk[p]), NT)
            span = pl.ds(q * many + p * group, group)
            qh[span, :rank], ql[span, :rank] = halves(wide)
            rest = jnp.concatenate([query[p][:, nope:] * scale, pad], axis=1)
            qh[span, rank:], ql[span, rank:] = halves(rest)

    def keys(d, p):
        for s in range(4):
            at = d * block + (p * 4 + s) * rows
            packed = jnp.concatenate(
                [lat_at(d, p, s, h)[pl.ds(tiles * hr, hr // 2), :] for h in range(2)], axis=0
            )
            for h in range(2):
                span = pl.ds(at + h * hr, hr)
                for j in range(tiles):
                    lane = pl.ds(j * LANE, LANE)
                    kh[span, lane], kl[span, lane] = halves(lat_at(d, p, s, h)[pl.ds(j * hr, hr), :])
                lane = pl.ds(rank, LANE)
                kh[span, lane], kl[span, lane] = halves(packed if h == 0 else pltpu.roll(packed, tail, 1))

    def lat_ready(d):
        landed = lat_at(d, 1, 0, 0, 4 * slot)
        remote(landed, landed, lat_send.at[d], twin_recv.at[d], twin).wait_recv()
        keys(d, 1)

    def place(s, parity, i):
        sx, sy = lax.rem(s, 2), lax.div(s, 2)
        x, y = lax.rem(xbit + sx, 2), lax.rem(ybit + sy, 2)
        return ((2 * y + x) * CORES + parity) * rows + i

    def causal_of(q, count):
        line = lax.rem(lax.broadcasted_iota(jnp.int32, (many, 1), 0), group)
        column = lax.broadcasted_iota(jnp.int32, (1, count * block), 1)
        there = lax.rem(lax.div(column, 4 * rows), CORES)
        inner = lax.rem(column, 4 * rows)
        asked = place(lax.div(line, r), core, q * r + lax.rem(line, r))
        held = place(lax.div(inner, rows), core + there - 2 * core * there, lax.rem(inner, rows))
        return asked >= jnp.where(column < block, held, -1)

    def attend(q, count, between):
        mine_q = pl.ds(q * many, many)
        those = pl.ds(0, count * block)
        scores = stacked((qh[mine_q, :], ql[mine_q, :]), (kh[those, :], kl[those, :]), NT)
        causal = causal_of(q, count)
        scores = jnp.where(causal, scores, FLOOR)
        weights = jnp.where(causal, jnp.exp(scores - jnp.max(scores, axis=1, keepdims=True)), 0.0)
        between()
        total[mine_q, :] = jnp.sum(weights, axis=1, keepdims=True)
        acc[mine_q, :] = stacked(halves(weights), (kh[those, :rank], kl[those, :rank]))

    def attend_whole(q, between=lambda: None):
        for count in range(1, ctx_n + 1):
            when(ctx + 1 == count, lambda count=count: attend(q, count, between))

    def span_of(q, t):
        low, high = [width // 2 // LANE * i // cuts[q] * LANE for i in (t // 2, t // 2 + 1)]
        return pl.ds(2 * low + t % 2 * (high - low), high - low)

    def axes_of(t):
        return (1, 2) if t % 2 == 0 else (2, 1)

    def sum_copy(q, t, j):
        first, second = axes_of(t)
        span = span_of(q, t)
        here = pl.ds(q * r, r)

        def part_of(s):
            return part.at[pl.ds(q * group + s * r, r), span]

        src, dst, target = [
            (part_of(3), mid.at[here, span], first),
            (part_of(first), near.at[here, span], first),
            (fwd.at[here, span], last.at[here, span], second),
        ][j]
        return remote(src, dst, sum_send.at[0], sum_recv.at[2 * sum(cuts[:q]) + t, min(j, 1)], side[target])

    def project(q, between=lambda: None):
        found = []
        for p in range(CORES):
            span = pl.ds(q * many + p * group, group)
            found.append(stacked(halves(acc[span, :] / total[span, :]), halves(wv[p])))
        attended = halves(jnp.concatenate(found, axis=1))
        for t in range(2 * cuts[q]):
            span = span_of(q, t)
            part[pl.ds(q * group, group), span] = stacked(attended, (woh[:, span], wol[:, span]))
            sum_copy(q, t, 0).start()
        between()
        for t in range(2 * cuts[q]):
            sum_copy(q, t, 1).start()

    def second_stage(q, low, high):
        here = pl.ds(q * r, r)
        for t in range(low, high):
            span = span_of(q, t)
            sum_copy(q, t, 0).wait_recv()
            keep = axes_of(t)[1]
            fwd[here, span] = part[pl.ds(q * group + keep * r, r), span] + mid[here, span]
            sum_copy(q, t, 2).start()

    def collect(q):
        here = pl.ds(q * r, r)
        for t in range(2 * cuts[q]):
            span = span_of(q, t)
            landed = near.at[pl.ds(0, 2 * r), span]
            remote(landed, landed, sum_send.at[0], sum_recv.at[2 * sum(cuts[:q]) + t, 1], twin).wait_recv()
            out[here, span] = part[pl.ds(q * group, r), span] + near[here, span] + last[here, span]

    def split_out():
        kept(2)
        for p in range(CORES):
            span = pl.ds(p * vdim, vdim)
            woh[span, :], wol[span, :] = halves(wo[p])

    def z_join():
        z_wait(1)
        lat_twin(1, 0, 4)

    def begin(d):
        when(ctx >= d, lambda: lat_relay(d))

    def done(d):
        lat_finish(d)
        keys(d, 0)

    def z_done():
        z_join()
        keys(1, 0)

    queries(0)
    done(0)
    if ctx_n > 1:
        when(ctx + 1 < ctx_n, z_end)
    for d in range(2, ctx_n):
        begin(d)
    for q in range(1, chunks):
        when(jnp.logical_or(ctx < 2, core == 0), lambda q=q: hid_direct(q, REST[:2]))
    split_out()
    if ctx_n > 2:
        when(ctx >= 2, lambda: done(2))
    if ctx_n > 1:
        when(ctx >= 1, z_done)
    for d in range(3, ctx_n):
        when(ctx >= d, lambda d=d: done(d))
    for q in range(1, chunks):
        when(jnp.logical_and(ctx >= 2, core == 1), lambda q=q: hid_direct(q, FIRST + REST[:2]))
    for q in range(1, chunks):
        hid_relay(q)
    lat_ready(0)
    for d in range(1, ctx_n):
        when(ctx >= d, lambda d=d: lat_ready(d))
    attend_whole(0)
    project(0)
    for q in range(1, chunks):
        queries(q)
        attend_whole(q)
        second_stage(q - 1, 0, 2)
        project(q, lambda: second_stage(q - 1, 2, 2 * cuts[q - 1]))
        second_stage(q, 0, 2 * cuts[q])
        collect(q - 1)
    collect(chunks - 1)

    sent = hid.at[pl.ds(0, 3 * rows)]
    for sem in (hid_send.at[0], sum_send.at[0]):
        remote(sent, sent, sem, hid_recv.at[0, 0], twin).wait_send()
    for d in range(ctx_n):
        def drain(d=d):
            sent = lat.at[pl.ds(0, (4 if d == 1 else 7) * slot)]
            remote(sent, sent, lat_send.at[d], twin_recv.at[d], twin).wait_send()

        def z_drain(d=d):
            sent = lat.at[pl.ds(0, (4 if d == 1 else 1) * slot)]
            remote(sent, sent, z_send.at[d - 1], z_recv.at[d - 1], head).wait_send()

        when(d <= ctx, drain)
        if d > 0:
            when(ctx + d < ctx_n, z_drain)


def square_call(ctx_n, hidden, w_query, w_down, gain, w_key_up, w_value_up, w_out):
    rows, width = hidden.shape
    rank, nope = w_key_up.shape
    vdim = w_value_up.shape[1]
    f32, bf16, dma = jnp.float32, jnp.bfloat16, pltpu.SemaphoreType.DMA
    chunks = 2
    cuts = (2, 2)
    r = rows // chunks
    block = CORES * 4 * rows
    lanes = rank + LANE
    steps = 3 if width % 384 == 0 else 1
    slot = rows * (rank // LANE) + rows // 2
    query = (CORES,) + w_query.shape
    both = (CORES * vdim, width)
    return pl.pallas_call(
        functools.partial(square_kernel, ctx_n, chunks, cuts),
        out_shape=pltpu.VMEM((rows, width), f32),
        in_specs=[pl.BlockSpec(memory_space=pltpu.HBM)] * 7,
        out_specs=pl.BlockSpec(memory_space=pltpu.VMEM),
        scratch_shapes=[
            pltpu.VMEM((rows, width), f32),
            pltpu.VMEM((4 * rows, width), f32),
            pltpu.VMEM(w_down.shape, f32),
            pltpu.VMEM((1, rank), f32),
            pltpu.VMEM(query, f32), pltpu.VMEM(query, bf16), pltpu.VMEM(query, bf16),
            pltpu.VMEM((CORES, rank, nope), f32),
            pltpu.VMEM((CORES, rank, vdim), f32),
            pltpu.VMEM((CORES, vdim, width), f32), pltpu.VMEM(both, bf16), pltpu.VMEM(both, bf16),
            pltpu.VMEM((ctx_n * CORES * 4 * slot, LANE), f32),
            pltpu.VMEM((ctx_n * block, lanes), bf16), pltpu.VMEM((ctx_n * block, lanes), bf16),
            pltpu.VMEM((block, lanes), bf16), pltpu.VMEM((block, lanes), bf16),
            pltpu.VMEM((block, 1), f32),
            pltpu.VMEM((block, rank), f32),
            pltpu.VMEM((4 * rows, width), f32),
        ] + [pltpu.VMEM((rows, width), f32)] * 4 + [
            dma((6 + steps,)),
            dma((3,)), dma((3,)),
            dma((1,)), dma((chunks, 3)),
            pltpu.SemaphoreType.REGULAR((max(ctx_n - 2, 1),)),
            dma((max(ctx_n - 1, 1),)), dma((max(ctx_n - 1, 1),)),
            dma((ctx_n,)), dma((ctx_n, 3)),
            dma((ctx_n,)),
            dma((1,)), dma((2 * sum(cuts), 2)),
        ],
        compiler_params=pltpu.CompilerParams(
            collective_id=0, has_side_effects=True, vmem_limit_bytes=60 * 1024 * 1024
        ),
    )(hidden, w_query, w_down, gain, w_key_up, w_value_up, w_out)


def on_device(ctx_n, chips, hidden, w_query, w_down, latent_gain, w_key_up, w_value_up, w_out):
    rows, width = hidden.shape
    rank, nope = w_key_up.shape
    vdim = w_value_up.shape[1]
    per_core = chips * rows
    block = CORES * per_core
    lanes = -(-w_down.shape[1] // 128) * 128
    steps = 3 if width % 384 == 0 else 1
    if chips == 4 and rows % 32 == 0 and width % 768 == 0 and rank % LANE == 0 and 2 * (w_down.shape[1] - rank) == LANE:
        return square_call(
            ctx_n, hidden, w_query.T, w_down.T, latent_gain.reshape(1, rank), w_key_up, w_value_up, w_out
        )
    square = chips == 4 and rows % 16 == 0 and width % 256 == 0
    pieces = 6 if width % 768 == 0 else 2
    f32, bf16, dma = jnp.float32, jnp.bfloat16, pltpu.SemaphoreType.DMA
    return pl.pallas_call(
        functools.partial(general_kernel, ctx_n, chips, square, steps, pieces),
        out_shape=jax.ShapeDtypeStruct((rows, width), f32),
        in_specs=[pl.BlockSpec(memory_space=pltpu.HBM)] * 7,
        out_specs=pl.BlockSpec(memory_space=pltpu.VMEM),
        scratch_shapes=[
            pltpu.VMEM((per_core, width), f32),
            pltpu.VMEM(w_down.shape[::-1], f32),
            pltpu.VMEM((CORES,) + w_query.shape[::-1], f32),
            pltpu.VMEM((1, rank), f32),
            pltpu.VMEM((CORES, rank, nope), f32),
            pltpu.VMEM((CORES, rank, vdim), f32),
            pltpu.VMEM((CORES, vdim, width), f32),
            pltpu.VMEM((ctx_n * block, lanes), f32),
            pltpu.VMEM((block, lanes), bf16),
            pltpu.VMEM((block, lanes), bf16),
            pltpu.VMEM((block, 1), f32),
            pltpu.VMEM((block, 1), f32),
            pltpu.VMEM((block, rank), f32),
            pltpu.VMEM((per_core, width), f32),
            pltpu.VMEM((per_core, width), f32),
            dma((2 + steps + 4,)),
            dma((4,)), dma((4,)),
            dma((chips, 2)), dma((chips, 2)),
            dma((ctx_n,)), dma((ctx_n,)),
            dma((ctx_n, chips, 2)), dma((ctx_n, chips, 2)),
            dma((ctx_n,)), dma((ctx_n,)),
            dma((pieces, chips)), dma((pieces, chips)),
        ],
        compiler_params=pltpu.CompilerParams(
            collective_id=0, has_side_effects=True, vmem_limit_bytes=60 * 1024 * 1024
        ),
    )(hidden, w_query.T, w_down.T, latent_gain.reshape(1, rank), w_key_up, w_value_up, w_out)


def solution(mesh):
    placed = (
        P(("ctx", "head"), None),
        P(None, "head"),
        P(),
        P(),
        P(None, "head"),
        P(None, "head"),
        P("head", None),
    )
    body = functools.partial(on_device, mesh.shape["ctx"], mesh.shape["head"] // CORES)
    return jax.shard_map(
        body, mesh=mesh, in_specs=placed, out_specs=P(("ctx", "head"), None), check_vma=False
    )
```

```python
import functools

import jax
import jax.numpy as jnp
from jax import lax
from jax.experimental import pallas as pl
from jax.experimental.pallas import tpu as pltpu
from jax.sharding import PartitionSpec as P

EPSILON = 1e-06
FLOOR = -1e30
CORES = 2
LANE = 128
FIRST = ((1, 0), (2, 1))
DIRECT = ((1, 0), (2, 1), (1, 1), (2, 0))
REST = ((1, 1), (2, 0), (3, 0), (3, 1))
MESH = pl.DeviceIdType.MESH
NN = (((1,), (0,)), ((), ()))
NT = (((1,), (1,)), ((), ()))


def halves(value):
    high = value.astype(jnp.bfloat16)
    return high, (value - high.astype(jnp.float32)).astype(jnp.bfloat16)


def product(left, right, dims=NN):
    (lh, ll), (rh, rl) = left, right
    dot = functools.partial(lax.dot_general, dimension_numbers=dims, preferred_element_type=jnp.float32)
    return dot(lh, rh) + (dot(ll, rh) + dot(lh, rl))


def stacked(left, right, dims=NN):
    (lh, ll), (rh, rl) = left, right
    dot = functools.partial(lax.dot_general, dimension_numbers=dims, preferred_element_type=jnp.float32)
    both = dot(jnp.concatenate([lh, ll], axis=0), rh)
    size = lh.shape[0]
    return both[:size] + (both[size:] + dot(lh, rl))


def general_kernel(
    ctx_n, chips, square, steps, pieces,
    hidden, w_query, w_down, gain, w_key, w_value, w_out, out,
    hid, wd, wq, gn, wk, wv, wo, lat, qh, ql, top, total, acc, part, landed,
    load_sem, swap_send, swap_recv, hid_send, hid_recv, col_send, col_recv,
    row_send, row_recv, twin_send, twin_recv, sum_send, sum_recv,
):
    rows, width = hidden.shape
    parts = 2 if square else 1
    rank = gn.shape[1]
    tail = wd.shape[0] - rank
    nope = wk.shape[2]
    per_core = chips * rows
    block = CORES * per_core
    lanes = lat.shape[1]
    ctx = lax.axis_index("ctx")
    head = lax.axis_index("head")
    chip, core = head // CORES, head % CORES
    twin = chip * CORES + (1 - core)

    def chip_at(offset):
        return lax.rem(chip + offset, chips)

    def to(o):
        if not square:
            return chip_at(o)
        return [chip, chip + 1 - 2 * lax.rem(chip, 2), lax.rem(chip + 2, 4), 3 - chip][o]

    def origin(o):
        return to(o) if square else chip_at(chips - o)

    def local(src, dst, sem):
        return pltpu.make_async_copy(src, dst, load_sem.at[sem])

    def remote(src, dst, send, recv, c, h):
        return pltpu.make_async_remote_copy(
            src_ref=src, dst_ref=dst, send_sem=send, recv_sem=recv,
            device_id={"ctx": c, "head": h}, device_id_type=MESH,
        )

    def at_rows(start, size):
        return pl.ds(pl.multiple_of(start, 8), size)

    my_hid = hid.at[at_rows(chip * rows, rows)]
    depth = width // steps
    loads = [local(hidden, my_hid, 0), local(gain, gn, 1)]
    for s in range(steps):
        span = pl.ds(s * depth, depth)
        loads.append(local(w_down.at[:, span], wd.at[:, span], 2 + s))
    pairs = [(w_query, wq), (w_key, wk), (w_value, wv), (w_out, wo)]
    own = [local(src, dst.at[core], 2 + steps + i) for i, (src, dst) in enumerate(pairs)]
    for copy in loads:
        copy.start()

    barrier = pltpu.get_barrier_semaphore()
    for o in range(1, chips):
        pl.semaphore_signal(barrier, inc=1, device_id={"ctx": ctx, "head": chip_at(o) * CORES + core}, device_id_type=MESH)
    pl.semaphore_signal(barrier, inc=1, device_id={"ctx": ctx, "head": twin}, device_id_type=MESH)
    for o in range(1, ctx_n):
        pl.semaphore_signal(barrier, inc=1, device_id={"ctx": lax.rem(ctx + o, ctx_n), "head": head}, device_id_type=MESH)
    pl.semaphore_wait(barrier, chips - 1 + 1 + ctx_n - 1)

    def share(source, spot, send, recv):
        def start_of(o, h):
            target = to(o)
            return remote(source(h), spot(chip, h), send(o, h), recv(o, h), ctx, target * CORES + core)

        def seen(o, h):
            place_of = spot(origin(o), h)
            return remote(place_of, place_of, send(o, h), recv(o, h), ctx, twin)

        def passed(h):
            place_of = spot(to(1 + h), h)
            return remote(place_of, place_of, send(3, h), recv(3, h), ctx, to(2 - h) * CORES + core)

        direct = [(1, 0), (2, 1), (1, 1), (2, 0)] if square else [(o, 0) for o in range(1, chips)]

        def start():
            for o, h in direct:
                start_of(o, h).start()

        def relay():
            if square:
                for h in range(2):
                    seen(1 + h, h).wait_recv()
                    passed(h).start()

        def finish():
            for o, h in [(1, 1), (2, 0), (3, 0), (3, 1)] if square else direct:
                seen(o, h).wait_recv()

        def drain():
            for o, h in direct:
                start_of(o, h).wait_send()
            if square:
                for h in range(2):
                    passed(h).wait_send()

        return start, relay, finish, drain

    half = width // parts

    def hid_half(h):
        return pl.ds(h * half, half)

    hid_start, hid_relay, hid_finish, hid_drain = share(
        lambda h: hidden.at[:, hid_half(h)],
        lambda k, h: hid.at[at_rows(k * rows, rows), hid_half(h)],
        lambda o, h: hid_send.at[o, h],
        lambda o, h: hid_recv.at[o, h],
    )
    hid_start()
    swaps = [remote(src, dst.at[core], swap_send.at[i], swap_recv.at[i], ctx, twin) for i, (src, dst) in enumerate(pairs)]
    for copy in own:
        copy.start()
    for copy in swaps:
        copy.start()

    loads[0].wait()
    loads[1].wait()
    down = jnp.zeros((rows, rank + tail), jnp.float32)
    for s in range(steps):
        loads[2 + s].wait()
        span = pl.ds(s * depth, depth)
        down += product(halves(my_hid[:, span]), halves(wd[:, span]), NT)
    raw = down[:, :rank]
    meansq = jnp.mean(raw * raw, axis=-1, keepdims=True)
    blank = jnp.zeros((rows, lanes - rank - tail), jnp.float32)

    def place(b, p, k):
        return ((b * CORES + p) * chips + k) * rows

    mine = at_rows(place(ctx, core, chip), rows)
    lat[mine, :rank] = raw * lax.rsqrt(meansq + EPSILON) * gn[...]
    lat[mine, rank:] = jnp.concatenate([down[:, rank:], blank], axis=1)

    def col_copy(b):
        spot = lat.at[at_rows(place(b, core, chip), rows)]
        return remote(spot, spot, col_send.at[b], col_recv.at[b], jnp.minimum(ctx + 1, ctx_n - 1), head)

    def latents(b):
        def spot(k, h):
            return lat.at[at_rows(place(b, core, k) + h * (rows // parts), rows // parts)]

        return share(
            lambda h: spot(chip, h), spot, lambda o, h: row_send.at[b, o, h], lambda o, h: row_recv.at[b, o, h]
        )

    def twin_copy(b, p):
        spot = lat.at[at_rows(place(b, p, 0), per_core)]
        return remote(spot, spot, twin_send.at[b], twin_recv.at[b], ctx, twin)

    def spread(b):
        @pl.when(ctx + 1 < ctx_n)
        def _():
            col_copy(b).start()

        latents(b)[0]()

    def gather_rows(b):
        latents(b)[2]()
        twin_copy(b, core).start()

    spread(ctx)
    hid_relay()
    for d in range(1, ctx_n):
        @pl.when(d <= ctx)
        def _():
            col_copy(ctx - d).wait_recv()
            spread(ctx - d)

    latents(ctx)[1]()

    hid_finish()
    for i in range(2):
        own[i].wait()
        swaps[i].wait()
    scale = wq.shape[1] ** (-0.5)
    pad = jnp.zeros((per_core, lanes - rank - tail), jnp.float32)
    query = [jnp.zeros((per_core, wq.shape[1]), jnp.float32) for _ in range(CORES)]
    for s in range(steps):
        span = pl.ds(s * depth, depth)
        piece = halves(hid[:, span])
        for p in range(CORES):
            query[p] += product(piece, halves(wq[p, :, span]), NT)
    for p in range(CORES):
        wide = product(halves(query[p][:, :nope] * scale), halves(wk[p]), NT)
        span = pl.ds(p * per_core, per_core)
        qh[span, :rank], ql[span, :rank] = halves(wide)
        qh[span, rank:], ql[span, rank:] = halves(jnp.concatenate([query[p][:, nope:] * scale, pad], axis=1))

    def spots(index, parity):
        inner = lax.rem(index, per_core)
        return (lax.div(inner, rows) * CORES + parity) * rows + lax.rem(inner, rows)

    def attend(b, first):
        keys = halves(lat[at_rows(place(b, 0, 0), block), :])
        scores = product((qh[...], ql[...]), keys, NT)
        if first:
            line = lax.broadcasted_iota(jnp.int32, (block, 1), 0)
            column = lax.broadcasted_iota(jnp.int32, (1, block), 1)
            causal = spots(line, core) >= spots(column, lax.div(column, per_core))
            scores = jnp.where(causal, scores, FLOOR)
            peak = jnp.max(scores, axis=1, keepdims=True)
        else:
            peak = jnp.maximum(top[...], jnp.max(scores, axis=1, keepdims=True))
        weights = jnp.exp(scores - peak)
        if first:
            weights = jnp.where(causal, weights, 0.0)
        mixed = product(halves(weights), (keys[0][:, :rank], keys[1][:, :rank]))
        added = jnp.sum(weights, axis=1, keepdims=True)
        if first:
            total[...] = added
            acc[...] = mixed
        else:
            fade = jnp.exp(top[...] - peak)
            total[...] = total[...] * fade + added
            acc[...] = acc[...] * fade + mixed
        top[...] = peak

    def relay_at(d):
        if d < ctx_n:
            @pl.when(d <= ctx)
            def _():
                latents(ctx - d)[1]()

    relay_at(1)
    gather_rows(ctx)
    twin_copy(ctx, 1 - core).wait_recv()
    attend(ctx, True)
    for d in range(1, ctx_n):
        @pl.when(d <= ctx)
        def _():
            relay_at(d + 1)
            gather_rows(ctx - d)
            twin_copy(ctx - d, 1 - core).wait_recv()
            attend(ctx - d, False)

    for i in range(2, 4):
        own[i].wait()
        swaps[i].wait()
    heads = []
    for p in range(CORES):
        span = pl.ds(p * per_core, per_core)
        heads.append(product(halves(acc[span, :] / total[span, :]), halves(wv[p])))
    attended = halves(jnp.concatenate(heads, axis=1))
    columns = width // pieces

    def cut(ref, k, t):
        return ref.at[at_rows(k * rows, rows), pl.ds(t * columns, columns)]

    def axes_of(t):
        return (1, 2) if t % 2 == 0 else (2, 1)

    def sum_copy(t, j):
        if not square:
            return remote(
                cut(part, chip_at(j), t), cut(landed, chip, t), sum_send.at[t, j], sum_recv.at[t, j],
                ctx, chip_at(j) * CORES + core,
            )
        first, second = axes_of(t)
        src = [to(3), to(first), to(second)][j]
        dst = [to(3), to(first), to(3)][j]
        target = [to(first), to(first), to(second)][j]
        return remote(cut(part, src, t), cut(landed, dst, t), sum_send.at[t, j], sum_recv.at[t, j], ctx, target * CORES + core)

    def second_stage(t):
        sum_copy(t, 0).wait_recv()
        keep = to(axes_of(t)[1])
        cut(part, keep, t)[...] = cut(part, keep, t)[...] + cut(landed, keep, t)[...]
        sum_copy(t, 2).start()

    kinds = (0, 1) if square else tuple(range(1, chips))
    for t in range(pieces):
        span = pl.ds(t * columns, columns)
        weight = jnp.concatenate([wo[p, :, span] for p in range(CORES)], axis=0)
        part[:, span] = product(attended, halves(weight))
        for j in kinds:
            sum_copy(t, j).start()
        if square and t >= 2:
            second_stage(t - 2)
    if square:
        for t in range(max(pieces - 2, 0), pieces):
            second_stage(t)
    for t in range(pieces):
        result = cut(part, chip, t)[...]
        if square:
            for j in (1, 2):
                sum_copy(t, j).wait_recv()
            result += cut(landed, chip, t)[...] + cut(landed, to(axes_of(t)[0]), t)[...]
        else:
            for j in kinds:
                sum_copy(t, j).wait_recv()
                result += cut(landed, origin(j), t)[...]
        out[:, pl.ds(t * columns, columns)] = result

    hid_drain()
    for t in range(pieces):
        for j in kinds + ((2,) if square else ()):
            sum_copy(t, j).wait_send()
    for d in range(ctx_n):
        @pl.when(d <= ctx)
        def _():
            @pl.when(ctx + 1 < ctx_n)
            def _():
                col_copy(ctx - d).wait_send()

            latents(ctx - d)[3]()
            twin_copy(ctx - d, core).wait_send()


def square_kernel(
    ctx_n, chunks, cuts,
    hidden, w_query, w_down, gain, w_key, w_value, w_out, out,
    mine, hid, wd, gn, wq, wqh, wql, wk, wv, wo, woh, wol, lat, kh, kl, qh, ql, total, acc,
    part, mid, fwd, near, last,
    load_sem, swap_send, swap_recv, hid_send, hid_recv, far_sem, z_send, z_recv,
    lat_send, lat_recv, twin_recv, sum_send, sum_recv,
):
    rows, width = hidden.shape
    rank = gn.shape[1]
    tail = wd.shape[0] - rank
    nope, vdim = wk.shape[2], wv.shape[2]
    key_width = wq.shape[1]
    lanes = kh.shape[1]
    r = rows // chunks
    group = 4 * r
    many = CORES * group
    block = CORES * 4 * rows
    hr = rows // 2
    tiles = rank // LANE
    piece = hr * tiles + hr // 2
    slot = 2 * piece
    half = width // 2
    steps = 3 if width % 384 == 0 else 1
    depth = width // steps
    ctx = lax.axis_index("ctx")
    head = lax.axis_index("head")
    chip, core = head // CORES, head % CORES
    twin = chip * CORES + (1 - core)
    xbit, ybit = lax.rem(chip, 2), lax.div(chip, 2)
    side = [None, (2 * ybit + 1 - xbit) * CORES + core, (2 * (1 - ybit) + xbit) * CORES + core]

    def local(src, dst, sem):
        return pltpu.make_async_copy(src, dst, sem)

    def remote(src, dst, send, recv, h, c=ctx):
        return pltpu.make_async_remote_copy(
            src_ref=src, dst_ref=dst, send_sem=send, recv_sem=recv,
            device_id={"ctx": c, "head": h}, device_id_type=MESH,
        )

    def signal(sem, c, h):
        pl.semaphore_signal(sem, inc=1, device_id={"ctx": c, "head": h}, device_id_type=MESH)

    def when(condition, *actions):
        @pl.when(condition)
        def _():
            for action in actions:
                action()

    def spot(q, s, h):
        return hid.at[pl.ds((q * 4 + s) * r, r), pl.ds(h * half, half)]

    def hid_direct(q, order):
        for a, h in order:
            remote(
                hidden.at[pl.ds(q * r, r), pl.ds(h * half, half)], spot(q, a, h),
                hid_send.at[0], hid_recv.at[q, h if (a, h) in FIRST else 2], side[a],
            ).start()

    def hid_relay(q):
        for h in range(2):
            landed = spot(q, 1 + h, h)
            remote(landed, landed, hid_send.at[0], hid_recv.at[q, h], twin).wait_recv()
            remote(landed, spot(q, 3, h), hid_send.at[0], hid_recv.at[q, 2], side[2 - h]).start()

    def hid_finish(q):
        landed = hid.at[pl.ds((q * 4 + 1) * r, 2 * r)]
        remote(landed, landed, hid_send.at[0], hid_recv.at[q, 2], twin).wait_recv()

    def lat_at(d, p, s, h=0, size=piece):
        return lat.at[pl.ds(((d * CORES + p) * 4 + s) * slot + h * piece, size)]

    def lat_twin(d, s, count):
        size = count * slot
        remote(lat_at(d, 0, s, 0, size), lat_at(d, 1, s, 0, size), lat_send.at[d], twin_recv.at[0], twin).start()

    def z_copy(d, s, h, size):
        c = jnp.minimum(ctx + d, ctx_n - 1)
        return remote(lat_at(0, 0, s, h, size), lat_at(d, 0, s, h, size), z_send.at[d - 1], z_recv.at[d - 1], head, c)

    def z_wait(d):
        landed = lat_at(d, 0, 0, 0, 4 * slot if d == 1 else slot)
        remote(landed, landed, z_send.at[d - 1], z_recv.at[d - 1], head).wait_recv()

    def lat_direct(d, order):
        for a, h in order:
            remote(
                lat_at(d, 0, 0, h), lat_at(d, 0, a, h), lat_send.at[d],
                lat_recv.at[max(d - 1, 0), h if (a, h) in FIRST else 2], side[a],
            ).start()

    def lat_fetch(d):
        z_wait(d)
        lat_direct(d, FIRST)
        lat_twin(d, 0, 1)

    def lat_relay(d):
        for h in range(2):
            landed = lat_at(d, 0, 1 + h, h)
            remote(landed, landed, lat_send.at[d], lat_recv.at[max(d - 1, 0), h], twin).wait_recv()
            remote(landed, lat_at(d, 0, 3, h), lat_send.at[d], lat_recv.at[max(d - 1, 0), 2], side[2 - h]).start()

    def lat_finish(d):
        landed = lat_at(d, 0, 1, 0, 2 * slot)
        remote(landed, landed, lat_send.at[d], lat_recv.at[max(d - 1, 0), 2], twin).wait_recv()
        lat_twin(d, 1, 3)
    def z_begin():
        z_copy(1, 0, 0, slot).start()
        z_copy(1, 1, 0, piece).start()
        z_copy(1, 2, 1, piece).start()

    def z_end():
        z_copy(1, 1, 1, 2 * piece).start()
        z_copy(1, 3, 0, slot).start()

    loads = [local(hidden, mine, load_sem.at[0]), local(gain, gn, load_sem.at[1])]
    for i in range(steps):
        span = pl.ds(i * depth, depth)
        loads.append(local(w_down.at[:, span], wd.at[:, span], load_sem.at[2 + i]))
    pairs = [(w_query, wq), (w_key, wk), (w_value, wv), (w_out, wo)]
    lots = (0, 1, 1, 2)
    own = [local(src, dst.at[0], load_sem.at[2 + steps + lot]) for (src, dst), lot in zip(pairs, lots)]
    for q in range(chunks):
        own.append(local(hidden.at[pl.ds(q * r, r)], hid.at[pl.ds(q * group, r)], load_sem.at[5 + steps]))
    for copy in loads:
        copy.start()

    barrier = pltpu.get_barrier_semaphore()
    for h in (twin, side[1], side[2]):
        signal(barrier, ctx, h)
    when(ctx > 0, lambda: signal(barrier, ctx - 1, head))
    when(ctx + 1 < ctx_n, lambda: signal(barrier, ctx + 1, head))
    pl.semaphore_wait(barrier, 3 + jnp.minimum(ctx, 1) + jnp.minimum(ctx_n - 1 - ctx, 1))

    hid_direct(0, FIRST)
    swaps = [
        remote(src, dst.at[1], swap_send.at[lot], swap_recv.at[lot], twin) for (src, dst), lot in zip(pairs, lots)
    ]
    for copy in own:
        copy.start()
    for copy in swaps:
        copy.start()

    if ctx_n > 2:
        when(jnp.logical_and(ctx >= 1, ctx + 2 <= ctx_n), lambda: signal(far_sem.at[0], ctx - 1, head))

    loads[0].wait()
    loads[1].wait()
    down = jnp.zeros((rows, rank + tail), jnp.float32)
    for i in range(steps):
        loads[2 + i].wait()
        span = pl.ds(i * depth, depth)
        down += stacked(halves(mine[:, span]), halves(wd[:, span]), NT)
    raw = down[:, :rank]
    meansq = jnp.mean(raw * raw, axis=-1, keepdims=True)
    latent = raw * lax.rsqrt(meansq + EPSILON) * gn[...]
    shared = jnp.concatenate([down[:hr, rank:], down[hr:, rank:]], axis=1)
    for h in range(2):
        for j in range(tiles):
            lat_at(0, 0, 0, h)[pl.ds(j * hr, hr), :] = latent[h * hr : (h + 1) * hr, j * LANE : (j + 1) * LANE]
        lat_at(0, 0, 0, h)[pl.ds(tiles * hr, hr // 2), :] = shared[h * hr // 2 : (h + 1) * hr // 2]

    for d in range(2, ctx_n):
        when(ctx + d < ctx_n, lambda d=d: pl.semaphore_wait(far_sem.at[d - 2], 1))
        if d + 1 < ctx_n:
            when(
                jnp.logical_and(ctx >= 1, ctx + d < ctx_n),
                lambda d=d: signal(far_sem.at[d - 1], ctx - 1, head),
            )
    for d in range(2, ctx_n):
        when(ctx + d < ctx_n, lambda d=d: z_copy(d, 0, 0, slot).start())
    lat_direct(0, DIRECT)
    hid_direct(0, REST[:2])
    lat_twin(0, 0, 1)

    def split_query(p):
        wqh[p], wql[p] = halves(wq[p])

    def kept(lot):
        whole = {0: wq.at[0], 1: wk, 2: wo.at[0]}[lot]
        local(whole, whole, load_sem.at[2 + steps + lot]).wait()
        remote(whole, whole, swap_send.at[lot], swap_recv.at[lot], twin).wait()

    hid_relay(0)
    own[0].wait()
    split_query(0)
    lat_relay(0)
    if ctx_n > 1:
        when(ctx + 1 < ctx_n, z_begin)
    swaps[0].wait()
    split_query(1)
    for d in range(2, ctx_n):
        when(ctx >= d, lambda d=d: lat_fetch(d))
    for d in range(2, ctx_n):
        when(ctx >= d, lambda d=d: lat_direct(d, REST[:2]))
    for q in range(1, chunks):
        when(jnp.logical_or(ctx < 2, core == 0), lambda q=q: hid_direct(q, FIRST))
    kept(1)
    local(mine, mine, load_sem.at[5 + steps]).wait()

    scale = key_width ** (-0.5)
    pad = jnp.zeros((group, lanes - rank - tail), jnp.float32)

    def queries(q):
        hid_finish(q)
        query = [jnp.zeros((group, key_width), jnp.float32) for _ in range(CORES)]
        for i in range(steps):
            span = pl.ds(i * depth, depth)
            given = halves(hid[pl.ds(q * group, group), span])
            for p in range(CORES):
                query[p] += stacked(given, (wqh[p, :, span], wql[p, :, span]), NT)
        for p in range(CORES):
            wide = stacked(halves(query[p][:, :nope] * scale), halves(wk[p]), NT)
            span = pl.ds(q * many + p * group, group)
            qh[span, :rank], ql[span, :rank] = halves(wide)
            rest = jnp.concatenate([query[p][:, nope:] * scale, pad], axis=1)
            qh[span, rank:], ql[span, rank:] = halves(rest)

    def keys(d, p):
        for s in range(4):
            at = d * block + (p * 4 + s) * rows
            packed = jnp.concatenate(
                [lat_at(d, p, s, h)[pl.ds(tiles * hr, hr // 2), :] for h in range(2)], axis=0
            )
            for h in range(2):
                span = pl.ds(at + h * hr, hr)
                for j in range(tiles):
                    lane = pl.ds(j * LANE, LANE)
                    kh[span, lane], kl[span, lane] = halves(lat_at(d, p, s, h)[pl.ds(j * hr, hr), :])
                lane = pl.ds(rank, LANE)
                kh[span, lane], kl[span, lane] = halves(packed if h == 0 else pltpu.roll(packed, tail, 1))

    def lat_ready(count):
        landed = lat.at[pl.ds(0, 4 * count * slot)]
        remote(landed, landed, lat_send.at[0], twin_recv.at[0], twin).wait_recv()
        for d in range(count):
            keys(d, 1)

    def place(s, parity, i):
        sx, sy = lax.rem(s, 2), lax.div(s, 2)
        x, y = lax.rem(xbit + sx, 2), lax.rem(ybit + sy, 2)
        return ((2 * y + x) * CORES + parity) * rows + i

    def causal_of(q, count):
        line = lax.rem(lax.broadcasted_iota(jnp.int32, (many, 1), 0), group)
        column = lax.broadcasted_iota(jnp.int32, (1, count * block), 1)
        there = lax.rem(lax.div(column, 4 * rows), CORES)
        inner = lax.rem(column, 4 * rows)
        asked = place(lax.div(line, r), core, q * r + lax.rem(line, r))
        held = place(lax.div(inner, rows), core + there - 2 * core * there, lax.rem(inner, rows))
        return asked >= jnp.where(column < block, held, -1)

    def attend(q, count, between):
        mine_q = pl.ds(q * many, many)
        those = pl.ds(0, count * block)
        scores = stacked((qh[mine_q, :], ql[mine_q, :]), (kh[those, :], kl[those, :]), NT)
        causal = causal_of(q, count)
        scores = jnp.where(causal, scores, FLOOR)
        weights = jnp.where(causal, jnp.exp(scores - jnp.max(scores, axis=1, keepdims=True)), 0.0)
        between()
        total[mine_q, :] = jnp.sum(weights, axis=1, keepdims=True)
        acc[mine_q, :] = stacked(halves(weights), (kh[those, :rank], kl[those, :rank]))

    def attend_whole(q, between=lambda: None):
        for count in range(1, ctx_n + 1):
            when(ctx + 1 == count, lambda count=count: attend(q, count, between))

    def span_of(q, t):
        low, high = [width // 2 // LANE * i // cuts[q] * LANE for i in (t // 2, t // 2 + 1)]
        return pl.ds(2 * low + t % 2 * (high - low), high - low)

    def axes_of(t):
        return (1, 2) if t % 2 == 0 else (2, 1)

    def sum_copy(q, t, j):
        first, second = axes_of(t)
        span = span_of(q, t)
        here = pl.ds(q * r, r)

        def part_of(s):
            return part.at[pl.ds(q * group + s * r, r), span]

        src, dst, target = [
            (part_of(3), mid.at[here, span], first),
            (part_of(first), near.at[here, span], first),
            (fwd.at[here, span], last.at[here, span], second),
        ][j]
        return remote(src, dst, sum_send.at[0], sum_recv.at[2 * sum(cuts[:q]) + t if j == 0 else 2 * sum(cuts) + q], side[target])

    def project(q, between=lambda: None):
        found = []
        for p in range(CORES):
            span = pl.ds(q * many + p * group, group)
            found.append(stacked(halves(acc[span, :] / total[span, :]), halves(wv[p])))
        attended = halves(jnp.concatenate(found, axis=1))
        for t in range(2 * cuts[q]):
            span = span_of(q, t)
            part[pl.ds(q * group, group), span] = stacked(attended, (woh[:, span], wol[:, span]))
            sum_copy(q, t, 0).start()
        between()
        for t in range(2 * cuts[q]):
            sum_copy(q, t, 1).start()

    def second_stage(q, low, high):
        here = pl.ds(q * r, r)
        for t in range(low, high):
            span = span_of(q, t)
            sum_copy(q, t, 0).wait_recv()
            keep = axes_of(t)[1]
            fwd[here, span] = part[pl.ds(q * group + keep * r, r), span] + mid[here, span]
            sum_copy(q, t, 2).start()

    def collect(q):
        here = pl.ds(q * r, r)
        landed = near.at[pl.ds(0, 2 * r)]
        remote(landed, landed, sum_send.at[0], sum_recv.at[2 * sum(cuts) + q], twin).wait_recv()
        out[here, :] = part[pl.ds(q * group, r), :] + near[here, :] + last[here, :]

    def split_out():
        kept(2)
        for p in range(CORES):
            span = pl.ds(p * vdim, vdim)
            woh[span, :], wol[span, :] = halves(wo[p])

    def z_join():
        z_wait(1)
        lat_twin(1, 0, 4)

    def begin(d):
        when(ctx >= d, lambda: lat_relay(d))

    def done(d):
        lat_finish(d)
        keys(d, 0)

    def z_done():
        z_join()
        keys(1, 0)

    def sent_on():
        done(0)
        if ctx_n > 1:
            when(ctx + 1 < ctx_n, z_end)

    when(ctx < 1, sent_on)
    queries(0)
    when(ctx >= 1, sent_on)
    for d in range(2, ctx_n):
        begin(d)
    for q in range(1, chunks):
        when(jnp.logical_or(ctx < 2, core == 0), lambda q=q: hid_direct(q, REST[:2]))
    split_out()
    if ctx_n > 2:
        when(ctx >= 2, lambda: done(2))
    if ctx_n > 1:
        when(ctx >= 1, z_done)
    for d in range(3, ctx_n):
        when(ctx >= d, lambda d=d: done(d))
    for q in range(1, chunks):
        when(jnp.logical_and(ctx >= 2, core == 1), lambda q=q: hid_direct(q, FIRST + REST[:2]))
    for q in range(1, chunks):
        hid_relay(q)
    for count in range(1, ctx_n + 1):
        when(ctx + 1 == count, lambda count=count: lat_ready(count))
    attend_whole(0)
    project(0)
    for q in range(1, chunks):
        queries(q)
        attend_whole(q, lambda: second_stage(q - 1, 0, 3))
        second_stage(q - 1, 3, 2 * cuts[q - 1])
        project(q)
        second_stage(q, 0, 2 * cuts[q])
        collect(q - 1)
    collect(chunks - 1)

    sent = hid.at[pl.ds(0, 3 * rows)]
    for sem in (hid_send.at[0], sum_send.at[0]):
        remote(sent, sent, sem, hid_recv.at[0, 0], twin).wait_send()
    for d in range(ctx_n):
        def drain(d=d):
            sent = lat.at[pl.ds(0, (4 if d == 1 else 7) * slot)]
            remote(sent, sent, lat_send.at[d], twin_recv.at[0], twin).wait_send()

        def z_drain(d=d):
            sent = lat.at[pl.ds(0, (4 if d == 1 else 1) * slot)]
            remote(sent, sent, z_send.at[d - 1], z_recv.at[d - 1], head).wait_send()

        when(d <= ctx, drain)
        if d > 0:
            when(ctx + d < ctx_n, z_drain)


def square_call(ctx_n, hidden, w_query, w_down, gain, w_key_up, w_value_up, w_out):
    rows, width = hidden.shape
    rank, nope = w_key_up.shape
    vdim = w_value_up.shape[1]
    f32, bf16, dma = jnp.float32, jnp.bfloat16, pltpu.SemaphoreType.DMA
    chunks = 2
    cuts = (2, 2)
    r = rows // chunks
    block = CORES * 4 * rows
    lanes = rank + LANE
    steps = 3 if width % 384 == 0 else 1
    slot = rows * (rank // LANE) + rows // 2
    query = (CORES,) + w_query.shape
    both = (CORES * vdim, width)
    return pl.pallas_call(
        functools.partial(square_kernel, ctx_n, chunks, cuts),
        out_shape=pltpu.VMEM((rows, width), f32),
        in_specs=[pl.BlockSpec(memory_space=pltpu.HBM)] * 7,
        out_specs=pl.BlockSpec(memory_space=pltpu.VMEM),
        scratch_shapes=[
            pltpu.VMEM((rows, width), f32),
            pltpu.VMEM((4 * rows, width), f32),
            pltpu.VMEM(w_down.shape, f32),
            pltpu.VMEM((1, rank), f32),
            pltpu.VMEM(query, f32), pltpu.VMEM(query, bf16), pltpu.VMEM(query, bf16),
            pltpu.VMEM((CORES, rank, nope), f32),
            pltpu.VMEM((CORES, rank, vdim), f32),
            pltpu.VMEM((CORES, vdim, width), f32), pltpu.VMEM(both, bf16), pltpu.VMEM(both, bf16),
            pltpu.VMEM((ctx_n * CORES * 4 * slot, LANE), f32),
            pltpu.VMEM((ctx_n * block, lanes), bf16), pltpu.VMEM((ctx_n * block, lanes), bf16),
            pltpu.VMEM((block, lanes), bf16), pltpu.VMEM((block, lanes), bf16),
            pltpu.VMEM((block, 1), f32),
            pltpu.VMEM((block, rank), f32),
            pltpu.VMEM((4 * rows, width), f32),
        ] + [pltpu.VMEM((rows, width), f32)] * 4 + [
            dma((6 + steps,)),
            dma((3,)), dma((3,)),
            dma((1,)), dma((chunks, 3)),
            pltpu.SemaphoreType.REGULAR((max(ctx_n - 2, 1),)),
            dma((max(ctx_n - 1, 1),)), dma((max(ctx_n - 1, 1),)),
            dma((ctx_n,)), dma((max(ctx_n - 1, 1), 3)),
            dma((1,)),
            dma((1,)), dma((2 * sum(cuts) + chunks,)),
        ],
        compiler_params=pltpu.CompilerParams(
            collective_id=0, has_side_effects=True, vmem_limit_bytes=60 * 1024 * 1024
        ),
    )(hidden, w_query, w_down, gain, w_key_up, w_value_up, w_out)


def on_device(ctx_n, chips, hidden, w_query, w_down, latent_gain, w_key_up, w_value_up, w_out):
    rows, width = hidden.shape
    rank, nope = w_key_up.shape
    vdim = w_value_up.shape[1]
    per_core = chips * rows
    block = CORES * per_core
    lanes = -(-w_down.shape[1] // 128) * 128
    steps = 3 if width % 384 == 0 else 1
    if chips == 4 and rows % 32 == 0 and width % 768 == 0 and rank % LANE == 0 and 2 * (w_down.shape[1] - rank) == LANE:
        return square_call(
            ctx_n, hidden, w_query.T, w_down.T, latent_gain.reshape(1, rank), w_key_up, w_value_up, w_out
        )
    square = chips == 4 and rows % 16 == 0 and width % 256 == 0
    pieces = 6 if width % 768 == 0 else 2
    f32, bf16, dma = jnp.float32, jnp.bfloat16, pltpu.SemaphoreType.DMA
    return pl.pallas_call(
        functools.partial(general_kernel, ctx_n, chips, square, steps, pieces),
        out_shape=jax.ShapeDtypeStruct((rows, width), f32),
        in_specs=[pl.BlockSpec(memory_space=pltpu.HBM)] * 7,
        out_specs=pl.BlockSpec(memory_space=pltpu.VMEM),
        scratch_shapes=[
            pltpu.VMEM((per_core, width), f32),
            pltpu.VMEM(w_down.shape[::-1], f32),
            pltpu.VMEM((CORES,) + w_query.shape[::-1], f32),
            pltpu.VMEM((1, rank), f32),
            pltpu.VMEM((CORES, rank, nope), f32),
            pltpu.VMEM((CORES, rank, vdim), f32),
            pltpu.VMEM((CORES, vdim, width), f32),
            pltpu.VMEM((ctx_n * block, lanes), f32),
            pltpu.VMEM((block, lanes), bf16),
            pltpu.VMEM((block, lanes), bf16),
            pltpu.VMEM((block, 1), f32),
            pltpu.VMEM((block, 1), f32),
            pltpu.VMEM((block, rank), f32),
            pltpu.VMEM((per_core, width), f32),
            pltpu.VMEM((per_core, width), f32),
            dma((2 + steps + 4,)),
            dma((4,)), dma((4,)),
            dma((chips, 2)), dma((chips, 2)),
            dma((ctx_n,)), dma((ctx_n,)),
            dma((ctx_n, chips, 2)), dma((ctx_n, chips, 2)),
            dma((ctx_n,)), dma((ctx_n,)),
            dma((pieces, chips)), dma((pieces, chips)),
        ],
        compiler_params=pltpu.CompilerParams(
            collective_id=0, has_side_effects=True, vmem_limit_bytes=60 * 1024 * 1024
        ),
    )(hidden, w_query.T, w_down.T, latent_gain.reshape(1, rank), w_key_up, w_value_up, w_out)


def solution(mesh):
    placed = (
        P(("ctx", "head"), None),
        P(None, "head"),
        P(),
        P(),
        P(None, "head"),
        P(None, "head"),
        P("head", None),
    )
    body = functools.partial(on_device, mesh.shape["ctx"], mesh.shape["head"] // CORES)
    return jax.shard_map(
        body, mesh=mesh, in_specs=placed, out_specs=P(("ctx", "head"), None), check_vma=False
    )
```

```python
import functools

import jax
import jax.numpy as jnp
from jax import lax
from jax.experimental import pallas as pl
from jax.experimental.pallas import tpu as pltpu
from jax.sharding import PartitionSpec as P

EPSILON = 1e-06
FLOOR = -1e30
CORES = 2
LANE = 128
FIRST = ((1, 0), (2, 1))
DIRECT = ((1, 0), (2, 1), (1, 1), (2, 0))
REST = ((1, 1), (2, 0), (3, 0), (3, 1))
MESH = pl.DeviceIdType.MESH
NN = (((1,), (0,)), ((), ()))
NT = (((1,), (1,)), ((), ()))


def halves(value):
    high = value.astype(jnp.bfloat16)
    return high, (value - high.astype(jnp.float32)).astype(jnp.bfloat16)


def product(left, right, dims=NN):
    (lh, ll), (rh, rl) = left, right
    dot = functools.partial(lax.dot_general, dimension_numbers=dims, preferred_element_type=jnp.float32)
    return dot(lh, rh) + (dot(ll, rh) + dot(lh, rl))


def stacked(left, right, dims=NN):
    (lh, ll), (rh, rl) = left, right
    dot = functools.partial(lax.dot_general, dimension_numbers=dims, preferred_element_type=jnp.float32)
    both = dot(jnp.concatenate([lh, ll], axis=0), rh)
    size = lh.shape[0]
    return both[:size] + (both[size:] + dot(lh, rl))


def general_kernel(
    ctx_n, chips, square, steps, pieces,
    hidden, w_query, w_down, gain, w_key, w_value, w_out, out,
    hid, wd, wq, gn, wk, wv, wo, lat, qh, ql, top, total, acc, part, landed,
    load_sem, swap_send, swap_recv, hid_send, hid_recv, col_send, col_recv,
    row_send, row_recv, twin_send, twin_recv, sum_send, sum_recv,
):
    rows, width = hidden.shape
    parts = 2 if square else 1
    rank = gn.shape[1]
    tail = wd.shape[0] - rank
    nope = wk.shape[2]
    per_core = chips * rows
    block = CORES * per_core
    lanes = lat.shape[1]
    ctx = lax.axis_index("ctx")
    head = lax.axis_index("head")
    chip, core = head // CORES, head % CORES
    twin = chip * CORES + (1 - core)

    def chip_at(offset):
        return lax.rem(chip + offset, chips)

    def to(o):
        if not square:
            return chip_at(o)
        return [chip, chip + 1 - 2 * lax.rem(chip, 2), lax.rem(chip + 2, 4), 3 - chip][o]

    def origin(o):
        return to(o) if square else chip_at(chips - o)

    def local(src, dst, sem):
        return pltpu.make_async_copy(src, dst, load_sem.at[sem])

    def remote(src, dst, send, recv, c, h):
        return pltpu.make_async_remote_copy(
            src_ref=src, dst_ref=dst, send_sem=send, recv_sem=recv,
            device_id={"ctx": c, "head": h}, device_id_type=MESH,
        )

    def at_rows(start, size):
        return pl.ds(pl.multiple_of(start, 8), size)

    my_hid = hid.at[at_rows(chip * rows, rows)]
    depth = width // steps
    loads = [local(hidden, my_hid, 0), local(gain, gn, 1)]
    for s in range(steps):
        span = pl.ds(s * depth, depth)
        loads.append(local(w_down.at[:, span], wd.at[:, span], 2 + s))
    pairs = [(w_query, wq), (w_key, wk), (w_value, wv), (w_out, wo)]
    own = [local(src, dst.at[core], 2 + steps + i) for i, (src, dst) in enumerate(pairs)]
    for copy in loads:
        copy.start()

    barrier = pltpu.get_barrier_semaphore()
    for o in range(1, chips):
        pl.semaphore_signal(barrier, inc=1, device_id={"ctx": ctx, "head": chip_at(o) * CORES + core}, device_id_type=MESH)
    pl.semaphore_signal(barrier, inc=1, device_id={"ctx": ctx, "head": twin}, device_id_type=MESH)
    for o in range(1, ctx_n):
        pl.semaphore_signal(barrier, inc=1, device_id={"ctx": lax.rem(ctx + o, ctx_n), "head": head}, device_id_type=MESH)
    pl.semaphore_wait(barrier, chips - 1 + 1 + ctx_n - 1)

    def share(source, spot, send, recv):
        def start_of(o, h):
            target = to(o)
            return remote(source(h), spot(chip, h), send(o, h), recv(o, h), ctx, target * CORES + core)

        def seen(o, h):
            place_of = spot(origin(o), h)
            return remote(place_of, place_of, send(o, h), recv(o, h), ctx, twin)

        def passed(h):
            place_of = spot(to(1 + h), h)
            return remote(place_of, place_of, send(3, h), recv(3, h), ctx, to(2 - h) * CORES + core)

        direct = [(1, 0), (2, 1), (1, 1), (2, 0)] if square else [(o, 0) for o in range(1, chips)]

        def start():
            for o, h in direct:
                start_of(o, h).start()

        def relay():
            if square:
                for h in range(2):
                    seen(1 + h, h).wait_recv()
                    passed(h).start()

        def finish():
            for o, h in [(1, 1), (2, 0), (3, 0), (3, 1)] if square else direct:
                seen(o, h).wait_recv()

        def drain():
            for o, h in direct:
                start_of(o, h).wait_send()
            if square:
                for h in range(2):
                    passed(h).wait_send()

        return start, relay, finish, drain

    half = width // parts

    def hid_half(h):
        return pl.ds(h * half, half)

    hid_start, hid_relay, hid_finish, hid_drain = share(
        lambda h: hidden.at[:, hid_half(h)],
        lambda k, h: hid.at[at_rows(k * rows, rows), hid_half(h)],
        lambda o, h: hid_send.at[o, h],
        lambda o, h: hid_recv.at[o, h],
    )
    hid_start()
    swaps = [remote(src, dst.at[core], swap_send.at[i], swap_recv.at[i], ctx, twin) for i, (src, dst) in enumerate(pairs)]
    for copy in own:
        copy.start()
    for copy in swaps:
        copy.start()

    loads[0].wait()
    loads[1].wait()
    down = jnp.zeros((rows, rank + tail), jnp.float32)
    for s in range(steps):
        loads[2 + s].wait()
        span = pl.ds(s * depth, depth)
        down += product(halves(my_hid[:, span]), halves(wd[:, span]), NT)
    raw = down[:, :rank]
    meansq = jnp.mean(raw * raw, axis=-1, keepdims=True)
    blank = jnp.zeros((rows, lanes - rank - tail), jnp.float32)

    def place(b, p, k):
        return ((b * CORES + p) * chips + k) * rows

    mine = at_rows(place(ctx, core, chip), rows)
    lat[mine, :rank] = raw * lax.rsqrt(meansq + EPSILON) * gn[...]
    lat[mine, rank:] = jnp.concatenate([down[:, rank:], blank], axis=1)

    def col_copy(b):
        spot = lat.at[at_rows(place(b, core, chip), rows)]
        return remote(spot, spot, col_send.at[b], col_recv.at[b], jnp.minimum(ctx + 1, ctx_n - 1), head)

    def latents(b):
        def spot(k, h):
            return lat.at[at_rows(place(b, core, k) + h * (rows // parts), rows // parts)]

        return share(
            lambda h: spot(chip, h), spot, lambda o, h: row_send.at[b, o, h], lambda o, h: row_recv.at[b, o, h]
        )

    def twin_copy(b, p):
        spot = lat.at[at_rows(place(b, p, 0), per_core)]
        return remote(spot, spot, twin_send.at[b], twin_recv.at[b], ctx, twin)

    def spread(b):
        @pl.when(ctx + 1 < ctx_n)
        def _():
            col_copy(b).start()

        latents(b)[0]()

    def gather_rows(b):
        latents(b)[2]()
        twin_copy(b, core).start()

    spread(ctx)
    hid_relay()
    for d in range(1, ctx_n):
        @pl.when(d <= ctx)
        def _():
            col_copy(ctx - d).wait_recv()
            spread(ctx - d)

    latents(ctx)[1]()

    hid_finish()
    for i in range(2):
        own[i].wait()
        swaps[i].wait()
    scale = wq.shape[1] ** (-0.5)
    pad = jnp.zeros((per_core, lanes - rank - tail), jnp.float32)
    query = [jnp.zeros((per_core, wq.shape[1]), jnp.float32) for _ in range(CORES)]
    for s in range(steps):
        span = pl.ds(s * depth, depth)
        piece = halves(hid[:, span])
        for p in range(CORES):
            query[p] += product(piece, halves(wq[p, :, span]), NT)
    for p in range(CORES):
        wide = product(halves(query[p][:, :nope] * scale), halves(wk[p]), NT)
        span = pl.ds(p * per_core, per_core)
        qh[span, :rank], ql[span, :rank] = halves(wide)
        qh[span, rank:], ql[span, rank:] = halves(jnp.concatenate([query[p][:, nope:] * scale, pad], axis=1))

    def spots(index, parity):
        inner = lax.rem(index, per_core)
        return (lax.div(inner, rows) * CORES + parity) * rows + lax.rem(inner, rows)

    def attend(b, first):
        keys = halves(lat[at_rows(place(b, 0, 0), block), :])
        scores = product((qh[...], ql[...]), keys, NT)
        if first:
            line = lax.broadcasted_iota(jnp.int32, (block, 1), 0)
            column = lax.broadcasted_iota(jnp.int32, (1, block), 1)
            causal = spots(line, core) >= spots(column, lax.div(column, per_core))
            scores = jnp.where(causal, scores, FLOOR)
            peak = jnp.max(scores, axis=1, keepdims=True)
        else:
            peak = jnp.maximum(top[...], jnp.max(scores, axis=1, keepdims=True))
        weights = jnp.exp(scores - peak)
        if first:
            weights = jnp.where(causal, weights, 0.0)
        mixed = product(halves(weights), (keys[0][:, :rank], keys[1][:, :rank]))
        added = jnp.sum(weights, axis=1, keepdims=True)
        if first:
            total[...] = added
            acc[...] = mixed
        else:
            fade = jnp.exp(top[...] - peak)
            total[...] = total[...] * fade + added
            acc[...] = acc[...] * fade + mixed
        top[...] = peak

    def relay_at(d):
        if d < ctx_n:
            @pl.when(d <= ctx)
            def _():
                latents(ctx - d)[1]()

    relay_at(1)
    gather_rows(ctx)
    twin_copy(ctx, 1 - core).wait_recv()
    attend(ctx, True)
    for d in range(1, ctx_n):
        @pl.when(d <= ctx)
        def _():
            relay_at(d + 1)
            gather_rows(ctx - d)
            twin_copy(ctx - d, 1 - core).wait_recv()
            attend(ctx - d, False)

    for i in range(2, 4):
        own[i].wait()
        swaps[i].wait()
    heads = []
    for p in range(CORES):
        span = pl.ds(p * per_core, per_core)
        heads.append(product(halves(acc[span, :] / total[span, :]), halves(wv[p])))
    attended = halves(jnp.concatenate(heads, axis=1))
    columns = width // pieces

    def cut(ref, k, t):
        return ref.at[at_rows(k * rows, rows), pl.ds(t * columns, columns)]

    def axes_of(t):
        return (1, 2) if t % 2 == 0 else (2, 1)

    def sum_copy(t, j):
        if not square:
            return remote(
                cut(part, chip_at(j), t), cut(landed, chip, t), sum_send.at[t, j], sum_recv.at[t, j],
                ctx, chip_at(j) * CORES + core,
            )
        first, second = axes_of(t)
        src = [to(3), to(first), to(second)][j]
        dst = [to(3), to(first), to(3)][j]
        target = [to(first), to(first), to(second)][j]
        return remote(cut(part, src, t), cut(landed, dst, t), sum_send.at[t, j], sum_recv.at[t, j], ctx, target * CORES + core)

    def second_stage(t):
        sum_copy(t, 0).wait_recv()
        keep = to(axes_of(t)[1])
        cut(part, keep, t)[...] = cut(part, keep, t)[...] + cut(landed, keep, t)[...]
        sum_copy(t, 2).start()

    kinds = (0, 1) if square else tuple(range(1, chips))
    for t in range(pieces):
        span = pl.ds(t * columns, columns)
        weight = jnp.concatenate([wo[p, :, span] for p in range(CORES)], axis=0)
        part[:, span] = product(attended, halves(weight))
        for j in kinds:
            sum_copy(t, j).start()
        if square and t >= 2:
            second_stage(t - 2)
    if square:
        for t in range(max(pieces - 2, 0), pieces):
            second_stage(t)
    for t in range(pieces):
        result = cut(part, chip, t)[...]
        if square:
            for j in (1, 2):
                sum_copy(t, j).wait_recv()
            result += cut(landed, chip, t)[...] + cut(landed, to(axes_of(t)[0]), t)[...]
        else:
            for j in kinds:
                sum_copy(t, j).wait_recv()
                result += cut(landed, origin(j), t)[...]
        out[:, pl.ds(t * columns, columns)] = result

    hid_drain()
    for t in range(pieces):
        for j in kinds + ((2,) if square else ()):
            sum_copy(t, j).wait_send()
    for d in range(ctx_n):
        @pl.when(d <= ctx)
        def _():
            @pl.when(ctx + 1 < ctx_n)
            def _():
                col_copy(ctx - d).wait_send()

            latents(ctx - d)[3]()
            twin_copy(ctx - d, core).wait_send()


def square_kernel(
    ctx_n, chunks, cuts,
    hidden, w_query, w_down, gain, w_key, w_value, w_out, out,
    mine, hid, wd, gn, wq, wqh, wql, wk, wv, wo, woh, wol, lat, kh, kl, qh, ql, total, acc,
    part, mid, fwd, near, last,
    load_sem, swap_send, swap_recv, hid_send, hid_recv, far_sem, z_send, z_recv,
    lat_send, lat_recv, twin_recv, sum_send, sum_recv,
):
    rows, width = hidden.shape
    rank = gn.shape[1]
    tail = wd.shape[0] - rank
    nope, vdim = wk.shape[2], wv.shape[2]
    key_width = wq.shape[1]
    lanes = kh.shape[1]
    r = rows // chunks
    group = 4 * r
    many = CORES * group
    block = CORES * 4 * rows
    hr = rows // 2
    tiles = rank // LANE
    piece = hr * tiles + hr // 2
    slot = 2 * piece
    half = width // 2
    steps = 3 if width % 384 == 0 else 1
    depth = width // steps
    ctx = lax.axis_index("ctx")
    head = lax.axis_index("head")
    chip, core = head // CORES, head % CORES
    twin = chip * CORES + (1 - core)
    xbit, ybit = lax.rem(chip, 2), lax.div(chip, 2)
    side = [None, (2 * ybit + 1 - xbit) * CORES + core, (2 * (1 - ybit) + xbit) * CORES + core]

    def local(src, dst, sem):
        return pltpu.make_async_copy(src, dst, sem)

    def remote(src, dst, send, recv, h, c=ctx):
        return pltpu.make_async_remote_copy(
            src_ref=src, dst_ref=dst, send_sem=send, recv_sem=recv,
            device_id={"ctx": c, "head": h}, device_id_type=MESH,
        )

    def signal(sem, c, h):
        pl.semaphore_signal(sem, inc=1, device_id={"ctx": c, "head": h}, device_id_type=MESH)

    def when(condition, *actions):
        @pl.when(condition)
        def _():
            for action in actions:
                action()

    def spot(q, s, h):
        return hid.at[pl.ds((q * 4 + s) * r, r), pl.ds(h * half, half)]

    def hid_direct(q, order):
        for a, h in order:
            remote(
                hidden.at[pl.ds(q * r, r), pl.ds(h * half, half)], spot(q, a, h),
                hid_send.at[0], hid_recv.at[q, h if (a, h) in FIRST else 2], side[a],
            ).start()

    def hid_relay(q):
        for h in range(2):
            landed = spot(q, 1 + h, h)
            remote(landed, landed, hid_send.at[0], hid_recv.at[q, h], twin).wait_recv()
            remote(landed, spot(q, 3, h), hid_send.at[0], hid_recv.at[q, 2], side[2 - h]).start()

    def hid_finish(q):
        landed = hid.at[pl.ds((q * 4 + 1) * r, 2 * r)]
        remote(landed, landed, hid_send.at[0], hid_recv.at[q, 2], twin).wait_recv()

    def lat_at(d, p, s, h=0, size=piece):
        return lat.at[pl.ds(((d * CORES + p) * 4 + s) * slot + h * piece, size)]

    def lat_twin(d, s, count):
        size = count * slot
        remote(lat_at(d, 0, s, 0, size), lat_at(d, 1, s, 0, size), lat_send.at[d], twin_recv.at[0], twin).start()

    def z_copy(d, s, h, size):
        c = jnp.minimum(ctx + d, ctx_n - 1)
        return remote(lat_at(0, 0, s, h, size), lat_at(d, 0, s, h, size), z_send.at[d - 1], z_recv.at[d - 1], head, c)

    def z_wait(d):
        landed = lat_at(d, 0, 0, 0, 4 * slot if d == 1 else slot)
        remote(landed, landed, z_send.at[d - 1], z_recv.at[d - 1], head).wait_recv()

    def lat_direct(d, order):
        for a, h in order:
            remote(
                lat_at(d, 0, 0, h), lat_at(d, 0, a, h), lat_send.at[d],
                lat_recv.at[max(d - 1, 0), h if (a, h) in FIRST else 2], side[a],
            ).start()

    def lat_fetch(d):
        z_wait(d)
        lat_direct(d, FIRST)
        lat_twin(d, 0, 1)

    def lat_relay(d):
        for h in range(2):
            landed = lat_at(d, 0, 1 + h, h)
            remote(landed, landed, lat_send.at[d], lat_recv.at[max(d - 1, 0), h], twin).wait_recv()
            remote(landed, lat_at(d, 0, 3, h), lat_send.at[d], lat_recv.at[max(d - 1, 0), 2], side[2 - h]).start()

    def lat_finish(d):
        landed = lat_at(d, 0, 1, 0, 2 * slot)
        remote(landed, landed, lat_send.at[d], lat_recv.at[max(d - 1, 0), 2], twin).wait_recv()
        lat_twin(d, 1, 3)
    def z_begin():
        z_copy(1, 0, 0, slot).start()
        z_copy(1, 1, 0, piece).start()
        z_copy(1, 2, 1, piece).start()

    def z_end():
        z_copy(1, 1, 1, 2 * piece).start()
        z_copy(1, 3, 0, slot).start()

    loads = [local(hidden, mine, load_sem.at[0]), local(gain, gn, load_sem.at[1])]
    for i in range(steps):
        span = pl.ds(i * depth, depth)
        loads.append(local(w_down.at[:, span], wd.at[:, span], load_sem.at[2 + i]))
    pairs = [(w_query, wq), (w_key, wk), (w_value, wv), (w_out, wo)]
    lots = (0, 1, 1, 2)
    own = [local(src, dst.at[0], load_sem.at[2 + steps + lot]) for (src, dst), lot in zip(pairs, lots)]
    for q in range(chunks):
        own.append(local(hidden.at[pl.ds(q * r, r)], hid.at[pl.ds(q * group, r)], load_sem.at[5 + steps]))
    for copy in loads:
        copy.start()

    barrier = pltpu.get_barrier_semaphore()
    for h in (twin, side[1], side[2]):
        signal(barrier, ctx, h)
    when(ctx > 0, lambda: signal(barrier, ctx - 1, head))
    when(ctx + 1 < ctx_n, lambda: signal(barrier, ctx + 1, head))
    pl.semaphore_wait(barrier, 3 + jnp.minimum(ctx, 1) + jnp.minimum(ctx_n - 1 - ctx, 1))

    hid_direct(0, FIRST)
    swaps = [
        remote(src, dst.at[1], swap_send.at[lot], swap_recv.at[lot], twin) for (src, dst), lot in zip(pairs, lots)
    ]
    for copy in own:
        copy.start()
    for copy in swaps:
        copy.start()

    if ctx_n > 2:
        when(jnp.logical_and(ctx >= 1, ctx + 2 <= ctx_n), lambda: signal(far_sem.at[0], ctx - 1, head))

    loads[0].wait()
    loads[1].wait()
    down = jnp.zeros((rows, rank + tail), jnp.float32)
    for i in range(steps):
        loads[2 + i].wait()
        span = pl.ds(i * depth, depth)
        down += stacked(halves(mine[:, span]), halves(wd[:, span]), NT)
    raw = down[:, :rank]
    meansq = jnp.mean(raw * raw, axis=-1, keepdims=True)
    latent = raw * lax.rsqrt(meansq + EPSILON) * gn[...]
    shared = jnp.concatenate([down[:hr, rank:], down[hr:, rank:]], axis=1)
    for h in range(2):
        for j in range(tiles):
            lat_at(0, 0, 0, h)[pl.ds(j * hr, hr), :] = latent[h * hr : (h + 1) * hr, j * LANE : (j + 1) * LANE]
        lat_at(0, 0, 0, h)[pl.ds(tiles * hr, hr // 2), :] = shared[h * hr // 2 : (h + 1) * hr // 2]

    for d in range(2, ctx_n):
        when(ctx + d < ctx_n, lambda d=d: pl.semaphore_wait(far_sem.at[d - 2], 1))
        if d + 1 < ctx_n:
            when(
                jnp.logical_and(ctx >= 1, ctx + d < ctx_n),
                lambda d=d: signal(far_sem.at[d - 1], ctx - 1, head),
            )
    for d in range(2, ctx_n):
        when(ctx + d < ctx_n, lambda d=d: z_copy(d, 0, 0, slot).start())
    lat_direct(0, DIRECT)
    hid_direct(0, REST[:2])
    lat_twin(0, 0, 1)

    def split_query(p):
        wqh[p], wql[p] = halves(wq[p])

    def kept(lot):
        whole = {0: wq.at[0], 1: wk, 2: wo.at[0]}[lot]
        local(whole, whole, load_sem.at[2 + steps + lot]).wait()
        remote(whole, whole, swap_send.at[lot], swap_recv.at[lot], twin).wait()

    hid_relay(0)
    own[0].wait()
    split_query(0)
    lat_relay(0)
    if ctx_n > 1:
        when(ctx + 1 < ctx_n, z_begin)
    swaps[0].wait()
    split_query(1)
    for d in range(2, ctx_n):
        when(ctx >= d, lambda d=d: lat_fetch(d))
    for d in range(2, ctx_n):
        when(ctx >= d, lambda d=d: lat_direct(d, REST[:2]))
    for q in range(1, chunks):
        when(jnp.logical_or(ctx < 2, core == 0), lambda q=q: hid_direct(q, FIRST))
    kept(1)
    local(mine, mine, load_sem.at[5 + steps]).wait()

    scale = key_width ** (-0.5)
    pad = jnp.zeros((group, lanes - rank - tail), jnp.float32)

    def queries(q):
        hid_finish(q)
        query = [jnp.zeros((group, key_width), jnp.float32) for _ in range(CORES)]
        for i in range(steps):
            span = pl.ds(i * depth, depth)
            given = halves(hid[pl.ds(q * group, group), span])
            for p in range(CORES):
                query[p] += stacked(given, (wqh[p, :, span], wql[p, :, span]), NT)
        for p in range(CORES):
            wide = stacked(halves(query[p][:, :nope] * scale), halves(wk[p]), NT)
            span = pl.ds(q * many + p * group, group)
            qh[span, :rank], ql[span, :rank] = halves(wide)
            rest = jnp.concatenate([query[p][:, nope:] * scale, pad], axis=1)
            qh[span, rank:], ql[span, rank:] = halves(rest)

    def keys(d, p):
        for s in range(4):
            at = d * block + (p * 4 + s) * rows
            packed = jnp.concatenate(
                [lat_at(d, p, s, h)[pl.ds(tiles * hr, hr // 2), :] for h in range(2)], axis=0
            )
            for h in range(2):
                span = pl.ds(at + h * hr, hr)
                for j in range(tiles):
                    lane = pl.ds(j * LANE, LANE)
                    kh[span, lane], kl[span, lane] = halves(lat_at(d, p, s, h)[pl.ds(j * hr, hr), :])
                lane = pl.ds(rank, LANE)
                kh[span, lane], kl[span, lane] = halves(packed if h == 0 else pltpu.roll(packed, tail, 1))

    def lat_ready(count):
        landed = lat.at[pl.ds(0, 4 * count * slot)]
        remote(landed, landed, lat_send.at[0], twin_recv.at[0], twin).wait_recv()
        for d in range(count):
            keys(d, 1)

    def place(s, parity, i):
        sx, sy = lax.rem(s, 2), lax.div(s, 2)
        x, y = lax.rem(xbit + sx, 2), lax.rem(ybit + sy, 2)
        return ((2 * y + x) * CORES + parity) * rows + i

    def causal_of(q, count):
        line = lax.rem(lax.broadcasted_iota(jnp.int32, (many, 1), 0), group)
        column = lax.broadcasted_iota(jnp.int32, (1, count * block), 1)
        there = lax.rem(lax.div(column, 4 * rows), CORES)
        inner = lax.rem(column, 4 * rows)
        asked = place(lax.div(line, r), core, q * r + lax.rem(line, r))
        held = place(lax.div(inner, rows), core + there - 2 * core * there, lax.rem(inner, rows))
        return asked >= jnp.where(column < block, held, -1)

    def attend(q, count, between):
        mine_q = pl.ds(q * many, many)
        those = pl.ds(0, count * block)
        scores = stacked((qh[mine_q, :], ql[mine_q, :]), (kh[those, :], kl[those, :]), NT)
        causal = causal_of(q, count)
        scores = jnp.where(causal, scores, FLOOR)
        weights = jnp.where(causal, jnp.exp(scores - jnp.max(scores, axis=1, keepdims=True)), 0.0)
        between()
        total[mine_q, :] = jnp.sum(weights, axis=1, keepdims=True)
        acc[mine_q, :] = stacked(halves(weights), (kh[those, :rank], kl[those, :rank]))

    def attend_whole(q, between=lambda: None):
        for count in range(1, ctx_n + 1):
            when(ctx + 1 == count, lambda count=count: attend(q, count, between))

    def span_of(q, t):
        low, high = [width // 2 // LANE * i // cuts[q] * LANE for i in (t // 2, t // 2 + 1)]
        return pl.ds(2 * low + t % 2 * (high - low), high - low)

    def axes_of(t):
        return (1, 2) if t % 2 == 0 else (2, 1)

    def sum_copy(q, t, j):
        first, second = axes_of(t)
        span = span_of(q, t)
        here = pl.ds(q * r, r)

        def part_of(s):
            return part.at[pl.ds(q * group + s * r, r), span]

        src, dst, target = [
            (part_of(3), mid.at[here, span], first),
            (part_of(first), near.at[here, span], first),
            (fwd.at[here, span], last.at[here, span], second),
        ][j]
        return remote(src, dst, sum_send.at[0], sum_recv.at[2 * sum(cuts[:q]) + t if j == 0 else 2 * sum(cuts) + q], side[target])

    def project(q, between=lambda: None):
        found = []
        for p in range(CORES):
            span = pl.ds(q * many + p * group, group)
            found.append(stacked(halves(acc[span, :] / total[span, :]), halves(wv[p])))
        attended = halves(jnp.concatenate(found, axis=1))
        for t in range(2 * cuts[q]):
            span = span_of(q, t)
            part[pl.ds(q * group, group), span] = stacked(attended, (woh[:, span], wol[:, span]))
            sum_copy(q, t, 0).start()
        between()
        for t in range(2 * cuts[q]):
            sum_copy(q, t, 1).start()

    def second_stage(q, low, high):
        here = pl.ds(q * r, r)
        for t in range(low, high):
            span = span_of(q, t)
            sum_copy(q, t, 0).wait_recv()
            keep = axes_of(t)[1]
            fwd[here, span] = part[pl.ds(q * group + keep * r, r), span] + mid[here, span]
            sum_copy(q, t, 2).start()

    def collect(q):
        here = pl.ds(q * r, r)
        landed = near.at[pl.ds(0, 2 * r)]
        remote(landed, landed, sum_send.at[0], sum_recv.at[2 * sum(cuts) + q], twin).wait_recv()
        out[here, :] = part[pl.ds(q * group, r), :] + near[here, :] + last[here, :]

    def split_out():
        kept(2)
        for p in range(CORES):
            span = pl.ds(p * vdim, vdim)
            woh[span, :], wol[span, :] = halves(wo[p])

    def z_join():
        z_wait(1)
        lat_twin(1, 0, 4)

    def begin(d):
        when(ctx >= d, lambda: lat_relay(d))

    def done(d):
        lat_finish(d)
        keys(d, 0)

    def z_done():
        z_join()
        keys(1, 0)

    def sent_on():
        done(0)
        if ctx_n > 1:
            when(ctx + 1 < ctx_n, z_end)

    when(ctx < 1, sent_on)
    queries(0)
    when(ctx >= 1, sent_on)
    for d in range(2, ctx_n):
        begin(d)
    for q in range(1, chunks):
        when(jnp.logical_or(ctx < 2, core == 0), lambda q=q: hid_direct(q, REST[:2]))
    split_out()
    if ctx_n > 2:
        when(ctx >= 2, lambda: done(2))
    if ctx_n > 1:
        when(ctx >= 1, z_done)
    for d in range(3, ctx_n):
        when(ctx >= d, lambda d=d: done(d))
    for q in range(1, chunks):
        when(jnp.logical_and(ctx >= 2, core == 1), lambda q=q: hid_direct(q, FIRST + REST[:2]))
    for q in range(1, chunks):
        hid_relay(q)
    for count in range(1, ctx_n + 1):
        when(ctx + 1 == count, lambda count=count: lat_ready(count))
    attend_whole(0)
    project(0)
    for q in range(1, chunks):
        queries(q)
        attend_whole(q, lambda: second_stage(q - 1, 0, 3))
        second_stage(q - 1, 3, 2 * cuts[q - 1])
        project(q)
        second_stage(q, 0, 2 * cuts[q])
        collect(q - 1)
    collect(chunks - 1)

    sent = hid.at[pl.ds(0, 3 * rows)]
    for sem in (hid_send.at[0], sum_send.at[0]):
        remote(sent, sent, sem, hid_recv.at[0, 0], twin).wait_send()
    for d in range(ctx_n):
        def drain(d=d):
            sent = lat.at[pl.ds(0, (4 if d == 1 else 7) * slot)]
            remote(sent, sent, lat_send.at[d], twin_recv.at[0], twin).wait_send()

        def z_drain(d=d):
            sent = lat.at[pl.ds(0, (4 if d == 1 else 1) * slot)]
            remote(sent, sent, z_send.at[d - 1], z_recv.at[d - 1], head).wait_send()

        when(d <= ctx, drain)
        if d > 0:
            when(ctx + d < ctx_n, z_drain)


def square_call(ctx_n, hidden, w_query, w_down, gain, w_key_up, w_value_up, w_out):
    rows, width = hidden.shape
    rank, nope = w_key_up.shape
    vdim = w_value_up.shape[1]
    f32, bf16, dma = jnp.float32, jnp.bfloat16, pltpu.SemaphoreType.DMA
    chunks = 2
    cuts = (2, 3)
    r = rows // chunks
    block = CORES * 4 * rows
    lanes = rank + LANE
    steps = 3 if width % 384 == 0 else 1
    slot = rows * (rank // LANE) + rows // 2
    query = (CORES,) + w_query.shape
    both = (CORES * vdim, width)
    return pl.pallas_call(
        functools.partial(square_kernel, ctx_n, chunks, cuts),
        out_shape=pltpu.VMEM((rows, width), f32),
        in_specs=[pl.BlockSpec(memory_space=pltpu.HBM)] * 7,
        out_specs=pl.BlockSpec(memory_space=pltpu.VMEM),
        scratch_shapes=[
            pltpu.VMEM((rows, width), f32),
            pltpu.VMEM((4 * rows, width), f32),
            pltpu.VMEM(w_down.shape, f32),
            pltpu.VMEM((1, rank), f32),
            pltpu.VMEM(query, f32), pltpu.VMEM(query, bf16), pltpu.VMEM(query, bf16),
            pltpu.VMEM((CORES, rank, nope), f32),
            pltpu.VMEM((CORES, rank, vdim), f32),
            pltpu.VMEM((CORES, vdim, width), f32), pltpu.VMEM(both, bf16), pltpu.VMEM(both, bf16),
            pltpu.VMEM((ctx_n * CORES * 4 * slot, LANE), f32),
            pltpu.VMEM((ctx_n * block, lanes), bf16), pltpu.VMEM((ctx_n * block, lanes), bf16),
            pltpu.VMEM((block, lanes), bf16), pltpu.VMEM((block, lanes), bf16),
            pltpu.VMEM((block, 1), f32),
            pltpu.VMEM((block, rank), f32),
            pltpu.VMEM((4 * rows, width), f32),
        ] + [pltpu.VMEM((rows, width), f32)] * 4 + [
            dma((6 + steps,)),
            dma((3,)), dma((3,)),
            dma((1,)), dma((chunks, 3)),
            pltpu.SemaphoreType.REGULAR((max(ctx_n - 2, 1),)),
            dma((max(ctx_n - 1, 1),)), dma((max(ctx_n - 1, 1),)),
            dma((ctx_n,)), dma((max(ctx_n - 1, 1), 3)),
            dma((1,)),
            dma((1,)), dma((2 * sum(cuts) + chunks,)),
        ],
        compiler_params=pltpu.CompilerParams(
            collective_id=0, has_side_effects=True, vmem_limit_bytes=60 * 1024 * 1024
        ),
    )(hidden, w_query, w_down, gain, w_key_up, w_value_up, w_out)


def on_device(ctx_n, chips, hidden, w_query, w_down, latent_gain, w_key_up, w_value_up, w_out):
    rows, width = hidden.shape
    rank, nope = w_key_up.shape
    vdim = w_value_up.shape[1]
    per_core = chips * rows
    block = CORES * per_core
    lanes = -(-w_down.shape[1] // 128) * 128
    steps = 3 if width % 384 == 0 else 1
    if chips == 4 and rows % 32 == 0 and width % 768 == 0 and rank % LANE == 0 and 2 * (w_down.shape[1] - rank) == LANE:
        return square_call(
            ctx_n, hidden, w_query.T, w_down.T, latent_gain.reshape(1, rank), w_key_up, w_value_up, w_out
        )
    square = chips == 4 and rows % 16 == 0 and width % 256 == 0
    pieces = 6 if width % 768 == 0 else 2
    f32, bf16, dma = jnp.float32, jnp.bfloat16, pltpu.SemaphoreType.DMA
    return pl.pallas_call(
        functools.partial(general_kernel, ctx_n, chips, square, steps, pieces),
        out_shape=jax.ShapeDtypeStruct((rows, width), f32),
        in_specs=[pl.BlockSpec(memory_space=pltpu.HBM)] * 7,
        out_specs=pl.BlockSpec(memory_space=pltpu.VMEM),
        scratch_shapes=[
            pltpu.VMEM((per_core, width), f32),
            pltpu.VMEM(w_down.shape[::-1], f32),
            pltpu.VMEM((CORES,) + w_query.shape[::-1], f32),
            pltpu.VMEM((1, rank), f32),
            pltpu.VMEM((CORES, rank, nope), f32),
            pltpu.VMEM((CORES, rank, vdim), f32),
            pltpu.VMEM((CORES, vdim, width), f32),
            pltpu.VMEM((ctx_n * block, lanes), f32),
            pltpu.VMEM((block, lanes), bf16),
            pltpu.VMEM((block, lanes), bf16),
            pltpu.VMEM((block, 1), f32),
            pltpu.VMEM((block, 1), f32),
            pltpu.VMEM((block, rank), f32),
            pltpu.VMEM((per_core, width), f32),
            pltpu.VMEM((per_core, width), f32),
            dma((2 + steps + 4,)),
            dma((4,)), dma((4,)),
            dma((chips, 2)), dma((chips, 2)),
            dma((ctx_n,)), dma((ctx_n,)),
            dma((ctx_n, chips, 2)), dma((ctx_n, chips, 2)),
            dma((ctx_n,)), dma((ctx_n,)),
            dma((pieces, chips)), dma((pieces, chips)),
        ],
        compiler_params=pltpu.CompilerParams(
            collective_id=0, has_side_effects=True, vmem_limit_bytes=60 * 1024 * 1024
        ),
    )(hidden, w_query.T, w_down.T, latent_gain.reshape(1, rank), w_key_up, w_value_up, w_out)


def solution(mesh):
    placed = (
        P(("ctx", "head"), None),
        P(None, "head"),
        P(),
        P(),
        P(None, "head"),
        P(None, "head"),
        P("head", None),
    )
    body = functools.partial(on_device, mesh.shape["ctx"], mesh.shape["head"] // CORES)
    return jax.shard_map(
        body, mesh=mesh, in_specs=placed, out_specs=P(("ctx", "head"), None), check_vma=False
    )
```

```python
import functools

import jax
import jax.numpy as jnp
from jax import lax
from jax.experimental import pallas as pl
from jax.experimental.pallas import tpu as pltpu
from jax.sharding import PartitionSpec as P

EPSILON = 1e-06
FLOOR = -1e30
CORES = 2
LANE = 128
FIRST = ((1, 0), (2, 1))
DIRECT = ((1, 0), (2, 1), (1, 1), (2, 0))
REST = ((1, 1), (2, 0), (3, 0), (3, 1))
MESH = pl.DeviceIdType.MESH
NN = (((1,), (0,)), ((), ()))
NT = (((1,), (1,)), ((), ()))


def halves(value):
    high = value.astype(jnp.bfloat16)
    return high, (value - high.astype(jnp.float32)).astype(jnp.bfloat16)


def product(left, right, dims=NN):
    (lh, ll), (rh, rl) = left, right
    dot = functools.partial(lax.dot_general, dimension_numbers=dims, preferred_element_type=jnp.float32)
    return dot(lh, rh) + (dot(ll, rh) + dot(lh, rl))


def stacked(left, right, dims=NN):
    (lh, ll), (rh, rl) = left, right
    dot = functools.partial(lax.dot_general, dimension_numbers=dims, preferred_element_type=jnp.float32)
    both = dot(jnp.concatenate([lh, ll], axis=0), rh)
    size = lh.shape[0]
    return both[:size] + (both[size:] + dot(lh, rl))


def general_kernel(
    ctx_n, chips, square, steps, pieces,
    hidden, w_query, w_down, gain, w_key, w_value, w_out, out,
    hid, wd, wq, gn, wk, wv, wo, lat, qh, ql, top, total, acc, part, landed,
    load_sem, swap_send, swap_recv, hid_send, hid_recv, col_send, col_recv,
    row_send, row_recv, twin_send, twin_recv, sum_send, sum_recv,
):
    rows, width = hidden.shape
    parts = 2 if square else 1
    rank = gn.shape[1]
    tail = wd.shape[0] - rank
    nope = wk.shape[2]
    per_core = chips * rows
    block = CORES * per_core
    lanes = lat.shape[1]
    ctx = lax.axis_index("ctx")
    head = lax.axis_index("head")
    chip, core = head // CORES, head % CORES
    twin = chip * CORES + (1 - core)

    def chip_at(offset):
        return lax.rem(chip + offset, chips)

    def to(o):
        if not square:
            return chip_at(o)
        return [chip, chip + 1 - 2 * lax.rem(chip, 2), lax.rem(chip + 2, 4), 3 - chip][o]

    def origin(o):
        return to(o) if square else chip_at(chips - o)

    def local(src, dst, sem):
        return pltpu.make_async_copy(src, dst, load_sem.at[sem])

    def remote(src, dst, send, recv, c, h):
        return pltpu.make_async_remote_copy(
            src_ref=src, dst_ref=dst, send_sem=send, recv_sem=recv,
            device_id={"ctx": c, "head": h}, device_id_type=MESH,
        )

    def at_rows(start, size):
        return pl.ds(pl.multiple_of(start, 8), size)

    my_hid = hid.at[at_rows(chip * rows, rows)]
    depth = width // steps
    loads = [local(hidden, my_hid, 0), local(gain, gn, 1)]
    for s in range(steps):
        span = pl.ds(s * depth, depth)
        loads.append(local(w_down.at[:, span], wd.at[:, span], 2 + s))
    pairs = [(w_query, wq), (w_key, wk), (w_value, wv), (w_out, wo)]
    own = [local(src, dst.at[core], 2 + steps + i) for i, (src, dst) in enumerate(pairs)]
    for copy in loads:
        copy.start()

    barrier = pltpu.get_barrier_semaphore()
    for o in range(1, chips):
        pl.semaphore_signal(barrier, inc=1, device_id={"ctx": ctx, "head": chip_at(o) * CORES + core}, device_id_type=MESH)
    pl.semaphore_signal(barrier, inc=1, device_id={"ctx": ctx, "head": twin}, device_id_type=MESH)
    for o in range(1, ctx_n):
        pl.semaphore_signal(barrier, inc=1, device_id={"ctx": lax.rem(ctx + o, ctx_n), "head": head}, device_id_type=MESH)
    pl.semaphore_wait(barrier, chips - 1 + 1 + ctx_n - 1)

    def share(source, spot, send, recv):
        def start_of(o, h):
            target = to(o)
            return remote(source(h), spot(chip, h), send(o, h), recv(o, h), ctx, target * CORES + core)

        def seen(o, h):
            place_of = spot(origin(o), h)
            return remote(place_of, place_of, send(o, h), recv(o, h), ctx, twin)

        def passed(h):
            place_of = spot(to(1 + h), h)
            return remote(place_of, place_of, send(3, h), recv(3, h), ctx, to(2 - h) * CORES + core)

        direct = [(1, 0), (2, 1), (1, 1), (2, 0)] if square else [(o, 0) for o in range(1, chips)]

        def start():
            for o, h in direct:
                start_of(o, h).start()

        def relay():
            if square:
                for h in range(2):
                    seen(1 + h, h).wait_recv()
                    passed(h).start()

        def finish():
            for o, h in [(1, 1), (2, 0), (3, 0), (3, 1)] if square else direct:
                seen(o, h).wait_recv()

        def drain():
            for o, h in direct:
                start_of(o, h).wait_send()
            if square:
                for h in range(2):
                    passed(h).wait_send()

        return start, relay, finish, drain

    half = width // parts

    def hid_half(h):
        return pl.ds(h * half, half)

    hid_start, hid_relay, hid_finish, hid_drain = share(
        lambda h: hidden.at[:, hid_half(h)],
        lambda k, h: hid.at[at_rows(k * rows, rows), hid_half(h)],
        lambda o, h: hid_send.at[o, h],
        lambda o, h: hid_recv.at[o, h],
    )
    hid_start()
    swaps = [remote(src, dst.at[core], swap_send.at[i], swap_recv.at[i], ctx, twin) for i, (src, dst) in enumerate(pairs)]
    for copy in own:
        copy.start()
    for copy in swaps:
        copy.start()

    loads[0].wait()
    loads[1].wait()
    down = jnp.zeros((rows, rank + tail), jnp.float32)
    for s in range(steps):
        loads[2 + s].wait()
        span = pl.ds(s * depth, depth)
        down += product(halves(my_hid[:, span]), halves(wd[:, span]), NT)
    raw = down[:, :rank]
    meansq = jnp.mean(raw * raw, axis=-1, keepdims=True)
    blank = jnp.zeros((rows, lanes - rank - tail), jnp.float32)

    def place(b, p, k):
        return ((b * CORES + p) * chips + k) * rows

    mine = at_rows(place(ctx, core, chip), rows)
    lat[mine, :rank] = raw * lax.rsqrt(meansq + EPSILON) * gn[...]
    lat[mine, rank:] = jnp.concatenate([down[:, rank:], blank], axis=1)

    def col_copy(b):
        spot = lat.at[at_rows(place(b, core, chip), rows)]
        return remote(spot, spot, col_send.at[b], col_recv.at[b], jnp.minimum(ctx + 1, ctx_n - 1), head)

    def latents(b):
        def spot(k, h):
            return lat.at[at_rows(place(b, core, k) + h * (rows // parts), rows // parts)]

        return share(
            lambda h: spot(chip, h), spot, lambda o, h: row_send.at[b, o, h], lambda o, h: row_recv.at[b, o, h]
        )

    def twin_copy(b, p):
        spot = lat.at[at_rows(place(b, p, 0), per_core)]
        return remote(spot, spot, twin_send.at[b], twin_recv.at[b], ctx, twin)

    def spread(b):
        @pl.when(ctx + 1 < ctx_n)
        def _():
            col_copy(b).start()

        latents(b)[0]()

    def gather_rows(b):
        latents(b)[2]()
        twin_copy(b, core).start()

    spread(ctx)
    hid_relay()
    for d in range(1, ctx_n):
        @pl.when(d <= ctx)
        def _():
            col_copy(ctx - d).wait_recv()
            spread(ctx - d)

    latents(ctx)[1]()

    hid_finish()
    for i in range(2):
        own[i].wait()
        swaps[i].wait()
    scale = wq.shape[1] ** (-0.5)
    pad = jnp.zeros((per_core, lanes - rank - tail), jnp.float32)
    query = [jnp.zeros((per_core, wq.shape[1]), jnp.float32) for _ in range(CORES)]
    for s in range(steps):
        span = pl.ds(s * depth, depth)
        piece = halves(hid[:, span])
        for p in range(CORES):
            query[p] += product(piece, halves(wq[p, :, span]), NT)
    for p in range(CORES):
        wide = product(halves(query[p][:, :nope] * scale), halves(wk[p]), NT)
        span = pl.ds(p * per_core, per_core)
        qh[span, :rank], ql[span, :rank] = halves(wide)
        qh[span, rank:], ql[span, rank:] = halves(jnp.concatenate([query[p][:, nope:] * scale, pad], axis=1))

    def spots(index, parity):
        inner = lax.rem(index, per_core)
        return (lax.div(inner, rows) * CORES + parity) * rows + lax.rem(inner, rows)

    def attend(b, first):
        keys = halves(lat[at_rows(place(b, 0, 0), block), :])
        scores = product((qh[...], ql[...]), keys, NT)
        if first:
            line = lax.broadcasted_iota(jnp.int32, (block, 1), 0)
            column = lax.broadcasted_iota(jnp.int32, (1, block), 1)
            causal = spots(line, core) >= spots(column, lax.div(column, per_core))
            scores = jnp.where(causal, scores, FLOOR)
            peak = jnp.max(scores, axis=1, keepdims=True)
        else:
            peak = jnp.maximum(top[...], jnp.max(scores, axis=1, keepdims=True))
        weights = jnp.exp(scores - peak)
        if first:
            weights = jnp.where(causal, weights, 0.0)
        mixed = product(halves(weights), (keys[0][:, :rank], keys[1][:, :rank]))
        added = jnp.sum(weights, axis=1, keepdims=True)
        if first:
            total[...] = added
            acc[...] = mixed
        else:
            fade = jnp.exp(top[...] - peak)
            total[...] = total[...] * fade + added
            acc[...] = acc[...] * fade + mixed
        top[...] = peak

    def relay_at(d):
        if d < ctx_n:
            @pl.when(d <= ctx)
            def _():
                latents(ctx - d)[1]()

    relay_at(1)
    gather_rows(ctx)
    twin_copy(ctx, 1 - core).wait_recv()
    attend(ctx, True)
    for d in range(1, ctx_n):
        @pl.when(d <= ctx)
        def _():
            relay_at(d + 1)
            gather_rows(ctx - d)
            twin_copy(ctx - d, 1 - core).wait_recv()
            attend(ctx - d, False)

    for i in range(2, 4):
        own[i].wait()
        swaps[i].wait()
    heads = []
    for p in range(CORES):
        span = pl.ds(p * per_core, per_core)
        heads.append(product(halves(acc[span, :] / total[span, :]), halves(wv[p])))
    attended = halves(jnp.concatenate(heads, axis=1))
    columns = width // pieces

    def cut(ref, k, t):
        return ref.at[at_rows(k * rows, rows), pl.ds(t * columns, columns)]

    def axes_of(t):
        return (1, 2) if t % 2 == 0 else (2, 1)

    def sum_copy(t, j):
        if not square:
            return remote(
                cut(part, chip_at(j), t), cut(landed, chip, t), sum_send.at[t, j], sum_recv.at[t, j],
                ctx, chip_at(j) * CORES + core,
            )
        first, second = axes_of(t)
        src = [to(3), to(first), to(second)][j]
        dst = [to(3), to(first), to(3)][j]
        target = [to(first), to(first), to(second)][j]
        return remote(cut(part, src, t), cut(landed, dst, t), sum_send.at[t, j], sum_recv.at[t, j], ctx, target * CORES + core)

    def second_stage(t):
        sum_copy(t, 0).wait_recv()
        keep = to(axes_of(t)[1])
        cut(part, keep, t)[...] = cut(part, keep, t)[...] + cut(landed, keep, t)[...]
        sum_copy(t, 2).start()

    kinds = (0, 1) if square else tuple(range(1, chips))
    for t in range(pieces):
        span = pl.ds(t * columns, columns)
        weight = jnp.concatenate([wo[p, :, span] for p in range(CORES)], axis=0)
        part[:, span] = product(attended, halves(weight))
        for j in kinds:
            sum_copy(t, j).start()
        if square and t >= 2:
            second_stage(t - 2)
    if square:
        for t in range(max(pieces - 2, 0), pieces):
            second_stage(t)
    for t in range(pieces):
        result = cut(part, chip, t)[...]
        if square:
            for j in (1, 2):
                sum_copy(t, j).wait_recv()
            result += cut(landed, chip, t)[...] + cut(landed, to(axes_of(t)[0]), t)[...]
        else:
            for j in kinds:
                sum_copy(t, j).wait_recv()
                result += cut(landed, origin(j), t)[...]
        out[:, pl.ds(t * columns, columns)] = result

    hid_drain()
    for t in range(pieces):
        for j in kinds + ((2,) if square else ()):
            sum_copy(t, j).wait_send()
    for d in range(ctx_n):
        @pl.when(d <= ctx)
        def _():
            @pl.when(ctx + 1 < ctx_n)
            def _():
                col_copy(ctx - d).wait_send()

            latents(ctx - d)[3]()
            twin_copy(ctx - d, core).wait_send()


def square_kernel(
    ctx_n, chunks, cuts,
    hidden, w_query, w_down, gain, w_key, w_value, w_out, out,
    mine, hid, wd, gn, wq, wqh, wql, wk, wv, wo, woh, wol, lat, kh, kl, qh, ql, total, acc,
    part, mid, fwd, near, last,
    load_sem, swap_send, swap_recv, hid_send, hid_recv, far_sem, z_send, z_recv,
    lat_send, lat_recv, twin_recv, sum_send, sum_recv,
):
    rows, width = hidden.shape
    rank = gn.shape[1]
    tail = wd.shape[0] - rank
    nope, vdim = wk.shape[2], wv.shape[2]
    key_width = wq.shape[1]
    lanes = kh.shape[1]
    r = rows // chunks
    group = 4 * r
    many = CORES * group
    block = CORES * 4 * rows
    hr = rows // 2
    tiles = rank // LANE
    piece = hr * tiles + hr // 2
    slot = 2 * piece
    half = width // 2
    steps = 3 if width % 384 == 0 else 1
    depth = width // steps
    ctx = lax.axis_index("ctx")
    head = lax.axis_index("head")
    chip, core = head // CORES, head % CORES
    twin = chip * CORES + (1 - core)
    xbit, ybit = lax.rem(chip, 2), lax.div(chip, 2)
    side = [None, (2 * ybit + 1 - xbit) * CORES + core, (2 * (1 - ybit) + xbit) * CORES + core]

    def local(src, dst, sem):
        return pltpu.make_async_copy(src, dst, sem)

    def remote(src, dst, send, recv, h, c=ctx):
        return pltpu.make_async_remote_copy(
            src_ref=src, dst_ref=dst, send_sem=send, recv_sem=recv,
            device_id={"ctx": c, "head": h}, device_id_type=MESH,
        )

    def signal(sem, c, h):
        pl.semaphore_signal(sem, inc=1, device_id={"ctx": c, "head": h}, device_id_type=MESH)

    def when(condition, *actions):
        @pl.when(condition)
        def _():
            for action in actions:
                action()

    def spot(q, s, h):
        return hid.at[pl.ds((q * 4 + s) * r, r), pl.ds(h * half, half)]

    def hid_direct(q, order):
        for a, h in order:
            remote(
                hidden.at[pl.ds(q * r, r), pl.ds(h * half, half)], spot(q, a, h),
                hid_send.at[0], hid_recv.at[q, h if (a, h) in FIRST else 2], side[a],
            ).start()

    def hid_relay(q):
        for h in range(2):
            landed = spot(q, 1 + h, h)
            remote(landed, landed, hid_send.at[0], hid_recv.at[q, h], twin).wait_recv()
            remote(landed, spot(q, 3, h), hid_send.at[0], hid_recv.at[q, 2], side[2 - h]).start()

    def hid_finish(q):
        landed = hid.at[pl.ds((q * 4 + 1) * r, 2 * r)]
        remote(landed, landed, hid_send.at[0], hid_recv.at[q, 2], twin).wait_recv()

    def lat_at(d, p, s, h=0, size=piece):
        return lat.at[pl.ds(((d * CORES + p) * 4 + s) * slot + h * piece, size)]

    def lat_twin(d, s, count):
        size = count * slot
        remote(lat_at(d, 0, s, 0, size), lat_at(d, 1, s, 0, size), lat_send.at[0], twin_recv.at[0], twin).start()

    def z_copy(d, s, h, size):
        c = jnp.minimum(ctx + d, ctx_n - 1)
        return remote(lat_at(0, 0, s, h, size), lat_at(d, 0, s, h, size), z_send.at[0], z_recv.at[d - 1], head, c)

    def z_wait(d):
        landed = lat_at(d, 0, 0, 0, 4 * slot if d == 1 else slot)
        remote(landed, landed, z_send.at[0], z_recv.at[d - 1], head).wait_recv()

    def lat_direct(d, order):
        for a, h in order:
            remote(
                lat_at(d, 0, 0, h), lat_at(d, 0, a, h), lat_send.at[0],
                lat_recv.at[max(d - 1, 0), h if (a, h) in FIRST else 2], side[a],
            ).start()

    def lat_fetch(d):
        z_wait(d)
        lat_direct(d, FIRST)
        lat_twin(d, 0, 1)

    def lat_relay(d):
        for h in range(2):
            landed = lat_at(d, 0, 1 + h, h)
            remote(landed, landed, lat_send.at[0], lat_recv.at[max(d - 1, 0), h], twin).wait_recv()
            remote(landed, lat_at(d, 0, 3, h), lat_send.at[0], lat_recv.at[max(d - 1, 0), 2], side[2 - h]).start()

    def lat_finish(d):
        landed = lat_at(d, 0, 1, 0, 2 * slot)
        remote(landed, landed, lat_send.at[0], lat_recv.at[max(d - 1, 0), 2], twin).wait_recv()
        lat_twin(d, 1, 3)
    def z_begin():
        z_copy(1, 0, 0, slot).start()
        z_copy(1, 1, 0, piece).start()
        z_copy(1, 2, 1, piece).start()

    def z_end():
        z_copy(1, 1, 1, 2 * piece).start()
        z_copy(1, 3, 0, slot).start()

    loads = [local(hidden, mine, load_sem.at[0]), local(gain, gn, load_sem.at[1])]
    for i in range(steps):
        span = pl.ds(i * depth, depth)
        loads.append(local(w_down.at[:, span], wd.at[:, span], load_sem.at[2 + i]))
    pairs = [(w_query, wq), (w_key, wk), (w_value, wv), (w_out, wo)]
    lots = (0, 1, 1, 2)
    own = [local(src, dst.at[0], load_sem.at[2 + steps + lot]) for (src, dst), lot in zip(pairs, lots)]
    for q in range(chunks):
        own.append(local(hidden.at[pl.ds(q * r, r)], hid.at[pl.ds(q * group, r)], load_sem.at[5 + steps]))
    for copy in loads:
        copy.start()

    barrier = pltpu.get_barrier_semaphore()
    for h in (twin, side[1], side[2]):
        signal(barrier, ctx, h)
    when(ctx > 0, lambda: signal(barrier, ctx - 1, head))
    when(ctx + 1 < ctx_n, lambda: signal(barrier, ctx + 1, head))
    pl.semaphore_wait(barrier, 3 + jnp.minimum(ctx, 1) + jnp.minimum(ctx_n - 1 - ctx, 1))

    hid_direct(0, FIRST)
    swaps = [
        remote(src, dst.at[1], swap_send.at[lot], swap_recv.at[lot], twin) for (src, dst), lot in zip(pairs, lots)
    ]
    for copy in own:
        copy.start()
    for copy in swaps:
        copy.start()

    if ctx_n > 2:
        when(jnp.logical_and(ctx >= 1, ctx + 2 <= ctx_n), lambda: signal(far_sem.at[0], ctx - 1, head))

    loads[0].wait()
    loads[1].wait()
    down = jnp.zeros((rows, rank + tail), jnp.float32)
    for i in range(steps):
        loads[2 + i].wait()
        span = pl.ds(i * depth, depth)
        down += stacked(halves(mine[:, span]), halves(wd[:, span]), NT)
    raw = down[:, :rank]
    meansq = jnp.mean(raw * raw, axis=-1, keepdims=True)
    latent = raw * lax.rsqrt(meansq + EPSILON) * gn[...]
    shared = jnp.concatenate([down[:hr, rank:], down[hr:, rank:]], axis=1)
    for h in range(2):
        for j in range(tiles):
            lat_at(0, 0, 0, h)[pl.ds(j * hr, hr), :] = latent[h * hr : (h + 1) * hr, j * LANE : (j + 1) * LANE]
        lat_at(0, 0, 0, h)[pl.ds(tiles * hr, hr // 2), :] = shared[h * hr // 2 : (h + 1) * hr // 2]

    for d in range(2, ctx_n):
        when(ctx + d < ctx_n, lambda d=d: pl.semaphore_wait(far_sem.at[d - 2], 1))
        if d + 1 < ctx_n:
            when(
                jnp.logical_and(ctx >= 1, ctx + d < ctx_n),
                lambda d=d: signal(far_sem.at[d - 1], ctx - 1, head),
            )
    for d in range(2, ctx_n):
        when(ctx + d < ctx_n, lambda d=d: z_copy(d, 0, 0, slot).start())
    lat_direct(0, DIRECT)
    hid_direct(0, REST[:2])
    lat_twin(0, 0, 1)

    def split_query(p):
        wqh[p], wql[p] = halves(wq[p])

    def kept(lot):
        whole = {0: wq.at[0], 1: wk, 2: wo.at[0]}[lot]
        local(whole, whole, load_sem.at[2 + steps + lot]).wait()
        remote(whole, whole, swap_send.at[lot], swap_recv.at[lot], twin).wait()

    hid_relay(0)
    own[0].wait()
    split_query(0)
    lat_relay(0)
    if ctx_n > 1:
        when(ctx + 1 < ctx_n, z_begin)
    swaps[0].wait()
    split_query(1)
    for d in range(2, ctx_n):
        when(ctx >= d, lambda d=d: lat_fetch(d))
    for d in range(2, ctx_n):
        when(ctx >= d, lambda d=d: lat_direct(d, REST[:2]))
    for q in range(1, chunks):
        when(jnp.logical_or(ctx < 2, core == 0), lambda q=q: hid_direct(q, FIRST))
    kept(1)
    local(mine, mine, load_sem.at[5 + steps]).wait()

    scale = key_width ** (-0.5)
    pad = jnp.zeros((group, lanes - rank - tail), jnp.float32)

    def queries(q):
        hid_finish(q)
        query = [jnp.zeros((group, key_width), jnp.float32) for _ in range(CORES)]
        for i in range(steps):
            span = pl.ds(i * depth, depth)
            given = halves(hid[pl.ds(q * group, group), span])
            for p in range(CORES):
                query[p] += stacked(given, (wqh[p, :, span], wql[p, :, span]), NT)
        for p in range(CORES):
            wide = stacked(halves(query[p][:, :nope] * scale), halves(wk[p]), NT)
            span = pl.ds(q * many + p * group, group)
            qh[span, :rank], ql[span, :rank] = halves(wide)
            rest = jnp.concatenate([query[p][:, nope:] * scale, pad], axis=1)
            qh[span, rank:], ql[span, rank:] = halves(rest)

    def keys(d, p):
        for s in range(4):
            at = d * block + (p * 4 + s) * rows
            packed = jnp.concatenate(
                [lat_at(d, p, s, h)[pl.ds(tiles * hr, hr // 2), :] for h in range(2)], axis=0
            )
            for h in range(2):
                span = pl.ds(at + h * hr, hr)
                for j in range(tiles):
                    lane = pl.ds(j * LANE, LANE)
                    kh[span, lane], kl[span, lane] = halves(lat_at(d, p, s, h)[pl.ds(j * hr, hr), :])
                lane = pl.ds(rank, LANE)
                kh[span, lane], kl[span, lane] = halves(packed if h == 0 else pltpu.roll(packed, tail, 1))

    def lat_ready(count):
        landed = lat.at[pl.ds(0, 4 * count * slot)]
        remote(landed, landed, lat_send.at[0], twin_recv.at[0], twin).wait_recv()
        for d in range(count):
            keys(d, 1)

    def place(s, parity, i):
        sx, sy = lax.rem(s, 2), lax.div(s, 2)
        x, y = lax.rem(xbit + sx, 2), lax.rem(ybit + sy, 2)
        return ((2 * y + x) * CORES + parity) * rows + i

    def causal_of(q, count):
        line = lax.rem(lax.broadcasted_iota(jnp.int32, (many, 1), 0), group)
        column = lax.broadcasted_iota(jnp.int32, (1, count * block), 1)
        there = lax.rem(lax.div(column, 4 * rows), CORES)
        inner = lax.rem(column, 4 * rows)
        asked = place(lax.div(line, r), core, q * r + lax.rem(line, r))
        held = place(lax.div(inner, rows), core + there - 2 * core * there, lax.rem(inner, rows))
        return asked >= jnp.where(column < block, held, -1)

    def attend(q, count, between):
        mine_q = pl.ds(q * many, many)
        those = pl.ds(0, count * block)
        scores = stacked((qh[mine_q, :], ql[mine_q, :]), (kh[those, :], kl[those, :]), NT)
        causal = causal_of(q, count)
        scores = jnp.where(causal, scores, FLOOR)
        weights = jnp.where(causal, jnp.exp(scores - jnp.max(scores, axis=1, keepdims=True)), 0.0)
        between()
        total[mine_q, :] = jnp.sum(weights, axis=1, keepdims=True)
        acc[mine_q, :] = stacked(halves(weights), (kh[those, :rank], kl[those, :rank]))

    def attend_whole(q, between=lambda: None):
        for count in range(1, ctx_n + 1):
            when(ctx + 1 == count, lambda count=count: attend(q, count, between))

    def span_of(q, t):
        low, high = [width // 2 // LANE * i // cuts[q] * LANE for i in (t // 2, t // 2 + 1)]
        return pl.ds(2 * low + t % 2 * (high - low), high - low)

    def axes_of(t):
        return (1, 2) if t % 2 == 0 else (2, 1)

    def sum_copy(q, t, j):
        first, second = axes_of(t)
        span = span_of(q, t)
        here = pl.ds(q * r, r)

        def part_of(s):
            return part.at[pl.ds(q * group + s * r, r), span]

        src, dst, target = [
            (part_of(3), mid.at[here, span], first),
            (part_of(first), near.at[here, span], first),
            (fwd.at[here, span], last.at[here, span], second),
        ][j]
        return remote(src, dst, sum_send.at[0], sum_recv.at[2 * sum(cuts[:q]) + t if j == 0 else 2 * sum(cuts) + q], side[target])

    def project(q, between=lambda: None):
        found = []
        for p in range(CORES):
            span = pl.ds(q * many + p * group, group)
            found.append(stacked(halves(acc[span, :] / total[span, :]), halves(wv[p])))
        attended = halves(jnp.concatenate(found, axis=1))
        for t in range(2 * cuts[q]):
            span = span_of(q, t)
            part[pl.ds(q * group, group), span] = stacked(attended, (woh[:, span], wol[:, span]))
            sum_copy(q, t, 0).start()
        between()
        for t in range(2 * cuts[q]):
            sum_copy(q, t, 1).start()

    def second_stage(q, low, high):
        here = pl.ds(q * r, r)
        for t in range(low, high):
            span = span_of(q, t)
            sum_copy(q, t, 0).wait_recv()
            keep = axes_of(t)[1]
            fwd[here, span] = part[pl.ds(q * group + keep * r, r), span] + mid[here, span]
            sum_copy(q, t, 2).start()

    def collect(q):
        here = pl.ds(q * r, r)
        landed = near.at[pl.ds(0, 2 * r)]
        remote(landed, landed, sum_send.at[0], sum_recv.at[2 * sum(cuts) + q], twin).wait_recv()
        out[here, :] = part[pl.ds(q * group, r), :] + near[here, :] + last[here, :]

    def split_out():
        kept(2)
        for p in range(CORES):
            span = pl.ds(p * vdim, vdim)
            woh[span, :], wol[span, :] = halves(wo[p])

    def z_join():
        z_wait(1)
        lat_twin(1, 0, 4)

    def begin(d):
        when(ctx >= d, lambda: lat_relay(d))

    def done(d):
        lat_finish(d)
        keys(d, 0)

    def z_done():
        z_join()
        keys(1, 0)

    def sent_on():
        done(0)
        if ctx_n > 1:
            when(ctx + 1 < ctx_n, z_end)

    when(ctx < 1, sent_on)
    queries(0)
    when(ctx >= 1, sent_on)
    for d in range(2, ctx_n):
        begin(d)
    for q in range(1, chunks):
        when(jnp.logical_or(ctx < 2, core == 0), lambda q=q: hid_direct(q, REST[:2]))
    split_out()
    if ctx_n > 2:
        when(ctx >= 2, lambda: done(2))
    if ctx_n > 1:
        when(ctx >= 1, z_done)
    for d in range(3, ctx_n):
        when(ctx >= d, lambda d=d: done(d))
    for q in range(1, chunks):
        when(jnp.logical_and(ctx >= 2, core == 1), lambda q=q: hid_direct(q, FIRST + REST[:2]))
    for q in range(1, chunks):
        hid_relay(q)
    for count in range(1, ctx_n + 1):
        when(ctx + 1 == count, lambda count=count: lat_ready(count))
    attend_whole(0)
    project(0)
    for q in range(1, chunks):
        queries(q)
        attend_whole(q, lambda: second_stage(q - 1, 0, 3))
        second_stage(q - 1, 3, 2 * cuts[q - 1])
        project(q)
        second_stage(q, 0, 2 * cuts[q])
        collect(q - 1)
    collect(chunks - 1)

    sent = hid.at[pl.ds(0, 3 * rows)]
    for sem in (hid_send.at[0], sum_send.at[0]):
        remote(sent, sent, sem, hid_recv.at[0, 0], twin).wait_send()
    for here in range(ctx_n):
        def drain(here=here):
            slots = 7 * (here + 1) - 3 * (here > 0)
            sent = lat.at[pl.ds(0, slots * slot)]
            remote(sent, sent, lat_send.at[0], twin_recv.at[0], twin).wait_send()
            if here + 1 < ctx_n:
                sent = lat.at[pl.ds(0, (ctx_n - here + 2) * slot)]
                remote(sent, sent, z_send.at[0], z_recv.at[0], head).wait_send()

        when(ctx == here, drain)


def square_call(ctx_n, hidden, w_query, w_down, gain, w_key_up, w_value_up, w_out):
    rows, width = hidden.shape
    rank, nope = w_key_up.shape
    vdim = w_value_up.shape[1]
    f32, bf16, dma = jnp.float32, jnp.bfloat16, pltpu.SemaphoreType.DMA
    chunks = 2
    cuts = (2, 3)
    r = rows // chunks
    block = CORES * 4 * rows
    lanes = rank + LANE
    steps = 3 if width % 384 == 0 else 1
    slot = rows * (rank // LANE) + rows // 2
    query = (CORES,) + w_query.shape
    both = (CORES * vdim, width)
    return pl.pallas_call(
        functools.partial(square_kernel, ctx_n, chunks, cuts),
        out_shape=pltpu.VMEM((rows, width), f32),
        in_specs=[pl.BlockSpec(memory_space=pltpu.HBM)] * 7,
        out_specs=pl.BlockSpec(memory_space=pltpu.VMEM),
        scratch_shapes=[
            pltpu.VMEM((rows, width), f32),
            pltpu.VMEM((4 * rows, width), f32),
            pltpu.VMEM(w_down.shape, f32),
            pltpu.VMEM((1, rank), f32),
            pltpu.VMEM(query, f32), pltpu.VMEM(query, bf16), pltpu.VMEM(query, bf16),
            pltpu.VMEM((CORES, rank, nope), f32),
            pltpu.VMEM((CORES, rank, vdim), f32),
            pltpu.VMEM((CORES, vdim, width), f32), pltpu.VMEM(both, bf16), pltpu.VMEM(both, bf16),
            pltpu.VMEM((ctx_n * CORES * 4 * slot, LANE), f32),
            pltpu.VMEM((ctx_n * block, lanes), bf16), pltpu.VMEM((ctx_n * block, lanes), bf16),
            pltpu.VMEM((block, lanes), bf16), pltpu.VMEM((block, lanes), bf16),
            pltpu.VMEM((block, 1), f32),
            pltpu.VMEM((block, rank), f32),
            pltpu.VMEM((4 * rows, width), f32),
        ] + [pltpu.VMEM((rows, width), f32)] * 4 + [
            dma((6 + steps,)),
            dma((3,)), dma((3,)),
            dma((1,)), dma((chunks, 3)),
            pltpu.SemaphoreType.REGULAR((max(ctx_n - 2, 1),)),
            dma((1,)), dma((max(ctx_n - 1, 1),)),
            dma((1,)), dma((max(ctx_n - 1, 1), 3)),
            dma((1,)),
            dma((1,)), dma((2 * sum(cuts) + chunks,)),
        ],
        compiler_params=pltpu.CompilerParams(
            collective_id=0, has_side_effects=True, vmem_limit_bytes=60 * 1024 * 1024
        ),
    )(hidden, w_query, w_down, gain, w_key_up, w_value_up, w_out)


def on_device(ctx_n, chips, hidden, w_query, w_down, latent_gain, w_key_up, w_value_up, w_out):
    rows, width = hidden.shape
    rank, nope = w_key_up.shape
    vdim = w_value_up.shape[1]
    per_core = chips * rows
    block = CORES * per_core
    lanes = -(-w_down.shape[1] // 128) * 128
    steps = 3 if width % 384 == 0 else 1
    if chips == 4 and rows % 32 == 0 and width % 768 == 0 and rank % LANE == 0 and 2 * (w_down.shape[1] - rank) == LANE:
        return square_call(
            ctx_n, hidden, w_query.T, w_down.T, latent_gain.reshape(1, rank), w_key_up, w_value_up, w_out
        )
    square = chips == 4 and rows % 16 == 0 and width % 256 == 0
    pieces = 6 if width % 768 == 0 else 2
    f32, bf16, dma = jnp.float32, jnp.bfloat16, pltpu.SemaphoreType.DMA
    return pl.pallas_call(
        functools.partial(general_kernel, ctx_n, chips, square, steps, pieces),
        out_shape=jax.ShapeDtypeStruct((rows, width), f32),
        in_specs=[pl.BlockSpec(memory_space=pltpu.HBM)] * 7,
        out_specs=pl.BlockSpec(memory_space=pltpu.VMEM),
        scratch_shapes=[
            pltpu.VMEM((per_core, width), f32),
            pltpu.VMEM(w_down.shape[::-1], f32),
            pltpu.VMEM((CORES,) + w_query.shape[::-1], f32),
            pltpu.VMEM((1, rank), f32),
            pltpu.VMEM((CORES, rank, nope), f32),
            pltpu.VMEM((CORES, rank, vdim), f32),
            pltpu.VMEM((CORES, vdim, width), f32),
            pltpu.VMEM((ctx_n * block, lanes), f32),
            pltpu.VMEM((block, lanes), bf16),
            pltpu.VMEM((block, lanes), bf16),
            pltpu.VMEM((block, 1), f32),
            pltpu.VMEM((block, 1), f32),
            pltpu.VMEM((block, rank), f32),
            pltpu.VMEM((per_core, width), f32),
            pltpu.VMEM((per_core, width), f32),
            dma((2 + steps + 4,)),
            dma((4,)), dma((4,)),
            dma((chips, 2)), dma((chips, 2)),
            dma((ctx_n,)), dma((ctx_n,)),
            dma((ctx_n, chips, 2)), dma((ctx_n, chips, 2)),
            dma((ctx_n,)), dma((ctx_n,)),
            dma((pieces, chips)), dma((pieces, chips)),
        ],
        compiler_params=pltpu.CompilerParams(
            collective_id=0, has_side_effects=True, vmem_limit_bytes=60 * 1024 * 1024
        ),
    )(hidden, w_query.T, w_down.T, latent_gain.reshape(1, rank), w_key_up, w_value_up, w_out)


def solution(mesh):
    placed = (
        P(("ctx", "head"), None),
        P(None, "head"),
        P(),
        P(),
        P(None, "head"),
        P(None, "head"),
        P("head", None),
    )
    body = functools.partial(on_device, mesh.shape["ctx"], mesh.shape["head"] // CORES)
    return jax.shard_map(
        body, mesh=mesh, in_specs=placed, out_specs=P(("ctx", "head"), None), check_vma=False
    )
```

```python
import functools

import jax
import jax.numpy as jnp
from jax import lax
from jax.experimental import pallas as pl
from jax.experimental.pallas import tpu as pltpu
from jax.sharding import PartitionSpec as P

EPSILON = 1e-06
FLOOR = -1e30
CORES = 2
LANE = 128
FIRST = ((1, 0), (2, 1))
DIRECT = ((1, 0), (2, 1), (1, 1), (2, 0))
REST = ((1, 1), (2, 0), (3, 0), (3, 1))
MESH = pl.DeviceIdType.MESH
NN = (((1,), (0,)), ((), ()))
NT = (((1,), (1,)), ((), ()))


def halves(value):
    high = value.astype(jnp.bfloat16)
    return high, (value - high.astype(jnp.float32)).astype(jnp.bfloat16)


def product(left, right, dims=NN):
    (lh, ll), (rh, rl) = left, right
    dot = functools.partial(lax.dot_general, dimension_numbers=dims, preferred_element_type=jnp.float32)
    return dot(lh, rh) + (dot(ll, rh) + dot(lh, rl))


def stacked(left, right, dims=NN):
    (lh, ll), (rh, rl) = left, right
    dot = functools.partial(lax.dot_general, dimension_numbers=dims, preferred_element_type=jnp.float32)
    both = dot(jnp.concatenate([lh, ll], axis=0), rh)
    size = lh.shape[0]
    return both[:size] + (both[size:] + dot(lh, rl))


def general_kernel(
    ctx_n, chips, square, steps, pieces,
    hidden, w_query, w_down, gain, w_key, w_value, w_out, out,
    hid, wd, wq, gn, wk, wv, wo, lat, qh, ql, top, total, acc, part, landed,
    load_sem, swap_send, swap_recv, hid_send, hid_recv, col_send, col_recv,
    row_send, row_recv, twin_send, twin_recv, sum_send, sum_recv,
):
    rows, width = hidden.shape
    parts = 2 if square else 1
    rank = gn.shape[1]
    tail = wd.shape[0] - rank
    nope = wk.shape[2]
    per_core = chips * rows
    block = CORES * per_core
    lanes = lat.shape[1]
    ctx = lax.axis_index("ctx")
    head = lax.axis_index("head")
    chip, core = head // CORES, head % CORES
    twin = chip * CORES + (1 - core)

    def chip_at(offset):
        return lax.rem(chip + offset, chips)

    def to(o):
        if not square:
            return chip_at(o)
        return [chip, chip + 1 - 2 * lax.rem(chip, 2), lax.rem(chip + 2, 4), 3 - chip][o]

    def origin(o):
        return to(o) if square else chip_at(chips - o)

    def local(src, dst, sem):
        return pltpu.make_async_copy(src, dst, load_sem.at[sem])

    def remote(src, dst, send, recv, c, h):
        return pltpu.make_async_remote_copy(
            src_ref=src, dst_ref=dst, send_sem=send, recv_sem=recv,
            device_id={"ctx": c, "head": h}, device_id_type=MESH,
        )

    def at_rows(start, size):
        return pl.ds(pl.multiple_of(start, 8), size)

    my_hid = hid.at[at_rows(chip * rows, rows)]
    depth = width // steps
    loads = [local(hidden, my_hid, 0), local(gain, gn, 1)]
    for s in range(steps):
        span = pl.ds(s * depth, depth)
        loads.append(local(w_down.at[:, span], wd.at[:, span], 2 + s))
    pairs = [(w_query, wq), (w_key, wk), (w_value, wv), (w_out, wo)]
    own = [local(src, dst.at[core], 2 + steps + i) for i, (src, dst) in enumerate(pairs)]
    for copy in loads:
        copy.start()

    barrier = pltpu.get_barrier_semaphore()
    for o in range(1, chips):
        pl.semaphore_signal(barrier, inc=1, device_id={"ctx": ctx, "head": chip_at(o) * CORES + core}, device_id_type=MESH)
    pl.semaphore_signal(barrier, inc=1, device_id={"ctx": ctx, "head": twin}, device_id_type=MESH)
    for o in range(1, ctx_n):
        pl.semaphore_signal(barrier, inc=1, device_id={"ctx": lax.rem(ctx + o, ctx_n), "head": head}, device_id_type=MESH)
    pl.semaphore_wait(barrier, chips - 1 + 1 + ctx_n - 1)

    def share(source, spot, send, recv):
        def start_of(o, h):
            target = to(o)
            return remote(source(h), spot(chip, h), send(o, h), recv(o, h), ctx, target * CORES + core)

        def seen(o, h):
            place_of = spot(origin(o), h)
            return remote(place_of, place_of, send(o, h), recv(o, h), ctx, twin)

        def passed(h):
            place_of = spot(to(1 + h), h)
            return remote(place_of, place_of, send(3, h), recv(3, h), ctx, to(2 - h) * CORES + core)

        direct = [(1, 0), (2, 1), (1, 1), (2, 0)] if square else [(o, 0) for o in range(1, chips)]

        def start():
            for o, h in direct:
                start_of(o, h).start()

        def relay():
            if square:
                for h in range(2):
                    seen(1 + h, h).wait_recv()
                    passed(h).start()

        def finish():
            for o, h in [(1, 1), (2, 0), (3, 0), (3, 1)] if square else direct:
                seen(o, h).wait_recv()

        def drain():
            for o, h in direct:
                start_of(o, h).wait_send()
            if square:
                for h in range(2):
                    passed(h).wait_send()

        return start, relay, finish, drain

    half = width // parts

    def hid_half(h):
        return pl.ds(h * half, half)

    hid_start, hid_relay, hid_finish, hid_drain = share(
        lambda h: hidden.at[:, hid_half(h)],
        lambda k, h: hid.at[at_rows(k * rows, rows), hid_half(h)],
        lambda o, h: hid_send.at[o, h],
        lambda o, h: hid_recv.at[o, h],
    )
    hid_start()
    swaps = [remote(src, dst.at[core], swap_send.at[i], swap_recv.at[i], ctx, twin) for i, (src, dst) in enumerate(pairs)]
    for copy in own:
        copy.start()
    for copy in swaps:
        copy.start()

    loads[0].wait()
    loads[1].wait()
    down = jnp.zeros((rows, rank + tail), jnp.float32)
    for s in range(steps):
        loads[2 + s].wait()
        span = pl.ds(s * depth, depth)
        down += product(halves(my_hid[:, span]), halves(wd[:, span]), NT)
    raw = down[:, :rank]
    meansq = jnp.mean(raw * raw, axis=-1, keepdims=True)
    blank = jnp.zeros((rows, lanes - rank - tail), jnp.float32)

    def place(b, p, k):
        return ((b * CORES + p) * chips + k) * rows

    mine = at_rows(place(ctx, core, chip), rows)
    lat[mine, :rank] = raw * lax.rsqrt(meansq + EPSILON) * gn[...]
    lat[mine, rank:] = jnp.concatenate([down[:, rank:], blank], axis=1)

    def col_copy(b):
        spot = lat.at[at_rows(place(b, core, chip), rows)]
        return remote(spot, spot, col_send.at[b], col_recv.at[b], jnp.minimum(ctx + 1, ctx_n - 1), head)

    def latents(b):
        def spot(k, h):
            return lat.at[at_rows(place(b, core, k) + h * (rows // parts), rows // parts)]

        return share(
            lambda h: spot(chip, h), spot, lambda o, h: row_send.at[b, o, h], lambda o, h: row_recv.at[b, o, h]
        )

    def twin_copy(b, p):
        spot = lat.at[at_rows(place(b, p, 0), per_core)]
        return remote(spot, spot, twin_send.at[b], twin_recv.at[b], ctx, twin)

    def spread(b):
        @pl.when(ctx + 1 < ctx_n)
        def _():
            col_copy(b).start()

        latents(b)[0]()

    def gather_rows(b):
        latents(b)[2]()
        twin_copy(b, core).start()

    spread(ctx)
    hid_relay()
    for d in range(1, ctx_n):
        @pl.when(d <= ctx)
        def _():
            col_copy(ctx - d).wait_recv()
            spread(ctx - d)

    latents(ctx)[1]()

    hid_finish()
    for i in range(2):
        own[i].wait()
        swaps[i].wait()
    scale = wq.shape[1] ** (-0.5)
    pad = jnp.zeros((per_core, lanes - rank - tail), jnp.float32)
    query = [jnp.zeros((per_core, wq.shape[1]), jnp.float32) for _ in range(CORES)]
    for s in range(steps):
        span = pl.ds(s * depth, depth)
        piece = halves(hid[:, span])
        for p in range(CORES):
            query[p] += product(piece, halves(wq[p, :, span]), NT)
    for p in range(CORES):
        wide = product(halves(query[p][:, :nope] * scale), halves(wk[p]), NT)
        span = pl.ds(p * per_core, per_core)
        qh[span, :rank], ql[span, :rank] = halves(wide)
        qh[span, rank:], ql[span, rank:] = halves(jnp.concatenate([query[p][:, nope:] * scale, pad], axis=1))

    def spots(index, parity):
        inner = lax.rem(index, per_core)
        return (lax.div(inner, rows) * CORES + parity) * rows + lax.rem(inner, rows)

    def attend(b, first):
        keys = halves(lat[at_rows(place(b, 0, 0), block), :])
        scores = product((qh[...], ql[...]), keys, NT)
        if first:
            line = lax.broadcasted_iota(jnp.int32, (block, 1), 0)
            column = lax.broadcasted_iota(jnp.int32, (1, block), 1)
            causal = spots(line, core) >= spots(column, lax.div(column, per_core))
            scores = jnp.where(causal, scores, FLOOR)
            peak = jnp.max(scores, axis=1, keepdims=True)
        else:
            peak = jnp.maximum(top[...], jnp.max(scores, axis=1, keepdims=True))
        weights = jnp.exp(scores - peak)
        if first:
            weights = jnp.where(causal, weights, 0.0)
        mixed = product(halves(weights), (keys[0][:, :rank], keys[1][:, :rank]))
        added = jnp.sum(weights, axis=1, keepdims=True)
        if first:
            total[...] = added
            acc[...] = mixed
        else:
            fade = jnp.exp(top[...] - peak)
            total[...] = total[...] * fade + added
            acc[...] = acc[...] * fade + mixed
        top[...] = peak

    def relay_at(d):
        if d < ctx_n:
            @pl.when(d <= ctx)
            def _():
                latents(ctx - d)[1]()

    relay_at(1)
    gather_rows(ctx)
    twin_copy(ctx, 1 - core).wait_recv()
    attend(ctx, True)
    for d in range(1, ctx_n):
        @pl.when(d <= ctx)
        def _():
            relay_at(d + 1)
            gather_rows(ctx - d)
            twin_copy(ctx - d, 1 - core).wait_recv()
            attend(ctx - d, False)

    for i in range(2, 4):
        own[i].wait()
        swaps[i].wait()
    heads = []
    for p in range(CORES):
        span = pl.ds(p * per_core, per_core)
        heads.append(product(halves(acc[span, :] / total[span, :]), halves(wv[p])))
    attended = halves(jnp.concatenate(heads, axis=1))
    columns = width // pieces

    def cut(ref, k, t):
        return ref.at[at_rows(k * rows, rows), pl.ds(t * columns, columns)]

    def axes_of(t):
        return (1, 2) if t % 2 == 0 else (2, 1)

    def sum_copy(t, j):
        if not square:
            return remote(
                cut(part, chip_at(j), t), cut(landed, chip, t), sum_send.at[t, j], sum_recv.at[t, j],
                ctx, chip_at(j) * CORES + core,
            )
        first, second = axes_of(t)
        src = [to(3), to(first), to(second)][j]
        dst = [to(3), to(first), to(3)][j]
        target = [to(first), to(first), to(second)][j]
        return remote(cut(part, src, t), cut(landed, dst, t), sum_send.at[t, j], sum_recv.at[t, j], ctx, target * CORES + core)

    def second_stage(t):
        sum_copy(t, 0).wait_recv()
        keep = to(axes_of(t)[1])
        cut(part, keep, t)[...] = cut(part, keep, t)[...] + cut(landed, keep, t)[...]
        sum_copy(t, 2).start()

    kinds = (0, 1) if square else tuple(range(1, chips))
    for t in range(pieces):
        span = pl.ds(t * columns, columns)
        weight = jnp.concatenate([wo[p, :, span] for p in range(CORES)], axis=0)
        part[:, span] = product(attended, halves(weight))
        for j in kinds:
            sum_copy(t, j).start()
        if square and t >= 2:
            second_stage(t - 2)
    if square:
        for t in range(max(pieces - 2, 0), pieces):
            second_stage(t)
    for t in range(pieces):
        result = cut(part, chip, t)[...]
        if square:
            for j in (1, 2):
                sum_copy(t, j).wait_recv()
            result += cut(landed, chip, t)[...] + cut(landed, to(axes_of(t)[0]), t)[...]
        else:
            for j in kinds:
                sum_copy(t, j).wait_recv()
                result += cut(landed, origin(j), t)[...]
        out[:, pl.ds(t * columns, columns)] = result

    hid_drain()
    for t in range(pieces):
        for j in kinds + ((2,) if square else ()):
            sum_copy(t, j).wait_send()
    for d in range(ctx_n):
        @pl.when(d <= ctx)
        def _():
            @pl.when(ctx + 1 < ctx_n)
            def _():
                col_copy(ctx - d).wait_send()

            latents(ctx - d)[3]()
            twin_copy(ctx - d, core).wait_send()


def square_kernel(
    ctx_n, chunks, cuts,
    hidden, w_query, w_down, gain, w_key, w_value, w_out, out,
    mine, hid, wd, gn, wq, wqh, wql, wk, wv, wo, woh, wol, lat, kh, kl, qh, ql, total, acc,
    part, mid, fwd, near, last,
    load_sem, swap_send, swap_recv, hid_send, hid_recv, far_sem, z_send, z_recv,
    lat_send, lat_recv, twin_recv, sum_send, sum_recv,
):
    rows, width = hidden.shape
    rank = gn.shape[1]
    tail = wd.shape[0] - rank
    nope, vdim = wk.shape[2], wv.shape[2]
    key_width = wq.shape[1]
    lanes = kh.shape[1]
    r = rows // chunks
    group = 4 * r
    many = CORES * group
    block = CORES * 4 * rows
    hr = rows // 2
    tiles = rank // LANE
    piece = hr * tiles + hr // 2
    slot = 2 * piece
    half = width // 2
    steps = 3 if width % 384 == 0 else 1
    depth = width // steps
    ctx = lax.axis_index("ctx")
    head = lax.axis_index("head")
    chip, core = head // CORES, head % CORES
    twin = chip * CORES + (1 - core)
    xbit, ybit = lax.rem(chip, 2), lax.div(chip, 2)
    side = [None, (2 * ybit + 1 - xbit) * CORES + core, (2 * (1 - ybit) + xbit) * CORES + core]

    def local(src, dst, sem):
        return pltpu.make_async_copy(src, dst, sem)

    def remote(src, dst, send, recv, h, c=ctx):
        return pltpu.make_async_remote_copy(
            src_ref=src, dst_ref=dst, send_sem=send, recv_sem=recv,
            device_id={"ctx": c, "head": h}, device_id_type=MESH,
        )

    def signal(sem, c, h):
        pl.semaphore_signal(sem, inc=1, device_id={"ctx": c, "head": h}, device_id_type=MESH)

    def when(condition, *actions):
        @pl.when(condition)
        def _():
            for action in actions:
                action()

    def spot(q, s, h):
        return hid.at[pl.ds((q * 4 + s) * r, r), pl.ds(h * half, half)]

    def hid_direct(q, order):
        for a, h in order:
            remote(
                hidden.at[pl.ds(q * r, r), pl.ds(h * half, half)], spot(q, a, h),
                hid_send.at[0], hid_recv.at[q, 0 if (a, h) in FIRST else 1], side[a],
            ).start()

    def hid_relay(q):
        landed = hid.at[pl.ds((q * 4 + 1) * r, r)]
        remote(landed, landed, hid_send.at[0], hid_recv.at[q, 0], twin).wait_recv()
        for h in range(2):
            remote(spot(q, 1 + h, h), spot(q, 3, h), hid_send.at[0], hid_recv.at[q, 1], side[2 - h]).start()

    def hid_finish(q):
        landed = hid.at[pl.ds((q * 4 + 1) * r, 2 * r)]
        remote(landed, landed, hid_send.at[0], hid_recv.at[q, 1], twin).wait_recv()

    def lat_at(d, p, s, h=0, size=piece):
        return lat.at[pl.ds(((d * CORES + p) * 4 + s) * slot + h * piece, size)]

    def lat_twin(d, s, count):
        size = count * slot
        remote(lat_at(d, 0, s, 0, size), lat_at(d, 1, s, 0, size), lat_send.at[0], twin_recv.at[0], twin).start()

    def z_copy(d, s, h, size):
        c = jnp.minimum(ctx + d, ctx_n - 1)
        return remote(lat_at(0, 0, s, h, size), lat_at(d, 0, s, h, size), z_send.at[0], z_recv.at[d - 1], head, c)

    def z_wait(d):
        landed = lat_at(d, 0, 0, 0, 4 * slot if d == 1 else slot)
        remote(landed, landed, z_send.at[0], z_recv.at[d - 1], head).wait_recv()

    def lat_direct(d, order):
        for a, h in order:
            remote(
                lat_at(d, 0, 0, h), lat_at(d, 0, a, h), lat_send.at[0],
                lat_recv.at[max(d - 1, 0), h if (a, h) in FIRST else 2], side[a],
            ).start()

    def lat_fetch(d):
        z_wait(d)
        lat_direct(d, FIRST)
        lat_twin(d, 0, 1)

    def lat_relay(d):
        for h in range(2):
            landed = lat_at(d, 0, 1 + h, h)
            remote(landed, landed, lat_send.at[0], lat_recv.at[max(d - 1, 0), h], twin).wait_recv()
            remote(landed, lat_at(d, 0, 3, h), lat_send.at[0], lat_recv.at[max(d - 1, 0), 2], side[2 - h]).start()

    def lat_finish(d):
        landed = lat_at(d, 0, 1, 0, 2 * slot)
        remote(landed, landed, lat_send.at[0], lat_recv.at[max(d - 1, 0), 2], twin).wait_recv()
        lat_twin(d, 1, 3)
    def z_begin():
        z_copy(1, 0, 0, slot).start()
        z_copy(1, 1, 0, piece).start()
        z_copy(1, 2, 1, piece).start()

    def z_end():
        z_copy(1, 1, 1, 2 * piece).start()
        z_copy(1, 3, 0, slot).start()

    loads = [local(hidden, mine, load_sem.at[0]), local(gain, gn, load_sem.at[1])]
    for i in range(steps):
        span = pl.ds(i * depth, depth)
        loads.append(local(w_down.at[:, span], wd.at[:, span], load_sem.at[2 + i]))
    pairs = [(w_query, wq), (w_key, wk), (w_value, wv), (w_out, wo)]
    lots = (0, 1, 1, 2)
    own = [local(src, dst.at[0], load_sem.at[2 + steps + lot]) for (src, dst), lot in zip(pairs, lots)]
    for q in range(chunks):
        own.append(local(hidden.at[pl.ds(q * r, r)], hid.at[pl.ds(q * group, r)], load_sem.at[5 + steps]))
    for copy in loads:
        copy.start()

    barrier = pltpu.get_barrier_semaphore()
    for h in (twin, side[1], side[2]):
        signal(barrier, ctx, h)
    when(ctx > 0, lambda: signal(barrier, ctx - 1, head))
    when(ctx + 1 < ctx_n, lambda: signal(barrier, ctx + 1, head))
    pl.semaphore_wait(barrier, 3 + jnp.minimum(ctx, 1) + jnp.minimum(ctx_n - 1 - ctx, 1))

    hid_direct(0, FIRST)
    swaps = [
        remote(src, dst.at[1], swap_send.at[lot], swap_recv.at[lot], twin) for (src, dst), lot in zip(pairs, lots)
    ]
    for copy in own:
        copy.start()
    for copy in swaps:
        copy.start()

    if ctx_n > 2:
        when(jnp.logical_and(ctx >= 1, ctx + 2 <= ctx_n), lambda: signal(far_sem.at[0], ctx - 1, head))

    loads[0].wait()
    loads[1].wait()
    down = jnp.zeros((rows, rank + tail), jnp.float32)
    for i in range(steps):
        loads[2 + i].wait()
        span = pl.ds(i * depth, depth)
        down += stacked(halves(mine[:, span]), halves(wd[:, span]), NT)
    raw = down[:, :rank]
    meansq = jnp.mean(raw * raw, axis=-1, keepdims=True)
    latent = raw * lax.rsqrt(meansq + EPSILON) * gn[...]
    shared = jnp.concatenate([down[:hr, rank:], down[hr:, rank:]], axis=1)
    for h in range(2):
        for j in range(tiles):
            lat_at(0, 0, 0, h)[pl.ds(j * hr, hr), :] = latent[h * hr : (h + 1) * hr, j * LANE : (j + 1) * LANE]
        lat_at(0, 0, 0, h)[pl.ds(tiles * hr, hr // 2), :] = shared[h * hr // 2 : (h + 1) * hr // 2]

    for d in range(2, ctx_n):
        when(ctx + d < ctx_n, lambda d=d: pl.semaphore_wait(far_sem.at[d - 2], 1))
        if d + 1 < ctx_n:
            when(
                jnp.logical_and(ctx >= 1, ctx + d < ctx_n),
                lambda d=d: signal(far_sem.at[d - 1], ctx - 1, head),
            )
    for d in range(2, ctx_n):
        when(ctx + d < ctx_n, lambda d=d: z_copy(d, 0, 0, slot).start())
    lat_direct(0, DIRECT)
    hid_direct(0, REST[:2])
    lat_twin(0, 0, 1)

    def split_query(p):
        wqh[p], wql[p] = halves(wq[p])

    def kept(lot):
        whole = {0: wq.at[0], 1: wk, 2: wo.at[0]}[lot]
        local(whole, whole, load_sem.at[2 + steps + lot]).wait()
        remote(whole, whole, swap_send.at[lot], swap_recv.at[lot], twin).wait()

    hid_relay(0)
    own[0].wait()
    split_query(0)
    lat_relay(0)
    if ctx_n > 1:
        when(ctx + 1 < ctx_n, z_begin)
    swaps[0].wait()
    split_query(1)
    for d in range(2, ctx_n):
        when(ctx >= d, lambda d=d: lat_fetch(d))
    for d in range(2, ctx_n):
        when(ctx >= d, lambda d=d: lat_direct(d, REST[:2]))
    for q in range(1, chunks):
        when(jnp.logical_or(ctx < 2, core == 0), lambda q=q: hid_direct(q, FIRST))
    kept(1)
    local(mine, mine, load_sem.at[5 + steps]).wait()

    scale = key_width ** (-0.5)
    pad = jnp.zeros((group, lanes - rank - tail), jnp.float32)

    def queries(q):
        hid_finish(q)
        query = [jnp.zeros((group, key_width), jnp.float32) for _ in range(CORES)]
        for i in range(steps):
            span = pl.ds(i * depth, depth)
            given = halves(hid[pl.ds(q * group, group), span])
            for p in range(CORES):
                query[p] += stacked(given, (wqh[p, :, span], wql[p, :, span]), NT)
        for p in range(CORES):
            wide = stacked(halves(query[p][:, :nope] * scale), halves(wk[p]), NT)
            span = pl.ds(q * many + p * group, group)
            qh[span, :rank], ql[span, :rank] = halves(wide)
            rest = jnp.concatenate([query[p][:, nope:] * scale, pad], axis=1)
            qh[span, rank:], ql[span, rank:] = halves(rest)

    def keys(d, p):
        for s in range(4):
            at = d * block + (p * 4 + s) * rows
            packed = jnp.concatenate(
                [lat_at(d, p, s, h)[pl.ds(tiles * hr, hr // 2), :] for h in range(2)], axis=0
            )
            for h in range(2):
                span = pl.ds(at + h * hr, hr)
                for j in range(tiles):
                    lane = pl.ds(j * LANE, LANE)
                    kh[span, lane], kl[span, lane] = halves(lat_at(d, p, s, h)[pl.ds(j * hr, hr), :])
                lane = pl.ds(rank, LANE)
                kh[span, lane], kl[span, lane] = halves(packed if h == 0 else pltpu.roll(packed, tail, 1))

    def lat_ready(count):
        landed = lat.at[pl.ds(0, 4 * count * slot)]
        remote(landed, landed, lat_send.at[0], twin_recv.at[0], twin).wait_recv()
        for d in range(count):
            keys(d, 1)

    def place(s, parity, i):
        sx, sy = lax.rem(s, 2), lax.div(s, 2)
        x, y = lax.rem(xbit + sx, 2), lax.rem(ybit + sy, 2)
        return ((2 * y + x) * CORES + parity) * rows + i

    def causal_of(q, count):
        line = lax.rem(lax.broadcasted_iota(jnp.int32, (many, 1), 0), group)
        column = lax.broadcasted_iota(jnp.int32, (1, count * block), 1)
        there = lax.rem(lax.div(column, 4 * rows), CORES)
        inner = lax.rem(column, 4 * rows)
        asked = place(lax.div(line, r), core, q * r + lax.rem(line, r))
        held = place(lax.div(inner, rows), core + there - 2 * core * there, lax.rem(inner, rows))
        return asked >= jnp.where(column < block, held, -1)

    def attend(q, count, between):
        mine_q = pl.ds(q * many, many)
        those = pl.ds(0, count * block)
        scores = stacked((qh[mine_q, :], ql[mine_q, :]), (kh[those, :], kl[those, :]), NT)
        causal = causal_of(q, count)
        scores = jnp.where(causal, scores, FLOOR)
        weights = jnp.where(causal, jnp.exp(scores - jnp.max(scores, axis=1, keepdims=True)), 0.0)
        between()
        total[mine_q, :] = jnp.sum(weights, axis=1, keepdims=True)
        acc[mine_q, :] = stacked(halves(weights), (kh[those, :rank], kl[those, :rank]))

    def attend_whole(q, between=lambda: None):
        for count in range(1, ctx_n + 1):
            when(ctx + 1 == count, lambda count=count: attend(q, count, between))

    def span_of(q, t):
        low, high = [width // 2 // LANE * i // cuts[q] * LANE for i in (t // 2, t // 2 + 1)]
        return pl.ds(2 * low + t % 2 * (high - low), high - low)

    def axes_of(t):
        return (1, 2) if t % 2 == 0 else (2, 1)

    def sum_copy(q, t, j):
        first, second = axes_of(t)
        span = span_of(q, t)
        here = pl.ds(q * r, r)

        def part_of(s):
            return part.at[pl.ds(q * group + s * r, r), span]

        src, dst, target = [
            (part_of(3), mid.at[here, span], first),
            (part_of(first), near.at[here, span], first),
            (fwd.at[here, span], last.at[here, span], second),
        ][j]
        return remote(src, dst, sum_send.at[0], sum_recv.at[2 * sum(cuts[:q]) + t if j == 0 else 2 * sum(cuts) + q], side[target])

    def project(q, between=lambda: None):
        found = []
        for p in range(CORES):
            span = pl.ds(q * many + p * group, group)
            found.append(stacked(halves(acc[span, :] / total[span, :]), halves(wv[p])))
        attended = halves(jnp.concatenate(found, axis=1))
        for t in range(2 * cuts[q]):
            span = span_of(q, t)
            part[pl.ds(q * group, group), span] = stacked(attended, (woh[:, span], wol[:, span]))
            sum_copy(q, t, 0).start()
        between()
        for t in range(2 * cuts[q]):
            sum_copy(q, t, 1).start()

    def second_stage(q, low, high):
        here = pl.ds(q * r, r)
        for t in range(low, high):
            span = span_of(q, t)
            sum_copy(q, t, 0).wait_recv()
            keep = axes_of(t)[1]
            fwd[here, span] = part[pl.ds(q * group + keep * r, r), span] + mid[here, span]
            sum_copy(q, t, 2).start()

    def collect(q):
        here = pl.ds(q * r, r)
        landed = near.at[pl.ds(0, 2 * r)]
        remote(landed, landed, sum_send.at[0], sum_recv.at[2 * sum(cuts) + q], twin).wait_recv()
        out[here, :] = part[pl.ds(q * group, r), :] + near[here, :] + last[here, :]

    def split_out():
        kept(2)
        for p in range(CORES):
            span = pl.ds(p * vdim, vdim)
            woh[span, :], wol[span, :] = halves(wo[p])

    def z_join():
        z_wait(1)
        lat_twin(1, 0, 4)

    def begin(d):
        when(ctx >= d, lambda: lat_relay(d))

    def done(d):
        lat_finish(d)
        keys(d, 0)

    def z_done():
        z_join()
        keys(1, 0)

    def sent_on():
        done(0)
        if ctx_n > 1:
            when(ctx + 1 < ctx_n, z_end)

    when(ctx < 1, sent_on)
    queries(0)
    when(ctx >= 1, sent_on)
    for d in range(2, ctx_n):
        begin(d)
    for q in range(1, chunks):
        when(jnp.logical_or(ctx < 2, core == 0), lambda q=q: hid_direct(q, REST[:2]))
    split_out()
    if ctx_n > 2:
        when(ctx >= 2, lambda: done(2))
    if ctx_n > 1:
        when(ctx >= 1, z_done)
    for d in range(3, ctx_n):
        when(ctx >= d, lambda d=d: done(d))
    for q in range(1, chunks):
        when(jnp.logical_and(ctx >= 2, core == 1), lambda q=q: hid_direct(q, FIRST + REST[:2]))
    for q in range(1, chunks):
        hid_relay(q)
    for count in range(1, ctx_n + 1):
        when(ctx + 1 == count, lambda count=count: lat_ready(count))
    attend_whole(0)
    project(0)
    for q in range(1, chunks):
        queries(q)
        attend_whole(q, lambda: second_stage(q - 1, 0, 3))
        second_stage(q - 1, 3, 2 * cuts[q - 1])
        project(q)
        second_stage(q, 0, 2 * cuts[q])
        collect(q - 1)
    collect(chunks - 1)

    sent = hid.at[pl.ds(0, 3 * rows)]
    for sem in (hid_send.at[0], sum_send.at[0]):
        remote(sent, sent, sem, hid_recv.at[0, 0], twin).wait_send()
    for here in range(ctx_n):
        def drain(here=here):
            slots = 7 * (here + 1) - 3 * (here > 0)
            sent = lat.at[pl.ds(0, slots * slot)]
            remote(sent, sent, lat_send.at[0], twin_recv.at[0], twin).wait_send()
            if here + 1 < ctx_n:
                sent = lat.at[pl.ds(0, (ctx_n - here + 2) * slot)]
                remote(sent, sent, z_send.at[0], z_recv.at[0], head).wait_send()

        when(ctx == here, drain)


def square_call(ctx_n, hidden, w_query, w_down, gain, w_key_up, w_value_up, w_out):
    rows, width = hidden.shape
    rank, nope = w_key_up.shape
    vdim = w_value_up.shape[1]
    f32, bf16, dma = jnp.float32, jnp.bfloat16, pltpu.SemaphoreType.DMA
    chunks = 2
    cuts = (2, 3)
    r = rows // chunks
    block = CORES * 4 * rows
    lanes = rank + LANE
    steps = 3 if width % 384 == 0 else 1
    slot = rows * (rank // LANE) + rows // 2
    query = (CORES,) + w_query.shape
    both = (CORES * vdim, width)
    return pl.pallas_call(
        functools.partial(square_kernel, ctx_n, chunks, cuts),
        out_shape=pltpu.VMEM((rows, width), f32),
        in_specs=[pl.BlockSpec(memory_space=pltpu.HBM)] * 7,
        out_specs=pl.BlockSpec(memory_space=pltpu.VMEM),
        scratch_shapes=[
            pltpu.VMEM((rows, width), f32),
            pltpu.VMEM((4 * rows, width), f32),
            pltpu.VMEM(w_down.shape, f32),
            pltpu.VMEM((1, rank), f32),
            pltpu.VMEM(query, f32), pltpu.VMEM(query, bf16), pltpu.VMEM(query, bf16),
            pltpu.VMEM((CORES, rank, nope), f32),
            pltpu.VMEM((CORES, rank, vdim), f32),
            pltpu.VMEM((CORES, vdim, width), f32), pltpu.VMEM(both, bf16), pltpu.VMEM(both, bf16),
            pltpu.VMEM((ctx_n * CORES * 4 * slot, LANE), f32),
            pltpu.VMEM((ctx_n * block, lanes), bf16), pltpu.VMEM((ctx_n * block, lanes), bf16),
            pltpu.VMEM((block, lanes), bf16), pltpu.VMEM((block, lanes), bf16),
            pltpu.VMEM((block, 1), f32),
            pltpu.VMEM((block, rank), f32),
            pltpu.VMEM((4 * rows, width), f32),
        ] + [pltpu.VMEM((rows, width), f32)] * 4 + [
            dma((6 + steps,)),
            dma((3,)), dma((3,)),
            dma((1,)), dma((chunks, 2)),
            pltpu.SemaphoreType.REGULAR((max(ctx_n - 2, 1),)),
            dma((1,)), dma((max(ctx_n - 1, 1),)),
            dma((1,)), dma((max(ctx_n - 1, 1), 3)),
            dma((1,)),
            dma((1,)), dma((2 * sum(cuts) + chunks,)),
        ],
        compiler_params=pltpu.CompilerParams(
            collective_id=0, has_side_effects=True, vmem_limit_bytes=60 * 1024 * 1024
        ),
    )(hidden, w_query, w_down, gain, w_key_up, w_value_up, w_out)


def on_device(ctx_n, chips, hidden, w_query, w_down, latent_gain, w_key_up, w_value_up, w_out):
    rows, width = hidden.shape
    rank, nope = w_key_up.shape
    vdim = w_value_up.shape[1]
    per_core = chips * rows
    block = CORES * per_core
    lanes = -(-w_down.shape[1] // 128) * 128
    steps = 3 if width % 384 == 0 else 1
    if chips == 4 and rows % 32 == 0 and width % 768 == 0 and rank % LANE == 0 and 2 * (w_down.shape[1] - rank) == LANE:
        return square_call(
            ctx_n, hidden, w_query.T, w_down.T, latent_gain.reshape(1, rank), w_key_up, w_value_up, w_out
        )
    square = chips == 4 and rows % 16 == 0 and width % 256 == 0
    pieces = 6 if width % 768 == 0 else 2
    f32, bf16, dma = jnp.float32, jnp.bfloat16, pltpu.SemaphoreType.DMA
    return pl.pallas_call(
        functools.partial(general_kernel, ctx_n, chips, square, steps, pieces),
        out_shape=jax.ShapeDtypeStruct((rows, width), f32),
        in_specs=[pl.BlockSpec(memory_space=pltpu.HBM)] * 7,
        out_specs=pl.BlockSpec(memory_space=pltpu.VMEM),
        scratch_shapes=[
            pltpu.VMEM((per_core, width), f32),
            pltpu.VMEM(w_down.shape[::-1], f32),
            pltpu.VMEM((CORES,) + w_query.shape[::-1], f32),
            pltpu.VMEM((1, rank), f32),
            pltpu.VMEM((CORES, rank, nope), f32),
            pltpu.VMEM((CORES, rank, vdim), f32),
            pltpu.VMEM((CORES, vdim, width), f32),
            pltpu.VMEM((ctx_n * block, lanes), f32),
            pltpu.VMEM((block, lanes), bf16),
            pltpu.VMEM((block, lanes), bf16),
            pltpu.VMEM((block, 1), f32),
            pltpu.VMEM((block, 1), f32),
            pltpu.VMEM((block, rank), f32),
            pltpu.VMEM((per_core, width), f32),
            pltpu.VMEM((per_core, width), f32),
            dma((2 + steps + 4,)),
            dma((4,)), dma((4,)),
            dma((chips, 2)), dma((chips, 2)),
            dma((ctx_n,)), dma((ctx_n,)),
            dma((ctx_n, chips, 2)), dma((ctx_n, chips, 2)),
            dma((ctx_n,)), dma((ctx_n,)),
            dma((pieces, chips)), dma((pieces, chips)),
        ],
        compiler_params=pltpu.CompilerParams(
            collective_id=0, has_side_effects=True, vmem_limit_bytes=60 * 1024 * 1024
        ),
    )(hidden, w_query.T, w_down.T, latent_gain.reshape(1, rank), w_key_up, w_value_up, w_out)


def solution(mesh):
    placed = (
        P(("ctx", "head"), None),
        P(None, "head"),
        P(),
        P(),
        P(None, "head"),
        P(None, "head"),
        P("head", None),
    )
    body = functools.partial(on_device, mesh.shape["ctx"], mesh.shape["head"] // CORES)
    return jax.shard_map(
        body, mesh=mesh, in_specs=placed, out_specs=P(("ctx", "head"), None), check_vma=False
    )
```
